32 devices in a mesh: groups: 1, ctx: 32 (over z, y, x, core), kv: 1.
Axes of the slice: x: 2, y: 2, z: 4, core: 2. Of those that a mesh axis runs over, the one named last changes fastest.
Arguments:
- queries: bfloat16 [128, 64, 128], P('groups', 'kv'), may hold values from -10 to 10
- cache_keys: bfloat16 [32768, 4, 128], P(('groups', 'ctx'), 'kv'), may hold values from -5 to 5
- cache_values: bfloat16 [32768, 4, 128], P(('groups', 'ctx'), 'kv'), may hold values from -5 to 5
- block_mask: int32 [1, 256], P('groups', 'ctx'), may hold values from 0 to 1
- key_counts: int32 [256], P(('groups', 'ctx')), may hold values from 1 to 128, as said below
- out_weight: bfloat16 [8192, 16384], P('kv', 'ctx'), may hold values from -0.25 to 0.25
Outputs:
- layer_out: float32 [128, 16384], P(('groups', 'kv'), 'ctx')
The draws below stay inside these ranges and needn't reach their ends.
Inputs may be any that keep to these rules, and one draw needn't show every extreme that they name: `key_counts`: key block 0 is full.
All inputs are finite; a program needn't handle non-finite values.
Results may differ from the reference program's by a relative error of at most 0.0065.
Values may be sent and summed in bfloat16 or wider, within the bound.
No kernel may reach another device: no remote copies, remote signals or barrier semaphores. Data moves between devices by JAX's collectives and lax.ppermute only.
A program may use at most 64 MiB of HBM per device.

```python
import math
import jax
import jax.numpy as jnp
from jax import lax

D = 16384
HD = 128
QH = 64
KVH = 4
BLK = 128
TOKENS = 128
CTX = 32768
QB = 1
KB_DEV = 8
KB = 256


def draw_queries(key, part):
    values_key = jax.random.fold_in(key, 11)
    draws = jnp.clip(2.5 * jax.random.normal(values_key, (TOKENS, QH, HD), jnp.float32), -10.0, 10.0)
    return draws.astype(jnp.bfloat16)


def draw_cache_keys(key, part):
    values_key = jax.random.fold_in(key, 23)
    draws = jnp.clip(jax.random.normal(values_key, (CTX, KVH, HD), jnp.float32), -5.0, 5.0)
    return draws.astype(jnp.bfloat16)


def draw_block_mask(key, part):
    level_key, coin_key = jax.random.split(jax.random.fold_in(key, 37))
    device_count = KB // KB_DEV
    levels = jnp.left_shift(jnp.int32(1), jax.random.randint(level_key, (device_count,), 0, 4))
    owner = jnp.arange(KB, dtype=jnp.int32) // KB_DEV
    level_of_block = jnp.sum(jnp.where(owner[:, None] == jnp.arange(device_count, dtype=jnp.int32)[None, :], levels[None, :], 0), axis=1)
    coins = jax.random.randint(coin_key, (QB, KB), 0, 16)
    allowed = (coins < level_of_block[None, :]).astype(jnp.int32)
    return allowed.at[:, 0].set(1)


def draw_key_counts(key, part):
    ragged = jax.random.randint(jax.random.fold_in(key, 53), (KB,), 1, BLK + 1)
    blocks = jnp.arange(KB, dtype=jnp.int32)
    counts = jnp.where(blocks % KB_DEV == KB_DEV - 1, ragged, BLK)
    return jnp.where(blocks == 0, BLK, counts).astype(jnp.int32)


def block_levels(key, shape, pieces, smallest, high):
    def one(position, parts):
        steps = jax.random.uniform(jax.random.fold_in(jax.random.fold_in(key, 6), position), (parts,), jnp.float32, smallest / len(pieces), high / len(pieces))
        return jnp.repeat(jnp.exp(steps), shape[position] // parts).reshape((-1,) + (1,) * (len(shape) - position - 1))

    loudness = one(*pieces[0])
    for cut in pieces[1:]:
        loudness = loudness * one(*cut)
    return loudness


def normal_values(stream_key, dims, spread, most, cuts=(), kind=jnp.bfloat16):
    values = spread * jax.random.normal(stream_key, dims, jnp.float32)
    if cuts:
        values = values * block_levels(stream_key, dims, cuts, -0.22, 0.18)
    return jnp.clip(values, -most, most).astype(kind)


def setup_inputs(seed: int = 0, part: int = 0) -> dict:
    key_of = jax.random.split(jax.random.key(seed), 7)
    part_splits = jax.random.split(jax.random.fold_in(key_of[6], part), 7)
    return {
        "queries": draw_queries(jax.random.fold_in(jax.random.fold_in(key_of[6], part), 71), part),
        "cache_keys": draw_cache_keys(jax.random.fold_in(jax.random.fold_in(key_of[6], part), 71), part),
        "cache_values": normal_values(part_splits[2], (CTX, KVH, HD), 1.0, 5.0, ((0, 32),)),
        "block_mask": draw_block_mask(jax.random.fold_in(jax.random.fold_in(key_of[6], part), 71), part),
        "key_counts": draw_key_counts(jax.random.fold_in(jax.random.fold_in(key_of[6], part), 71), part),
        "out_weight": normal_values(key_of[5], (QH * HD, D), (QH * HD // 16) ** -0.5, 0.25, ((1, 32),)),
    }


very_low = -1e+30

def reference(queries, cache_keys, cache_values, block_mask, key_counts, out_weight):
    group_size = QH // KVH
    grouped = queries.astype(jnp.float32).reshape(TOKENS, KVH, group_size, HD)
    block_of_token = jnp.arange(TOKENS, dtype=jnp.int32) // BLK
    row_mask = block_mask[block_of_token]
    score_scale = 1.0 / math.sqrt(HD)
    offsets = jnp.arange(BLK, dtype=jnp.int32)

    def update(key_block, run_state):
        out_sum, top_score, weight_sum = run_state
        key_part = lax.dynamic_slice_in_dim(cache_keys, key_block * BLK, BLK, 0).astype(jnp.float32)
        value_part = lax.dynamic_slice_in_dim(cache_values, key_block * BLK, BLK, 0).astype(jnp.float32)
        scores = jnp.einsum('tgqd,kgd->tgqk', grouped, key_part, precision=lax.Precision.HIGHEST) * score_scale
        active_rows = lax.dynamic_slice_in_dim(row_mask, key_block, 1, 1)[:, 0] > 0
        valid_count = lax.dynamic_slice_in_dim(key_counts, key_block, 1, 0)[0]
        valid = active_rows[:, None, None, None] & (offsets < valid_count)[None, None, None, :]
        scores = jnp.where(valid, scores, very_low)
        new_top = jnp.maximum(top_score, lax.optimization_barrier(jnp.max(scores, axis=-1)))
        weights = jnp.where(valid, jnp.exp(scores - new_top[..., None]), 0.0)
        factor = jnp.exp(top_score - new_top)
        new_sum = weight_sum * factor + lax.optimization_barrier(jnp.sum(weights, axis=-1))
        low_weights = weights.astype(jnp.bfloat16).astype(jnp.float32)
        new_out = out_sum * factor[..., None] + jnp.einsum('tgqk,kgd->tgqd', low_weights, value_part, precision=lax.Precision.HIGHEST)
        return (new_out, new_top, new_sum)

    def keep_state(key_block, run_state):
        return run_state

    def visit_block(run_state, key_block):
        active = jnp.any(lax.dynamic_slice_in_dim(row_mask, key_block, 1, 1) > 0)
        return (lax.cond(active, update, keep_state, key_block, run_state), None)
    initial = (jnp.zeros((TOKENS, KVH, group_size, HD), jnp.float32), jnp.full((TOKENS, KVH, group_size), very_low, jnp.float32), jnp.zeros((TOKENS, KVH, group_size), jnp.float32))
    final_state, _ = lax.scan(visit_block, initial, jnp.arange(KB, dtype=jnp.int32))
    out_sum, top_score, weight_sum = final_state
    attended = (out_sum / weight_sum[..., None]).astype(jnp.bfloat16).reshape(TOKENS, QH * HD)
    return jnp.dot(attended, out_weight, preferred_element_type=jnp.float32)
```

```python
import functools
import math

import jax
import jax.numpy as jnp
from jax import lax
from jax.experimental import pallas as pl
from jax.experimental.pallas import tpu as pltpu
from jax.sharding import PartitionSpec as P

BLK = 128
LANES = 128
STAT = 16
very_low = -1e30
lowest_top = -(2.0**99)
bf16 = jnp.bfloat16
f32 = jnp.float32


def pack_state(out, top, total):
    high = total.astype(bf16).astype(f32)
    low = total - high
    row = lax.broadcasted_iota(jnp.int32, (STAT, LANES), 0)
    stats = jnp.where(row == 0, top, jnp.where(row == 1, high, jnp.where(row == 2, low, 0.0)))
    return out.astype(bf16), stats.astype(bf16)


def attention_kernel(with_start, scale2, meta, mask_ref, counts_ref, q_ref, k_ref, v_ref, *rest):
    if with_start:
        starts, rest = rest[:4], rest[4:]
    outs, (listed, kept_counts, kd, vt, spread, acc, top, total) = rest[:4], rest[4:]
    group, my_xy = meta[0], meta[1]
    rows = acc.shape[1]
    d = acc.shape[0]
    kv_count = spread.shape[0] // BLK
    block_count = counts_ref.shape[0]
    z_size = outs[0].shape[0]

    def note(block, found):
        listed[found] = block
        kept_counts[found] = counts_ref[block]
        return found + (mask_ref[0, block] > 0).astype(jnp.int32)

    active = lax.fori_loop(0, block_count, note, jnp.int32(0))
    kept_counts[active] = 0

    def take(source, block):
        start = pl.multiple_of(block * (BLK * kv_count), BLK * kv_count)
        spread[...] = source[pl.ds(start, BLK * kv_count), :].astype(f32)
        return spread[pl.ds(group, BLK, stride=kv_count), :]

    def fetch(position, _):
        block = listed[position]
        offset = pl.multiple_of(position * BLK, BLK)
        kd[pl.ds(offset, BLK), :] = take(k_ref, block).astype(bf16)
        vt[:, pl.ds(offset, BLK)] = take(v_ref, block).T.astype(bf16)
        return _

    lax.fori_loop(0, active, fetch, 0)

    @pl.when(active < block_count)
    def _():
        offset = pl.multiple_of(active * BLK, BLK)
        vt[:, pl.ds(offset, BLK)] = jnp.zeros((d, BLK), bf16)

    if with_start:
        for j in range(4):
            for z in range(z_size):
                piece = ((my_xy ^ j) * z_size + z) * LANES
                at = pl.ds(pl.multiple_of(piece, LANES), LANES)
                stats = starts[j][z, d : d + STAT, :].astype(f32)
                acc[:, at] = starts[j][z, 0:d, :].astype(f32)
                top[:, at] = stats[0:1]
                total[:, at] = stats[1:2] + stats[2:3]
    else:
        acc[...] = jnp.zeros_like(acc)
        top[...] = jnp.full_like(top, lowest_top)
        total[...] = jnp.zeros_like(total)

    tile = min(512, rows)

    def visit(step, _):
        offset = pl.multiple_of(step * (2 * BLK), 2 * BLK)
        keys = kd[pl.ds(offset, 2 * BLK), :]
        values = vt[:, pl.ds(offset, 2 * BLK)]
        place = lax.broadcasted_iota(jnp.int32, (2 * BLK, LANES), 0)
        limit = jnp.where(place < BLK, kept_counts[2 * step], kept_counts[2 * step + 1] + BLK)
        valid = jnp.concatenate([place < limit] * (tile // LANES), axis=1)
        for part in range(rows // tile):
            at = slice(part * tile, (part + 1) * tile)
            q = q_ref[part * (tile // 16) : (part + 1) * (tile // 16)].reshape(tile, d)
            scores = lax.dot_general(
                keys, q, (((1,), (1,)), ((), ())), preferred_element_type=f32
            )
            scores = jnp.where(valid, scores, very_low)
            old_top = top[:, at]
            new_top = jnp.maximum(old_top, jnp.max(scores, axis=0, keepdims=True) * scale2)
            weights = jnp.exp2(scores * scale2 - new_top)
            factor = jnp.exp2(old_top - new_top)
            total[:, at] = total[:, at] * factor + jnp.sum(weights, axis=0, keepdims=True)
            acc[:, at] = acc[:, at] * factor + jnp.dot(
                values, weights.astype(bf16), preferred_element_type=f32
            )
            top[:, at] = new_top
        return _

    lax.fori_loop(0, (active + 1) // 2, visit, 0)

    for j in range(4):
        for z in range(z_size):
            piece = ((my_xy ^ j) * z_size + z) * LANES
            at = pl.ds(pl.multiple_of(piece, LANES), LANES)
            old_top = top[:, at]
            sent_top = old_top.astype(bf16).astype(f32)
            factor = jnp.exp2(old_top - sent_top)
            out, stats = pack_state(acc[:, at] * factor, sent_top, total[:, at] * factor)
            outs[j][z, 0:d, :] = out
            outs[j][z, d : d + STAT, :] = stats


def merged(parts, d):
    stats = [part[d : d + STAT, :].astype(f32) for part in parts]
    tops = [stat[0:1] for stat in stats]
    top = functools.reduce(jnp.maximum, tops)
    out, total = 0.0, 0.0
    for part, stat, one in zip(parts, stats, tops):
        factor = jnp.exp2(one - top)
        out = out + part[0:d, :].astype(f32) * factor
        total = total + (stat[1:2] + stat[2:3]) * factor
    return out, top, total


def plane_kernel(meta, *refs):
    ins, outs = refs[:4], refs[4:]
    my_z = meta[2]
    d = outs[0].shape[0] - STAT
    for k in range(len(outs)):
        z = my_z ^ k
        out, stats = pack_state(*merged([ref[z] for ref in ins], d))
        outs[k][0:d, :] = out
        outs[k][d : d + STAT, :] = stats


def line_kernel(*refs):
    ins, out_ref, turned = refs[:-2], refs[-2], refs[-1]
    d = ins[0].shape[0] - STAT
    out, _, total = merged([ref[...] for ref in ins], d)
    turned[...] = (out / total).T
    tokens = out_ref.shape[0]
    heads = LANES // tokens
    for h in range(heads):
        out_ref[:, h * d : (h + 1) * d] = turned[pl.ds(h, tokens, stride=heads), :].astype(bf16)


def project_kernel(last, meta, w_own, w_other, *refs):
    own, other, refs = refs[:4], refs[4:8], refs[8:]
    z_size, tokens, depth = own[0].shape
    total = None
    for parts, weight in ((own, w_own), (other, w_other)):
        left = jnp.concatenate(
            [part[...].reshape(z_size * tokens, depth) for part in parts], axis=0
        )
        product = jnp.dot(left, weight[...], preferred_element_type=f32)
        total = product if total is None else total + product
    if not last:
        refs[0][...] = total
        return
    earlier, out_ref = refs
    total = total + earlier[...]
    my_xy, my_z = meta[1], meta[2]
    for j in range(4):
        for k in range(z_size):
            row = (j * z_size + k) * tokens
            to = ((my_xy ^ j) * z_size + (my_z ^ k)) * tokens
            out_ref[pl.ds(pl.multiple_of(to, tokens), tokens), :] = total[row : row + tokens]


def hop(value, mask):
    pairs = [(source, source ^ mask) for source in range(lax.axis_size("ctx"))]
    return lax.ppermute(value, "ctx", pairs)


VMEM = pl.BlockSpec(memory_space=pltpu.VMEM)
SMEM = pl.BlockSpec(memory_space=pltpu.SMEM)


def fast_body(queries, cache_keys, cache_values, block_mask, key_counts, out_weight):
    index = lax.axis_index("ctx")
    z_size = lax.axis_size("ctx") // 8
    token_count, head_count, d = queries.shape
    kv_count = cache_keys.shape[1]
    group_size = head_count // kv_count
    rows = token_count * group_size
    positions = cache_keys.shape[0]
    features = out_weight.shape[1]
    core = index & 1
    my_xy = (index >> 1) & 3
    my_z = index >> 3
    tall = d + STAT
    scale2 = math.log2(math.e) / math.sqrt(d)
    keys = cache_keys.reshape(positions * kv_count, d)
    values = cache_values.reshape(positions * kv_count, d)

    def meta(group):
        return jnp.stack([group, my_xy, my_z]).astype(jnp.int32)

    def attend(group, starts):
        ins = [
            SMEM,
            SMEM,
            pl.BlockSpec((token_count, group_size, d), lambda i, m: (0, m[0], 0)),
            VMEM,
            VMEM,
        ] + [VMEM] * len(starts)
        blocks = positions // BLK
        return pl.pallas_call(
            functools.partial(attention_kernel, bool(starts), scale2),
            grid_spec=pltpu.PrefetchScalarGridSpec(
                num_scalar_prefetch=1,
                grid=(1,),
                in_specs=ins,
                out_specs=[VMEM] * 4,
                scratch_shapes=[
                    pltpu.SMEM((blocks + 1,), jnp.int32),
                    pltpu.SMEM((blocks + 1,), jnp.int32),
                    pltpu.VMEM((positions, d), bf16),
                    pltpu.VMEM((d, positions), bf16),
                    pltpu.VMEM((BLK * kv_count, d), f32),
                    pltpu.VMEM((d, rows), f32),
                    pltpu.VMEM((1, rows), f32),
                    pltpu.VMEM((1, rows), f32),
                ],
            ),
            out_shape=[jax.ShapeDtypeStruct((z_size, tall, LANES), bf16)] * 4,
            compiler_params=pltpu.CompilerParams(vmem_limit_bytes=32 << 20),
            cost_estimate=pl.CostEstimate(
                flops=4 * rows * positions * d,
                transcendentals=rows * positions,
                bytes_accessed=4 * positions * d * kv_count,
            ),
            name="attention",
        )(meta(group), block_mask, key_counts, queries, keys, values, *starts)

    def merge_plane(parts):
        return pl.pallas_call(
            plane_kernel,
            in_specs=[SMEM] + [VMEM] * 4,
            out_specs=[VMEM] * z_size,
            out_shape=[jax.ShapeDtypeStruct((tall, LANES), bf16)] * z_size,
            name="merge_plane",
        )(meta(core), *parts)

    def merge_line(parts):
        tokens = LANES // group_size
        return pl.pallas_call(
            line_kernel,
            in_specs=[VMEM] * len(parts),
            out_specs=VMEM,
            out_shape=jax.ShapeDtypeStruct((tokens, group_size * d), bf16),
            scratch_shapes=[pltpu.VMEM((LANES, d), f32)],
            name="merge_line",
        )(*parts)

    def project(chunk, own, other, earlier):
        depth = group_size * d
        whole = [pl.BlockSpec(a.shape, lambda i, m: (0, 0, 0)) for a in own + other]
        more = [] if earlier is None else [earlier]
        return pl.pallas_call(
            functools.partial(project_kernel, earlier is not None),
            grid_spec=pltpu.PrefetchScalarGridSpec(
                num_scalar_prefetch=1,
                grid=(1,),
                in_specs=[
                    pl.BlockSpec((depth, features), lambda i, m: (m[0], 0)),
                    pl.BlockSpec((depth, features), lambda i, m: (m[0] ^ 1, 0)),
                ]
                + whole
                + [VMEM] * len(more),
                out_specs=VMEM,
            ),
            out_shape=jax.ShapeDtypeStruct((token_count, features), f32),
            compiler_params=pltpu.CompilerParams(vmem_limit_bytes=32 << 20),
            cost_estimate=pl.CostEstimate(
                flops=4 * token_count * depth * features,
                transcendentals=0,
                bytes_accessed=4 * depth * features,
            ),
            name="project",
        )(meta(2 * chunk + core), out_weight, out_weight, *own, *other, *more)

    chunks = kv_count // 2
    sent = [attend(2 * c + 1 - core, []) for c in range(chunks)]
    partner = [[hop(part, 1) for part in one] for one in sent]
    total = None
    for c in range(chunks):
        state = attend(2 * c + core, partner[c])
        state = [state[0]] + [hop(state[j], 2 * j) for j in (1, 2, 3)]
        state = merge_plane(state)
        state = [state[0]] + [hop(state[k], 8 * k) for k in range(1, z_size)]
        attended = merge_line(state)
        line = [attended] + [hop(attended, 8 * k) for k in range(1, z_size)]
        line = jnp.stack(line)
        own = [line] + [hop(line, 2 * j) for j in (1, 2, 3)]
        other = [hop(part, 1) for part in own]
        total = project(c, own, other, total)
    return total


def partner_of(value, axis, distance):
    mask = 2**distance
    pairs = [(source, source ^ mask) for source in range(lax.axis_size(axis))]
    return lax.ppermute(value, axis, pairs)


def combine(earlier, later):
    out_one, top_one, sum_one = earlier
    out_two, top_two, sum_two = later
    new_top = jnp.maximum(top_one, top_two)
    factor_one = jnp.exp(top_one - new_top)
    factor_two = jnp.exp(top_two - new_top)
    new_out = out_one * factor_one[..., None] + out_two * factor_two[..., None]
    return (new_out, new_top, sum_one * factor_one + sum_two * factor_two)


def keep_state(key_block, run_state):
    return run_state


def partial_rows(rows_q, row_mask, cache_keys, cache_values, key_counts):
    row_count, head_count, head_size = rows_q.shape
    kv_count = cache_keys.shape[1]
    group_size = head_count // kv_count
    grouped = rows_q.reshape(row_count, kv_count, group_size, head_size)
    block_count = cache_keys.shape[0] // BLK
    score_scale = 1.0 / math.sqrt(head_size)
    offsets = jnp.arange(BLK, dtype=jnp.int32)

    def update(key_block, run_state):
        out_sum, top_score, weight_sum = run_state
        key_part = lax.dynamic_slice_in_dim(cache_keys, key_block * BLK, BLK, 0)
        value_part = lax.dynamic_slice_in_dim(cache_values, key_block * BLK, BLK, 0)
        scores = (
            jnp.einsum("rgqd,kgd->rgqk", grouped, key_part, preferred_element_type=jnp.float32)
            * score_scale
        )
        active_rows = lax.dynamic_slice_in_dim(row_mask, key_block, 1, 1)[:, 0] > 0
        valid_count = lax.dynamic_slice_in_dim(key_counts, key_block, 1, 0)[0]
        valid = active_rows[:, None, None, None] & (offsets < valid_count)[None, None, None, :]
        scores = jnp.where(valid, scores, very_low)
        new_top = jnp.maximum(top_score, jnp.max(scores, axis=-1))
        weights = jnp.where(valid, jnp.exp(scores - new_top[..., None]), 0.0)
        factor = jnp.exp(top_score - new_top)
        new_sum = weight_sum * factor + jnp.sum(weights, axis=-1)
        new_out = out_sum * factor[..., None] + jnp.einsum(
            "rgqk,kgd->rgqd",
            weights.astype(jnp.bfloat16),
            value_part,
            preferred_element_type=jnp.float32,
        )
        return (new_out, new_top, new_sum)

    def visit_block(key_block, run_state):
        active = jnp.any(lax.dynamic_slice_in_dim(row_mask, key_block, 1, 1) > 0)
        return lax.cond(active, update, keep_state, key_block, run_state)

    initial = (
        jnp.zeros((row_count, kv_count, group_size, head_size), jnp.float32),
        jnp.full((row_count, kv_count, group_size), very_low, jnp.float32),
        jnp.zeros((row_count, kv_count, group_size), jnp.float32),
    )
    return lax.fori_loop(0, block_count, visit_block, initial)


def general_body(queries, cache_keys, cache_values, block_mask, key_counts, out_weight):
    cycle_size = lax.axis_size("ctx")
    cycle_index = lax.axis_index("ctx")
    token_count, head_count, head_size = queries.shape
    segment = token_count // cycle_size
    query_blocks = queries.reshape(block_mask.shape[0], BLK, head_count, head_size)

    def per_block(block_item):
        rows_q, mask_row = block_item
        row_mask = jnp.broadcast_to(mask_row[None, :], (BLK, mask_row.shape[0]))
        return partial_rows(rows_q, row_mask, cache_keys, cache_values, key_counts)

    stacked = lax.map(per_block, (query_blocks, block_mask))
    run_state = tuple((part.reshape((token_count,) + part.shape[2:]) for part in stacked))
    bit_total = cycle_size.bit_length() - 1
    for bit_number in range(bit_total - 1, -1, -1):
        half_rows = run_state[1].shape[0] // 2
        upper_half = jnp.bitwise_and(jnp.right_shift(cycle_index, bit_number), 1)
        kept = tuple(
            (
                lax.dynamic_slice_in_dim(part, upper_half * half_rows, half_rows, 0)
                for part in run_state
            )
        )
        outgoing = tuple(
            (
                lax.dynamic_slice_in_dim(part, (1 - upper_half) * half_rows, half_rows, 0)
                for part in run_state
            )
        )
        received = partner_of((outgoing[0], outgoing[1], outgoing[2]), "ctx", bit_number)
        run_state = combine(kept, received)
    out_sum, top_score, weight_sum = run_state
    attended = (
        (out_sum / weight_sum[..., None])
        .astype(jnp.bfloat16)
        .reshape(segment, head_count * head_size)
    )
    partial_value = jnp.dot(
        lax.all_gather(attended, "ctx", axis=0, tiled=True),
        out_weight,
        preferred_element_type=jnp.float32,
    )
    return lax.psum_scatter(partial_value, "kv", scatter_dimension=0, tiled=True)


def body(queries, cache_keys, cache_values, block_mask, key_counts, out_weight):
    devices = lax.axis_size("ctx")
    token_count, head_count, d = queries.shape
    kv_count = cache_keys.shape[1]
    group_size = head_count // kv_count
    suits = (
        lax.axis_size("kv") == 1
        and devices == 32
        and token_count == BLK
        and block_mask.shape[0] == 1
        and kv_count % 2 == 0
        and d == LANES
        and group_size == 16
        and token_count * group_size == LANES * (devices // 2)
    )
    run = fast_body if suits else general_body
    return run(queries, cache_keys, cache_values, block_mask, key_counts, out_weight)


def solution(mesh):
    placed = (
        P("groups", "kv", None),
        P(("groups", "ctx"), "kv", None),
        P(("groups", "ctx"), "kv", None),
        P("groups", "ctx"),
        P(("groups", "ctx")),
        P("kv", "ctx"),
    )
    return jax.shard_map(
        body, mesh=mesh, in_specs=placed, out_specs=P(("groups", "kv"), "ctx"), check_vma=False
    )
```

```python
import functools
import math

import jax
import jax.numpy as jnp
from jax import lax
from jax.experimental import pallas as pl
from jax.experimental.pallas import tpu as pltpu
from jax.sharding import PartitionSpec as P

BLK = 128
LANES = 128
STAT = 16
very_low = -1e30
lowest_top = -(2.0**99)
bf16 = jnp.bfloat16
f32 = jnp.float32


def pack_state(out, top, total):
    high = total.astype(bf16).astype(f32)
    low = total - high
    row = lax.broadcasted_iota(jnp.int32, (STAT, LANES), 0)
    stats = jnp.where(row == 0, top, jnp.where(row == 1, high, jnp.where(row == 2, low, 0.0)))
    return out.astype(bf16), stats.astype(bf16)


def attention_kernel(
    chunk, scale2, meta, mask_ref, counts_ref, q_hbm, k_hbm, v_hbm, send_ref, keep_ref, *scratch
):
    listed, kept_counts, q_ref, k_ref, v_ref, kd, vt, spread, sems = scratch
    core = meta[0]
    d = k_hbm.shape[1]
    kv_count = spread.shape[0] // BLK
    rows = send_ref.shape[0] * LANES
    group_size = q_ref.shape[2]
    block_count = counts_ref.shape[0]

    copies = [
        pltpu.make_async_copy(k_hbm, k_ref, sems.at[0]),
        pltpu.make_async_copy(v_hbm, v_ref, sems.at[1]),
    ]
    for g in range(2):
        heads = pl.ds((2 * chunk + g) * group_size, group_size)
        copies.append(pltpu.make_async_copy(q_hbm.at[:, heads, :], q_ref.at[g], sems.at[2 + g]))
    for copy in copies:
        copy.start()

    def note(block, found):
        listed[found] = block
        kept_counts[found] = counts_ref[block]
        return found + (mask_ref[0, block] > 0).astype(jnp.int32)

    active = lax.fori_loop(0, block_count, note, jnp.int32(0))
    place = lax.broadcasted_iota(jnp.int32, (BLK, LANES), 0)
    across = lax.broadcasted_iota(jnp.int32, (STAT, LANES), 1)

    def split(source, position):
        start = pl.multiple_of(listed[position] * (BLK * kv_count), BLK * kv_count)
        spread[...] = source[pl.ds(start, BLK * kv_count), :].astype(f32)
        return [spread[pl.ds(2 * chunk + g, BLK, stride=kv_count), :] for g in range(2)]

    def fetch_keys(position, carry):
        at = pl.ds(pl.multiple_of(position * BLK, BLK), BLK)
        valid = place < kept_counts[position]
        for g, key in enumerate(split(k_ref, position)):
            kd[g, at, :] = jnp.where(valid, key, key[0:1]).astype(bf16)
        return carry

    def fetch_values(position, carry):
        at = pl.ds(pl.multiple_of(position * BLK, BLK), BLK)
        count = kept_counts[position]
        for g, value in enumerate(split(v_ref, position)):
            vt[g, 0:d, at] = jnp.where(place < count, value, 0.0).T.astype(bf16)
            vt[g, d:, at] = (across < count).astype(f32).astype(bf16)
        return carry

    copies[0].wait()
    lax.fori_loop(0, active, fetch_keys, 0)
    copies[1].wait()
    lax.fori_loop(0, active, fetch_values, 0)

    @pl.when(active % 2 == 1)
    def _():
        at = pl.ds(pl.multiple_of(active * BLK, BLK), BLK)
        before = pl.ds(pl.multiple_of((active - 1) * BLK, BLK), BLK)
        for g in range(2):
            kd[g, at, :] = kd[g, before, :]
            vt[g, :, at] = jnp.zeros((d + STAT, BLK), bf16)

    copies[2].wait()
    copies[3].wait()
    pairs = (active + 1) // 2
    row = lax.broadcasted_iota(jnp.int32, (STAT, rows), 0)

    def attend(width, role, carry):
        group = jnp.where(role == 0, 1 - core, core)
        q = q_ref[group].reshape(rows, d)
        scores = lax.dot_general(
            kd[group, 0:width, :], q, (((1,), (1,)), ((), ())), preferred_element_type=f32
        )
        top = (jnp.max(scores, axis=0, keepdims=True) * scale2).astype(bf16).astype(f32)
        weights = jnp.exp2(scores * scale2 - top).astype(bf16)
        sums = jnp.dot(vt[group, :, 0:width], weights, preferred_element_type=f32)
        total = sums[d:]
        high = total.astype(bf16).astype(f32)
        stats = jnp.where(row == 0, top, jnp.where(row == 1, high, total - high)).astype(bf16)
        out = sums[:d].astype(bf16)
        for ref, its_role in ((send_ref, 0), (keep_ref, 1)):

            @pl.when(role == its_role)
            def _():
                for piece in range(rows // LANES):
                    at = slice(piece * LANES, (piece + 1) * LANES)
                    ref[piece, 0:d] = out[:, at]
                    ref[piece, d:] = stats[:, at]

        return carry

    for n in range(1, block_count // 2 + 1):

        @pl.when(pairs == n)
        def _(n=n):
            lax.fori_loop(0, 2, functools.partial(attend, 2 * BLK * n), 0)

    @pl.when(pairs == 0)
    def _():
        row = lax.broadcasted_iota(jnp.int32, (d + STAT, LANES), 0)
        empty = jnp.where(row == d, lowest_top, 0.0).astype(bf16)
        for ref in (send_ref, keep_ref):
            for piece in range(rows // LANES):
                ref[piece] = empty


def merged(parts, d):
    stats = [part[d : d + STAT, :].astype(f32) for part in parts]
    tops = [stat[0:1] for stat in stats]
    top = functools.reduce(jnp.maximum, tops)
    out, total = 0.0, 0.0
    for part, stat, one in zip(parts, stats, tops):
        factor = jnp.exp2(one - top)
        out = out + part[0:d, :].astype(f32) * factor
        total = total + (stat[1:2] + stat[2:3]) * factor
    return out, top, total


def store_merged(ref, z, parts):
    d = ref.shape[1] - STAT
    out, stats = pack_state(*merged(parts, d))
    ref[z, 0:d, :] = out
    ref[z, d : d + STAT, :] = stats


def core_kernel(meta, kept, received, *outs):
    my_xy = meta[1]
    z_size = outs[0].shape[0]
    for j, out in enumerate(outs):
        for z in range(z_size):
            piece = (my_xy ^ j) * z_size + z
            store_merged(out, z, [kept[piece], received[piece]])


def plane_kernel(*refs):
    ins, out = refs[:-1], refs[-1]
    for z in range(out.shape[0]):
        store_merged(out, z, [ref[z] for ref in ins])


def last_kernel(*refs):
    ins, out_ref, turned = refs[:-2], refs[-2], refs[-1]
    d = ins[0].shape[1] - STAT
    tokens = out_ref.shape[1]
    heads = LANES // tokens
    for z in range(out_ref.shape[0]):
        out, _, total = merged([ref[z] for ref in ins], d)
        turned[z] = (out / total).T
        for h in range(heads):
            picked = turned[z, pl.ds(h, tokens, stride=heads), :]
            out_ref[z, :, h * d : (h + 1) * d] = picked.astype(bf16)


def project_kernel(last, meta, w_own, w_other, *refs):
    own, other, refs = refs[:4], refs[4:8], refs[8:]
    z_size, tokens, depth = own[0].shape
    total = None
    for parts, weight in ((own, w_own), (other, w_other)):
        left = jnp.concatenate(
            [part[...].reshape(z_size * tokens, depth) for part in parts], axis=0
        )
        product = jnp.dot(left, weight[...], preferred_element_type=f32)
        total = product if total is None else total + product
    if not last:
        refs[0][...] = total
        return
    earlier, out_ref = refs
    total = total + earlier[...]
    my_xy = meta[1]
    size = z_size * tokens
    for j in range(4):
        to = pl.ds(pl.multiple_of((my_xy ^ j) * size, size), size)
        out_ref[to, :] = total[j * size : (j + 1) * size]


def hop(value, mask):
    pairs = [(source, source ^ mask) for source in range(lax.axis_size("ctx"))]
    return lax.ppermute(value, "ctx", pairs)


VMEM = pl.BlockSpec(memory_space=pltpu.VMEM)
SMEM = pl.BlockSpec(memory_space=pltpu.SMEM)
HBM = pl.BlockSpec(memory_space=pltpu.HBM)


def fast_body(queries, cache_keys, cache_values, block_mask, key_counts, out_weight):
    index = lax.axis_index("ctx")
    z_size = lax.axis_size("ctx") // 8
    token_count, head_count, d = queries.shape
    kv_count = cache_keys.shape[1]
    group_size = head_count // kv_count
    rows = token_count * group_size
    pieces = rows // LANES
    positions = cache_keys.shape[0]
    features = out_weight.shape[1]
    core = index & 1
    my_xy = (index >> 1) & 3
    tall = d + STAT
    scale2 = math.log2(math.e) / math.sqrt(d)
    keys = cache_keys.reshape(positions * kv_count, d)
    values = cache_values.reshape(positions * kv_count, d)
    place = jnp.stack([core, my_xy]).astype(jnp.int32)
    state = jax.ShapeDtypeStruct((z_size, tall, LANES), bf16)

    def attend(chunk):
        blocks = positions // BLK
        return pl.pallas_call(
            functools.partial(attention_kernel, chunk, scale2),
            in_specs=[SMEM] * 3 + [HBM] * 3,
            out_specs=[VMEM] * 2,
            scratch_shapes=[
                pltpu.SMEM((blocks + 1,), jnp.int32),
                pltpu.SMEM((blocks + 1,), jnp.int32),
                pltpu.VMEM((2, token_count, group_size, d), bf16),
                pltpu.VMEM((positions * kv_count, d), bf16),
                pltpu.VMEM((positions * kv_count, d), bf16),
                pltpu.VMEM((2, positions, d), bf16),
                pltpu.VMEM((2, tall, positions), bf16),
                pltpu.VMEM((BLK * kv_count, d), f32),
                pltpu.SemaphoreType.DMA((4,)),
            ],
            out_shape=[jax.ShapeDtypeStruct((pieces, tall, LANES), bf16)] * 2,
            compiler_params=pltpu.CompilerParams(vmem_limit_bytes=40 << 20),
            cost_estimate=pl.CostEstimate(
                flops=8 * rows * positions * d,
                transcendentals=2 * rows * positions,
                bytes_accessed=4 * positions * d * kv_count,
            ),
            name="attention",
        )(place, block_mask, key_counts, queries, keys, values)

    def merge_cores(kept, received):
        return pl.pallas_call(
            core_kernel,
            in_specs=[SMEM] + [VMEM] * 2,
            out_specs=[VMEM] * 4,
            out_shape=[state] * 4,
            name="merge_cores",
        )(place, kept, received)

    def merge_chips(parts):
        return pl.pallas_call(
            plane_kernel,
            in_specs=[VMEM] * len(parts),
            out_specs=VMEM,
            out_shape=state,
            name="merge_chips",
        )(*parts)

    def finish(parts):
        tokens = LANES // group_size
        return pl.pallas_call(
            last_kernel,
            in_specs=[VMEM] * len(parts),
            out_specs=VMEM,
            out_shape=jax.ShapeDtypeStruct((z_size, tokens, group_size * d), bf16),
            scratch_shapes=[pltpu.VMEM((z_size, LANES, d), f32)],
            name="finish",
        )(*parts)

    def project(chunk, own, other, earlier):
        depth = group_size * d
        whole = [pl.BlockSpec(a.shape, lambda i, m: (0, 0, 0)) for a in own + other]
        more = [] if earlier is None else [earlier]
        return pl.pallas_call(
            functools.partial(project_kernel, earlier is not None),
            grid_spec=pltpu.PrefetchScalarGridSpec(
                num_scalar_prefetch=1,
                grid=(1,),
                in_specs=[
                    pl.BlockSpec((depth, features), lambda i, m: (2 * chunk + m[0], 0)),
                    pl.BlockSpec((depth, features), lambda i, m: (2 * chunk + 1 - m[0], 0)),
                ]
                + whole
                + [VMEM] * len(more),
                out_specs=VMEM,
            ),
            out_shape=jax.ShapeDtypeStruct((token_count, features), f32),
            compiler_params=pltpu.CompilerParams(vmem_limit_bytes=32 << 20),
            cost_estimate=pl.CostEstimate(
                flops=4 * token_count * depth * features,
                transcendentals=0,
                bytes_accessed=4 * depth * features,
            ),
            name="project",
        )(place, out_weight, out_weight, *own, *other, *more)

    chunks = kv_count // 2
    partials = []
    for c in range(chunks):
        sent, kept = attend(c)
        partials.append((kept, hop(sent, 1)))
    total = None
    for c in range(chunks):
        parts = merge_cores(*partials[c])
        parts = [parts[0]] + [hop(parts[j], 2 * j) for j in (1, 2, 3)]
        part = merge_chips(parts)
        reach = 1
        while 2 * reach < z_size:
            part = merge_chips([part, hop(part, 8 * reach)])
            reach *= 2
        attended = finish([part, hop(part, 8 * reach)])
        own = [attended] + [hop(attended, 2 * j) for j in (1, 2, 3)]
        other = [hop(part, 1) for part in own]
        total = project(c, own, other, total)
    return total


def partner_of(value, axis, distance):
    mask = 2**distance
    pairs = [(source, source ^ mask) for source in range(lax.axis_size(axis))]
    return lax.ppermute(value, axis, pairs)


def combine(earlier, later):
    out_one, top_one, sum_one = earlier
    out_two, top_two, sum_two = later
    new_top = jnp.maximum(top_one, top_two)
    factor_one = jnp.exp(top_one - new_top)
    factor_two = jnp.exp(top_two - new_top)
    new_out = out_one * factor_one[..., None] + out_two * factor_two[..., None]
    return (new_out, new_top, sum_one * factor_one + sum_two * factor_two)


def keep_state(key_block, run_state):
    return run_state


def partial_rows(rows_q, row_mask, cache_keys, cache_values, key_counts):
    row_count, head_count, head_size = rows_q.shape
    kv_count = cache_keys.shape[1]
    group_size = head_count // kv_count
    grouped = rows_q.reshape(row_count, kv_count, group_size, head_size)
    block_count = cache_keys.shape[0] // BLK
    score_scale = 1.0 / math.sqrt(head_size)
    offsets = jnp.arange(BLK, dtype=jnp.int32)

    def update(key_block, run_state):
        out_sum, top_score, weight_sum = run_state
        key_part = lax.dynamic_slice_in_dim(cache_keys, key_block * BLK, BLK, 0)
        value_part = lax.dynamic_slice_in_dim(cache_values, key_block * BLK, BLK, 0)
        scores = (
            jnp.einsum("rgqd,kgd->rgqk", grouped, key_part, preferred_element_type=jnp.float32)
            * score_scale
        )
        active_rows = lax.dynamic_slice_in_dim(row_mask, key_block, 1, 1)[:, 0] > 0
        valid_count = lax.dynamic_slice_in_dim(key_counts, key_block, 1, 0)[0]
        valid = active_rows[:, None, None, None] & (offsets < valid_count)[None, None, None, :]
        scores = jnp.where(valid, scores, very_low)
        new_top = jnp.maximum(top_score, jnp.max(scores, axis=-1))
        weights = jnp.where(valid, jnp.exp(scores - new_top[..., None]), 0.0)
        factor = jnp.exp(top_score - new_top)
        new_sum = weight_sum * factor + jnp.sum(weights, axis=-1)
        new_out = out_sum * factor[..., None] + jnp.einsum(
            "rgqk,kgd->rgqd",
            weights.astype(jnp.bfloat16),
            value_part,
            preferred_element_type=jnp.float32,
        )
        return (new_out, new_top, new_sum)

    def visit_block(key_block, run_state):
        active = jnp.any(lax.dynamic_slice_in_dim(row_mask, key_block, 1, 1) > 0)
        return lax.cond(active, update, keep_state, key_block, run_state)

    initial = (
        jnp.zeros((row_count, kv_count, group_size, head_size), jnp.float32),
        jnp.full((row_count, kv_count, group_size), very_low, jnp.float32),
        jnp.zeros((row_count, kv_count, group_size), jnp.float32),
    )
    return lax.fori_loop(0, block_count, visit_block, initial)


def general_body(queries, cache_keys, cache_values, block_mask, key_counts, out_weight):
    cycle_size = lax.axis_size("ctx")
    cycle_index = lax.axis_index("ctx")
    token_count, head_count, head_size = queries.shape
    segment = token_count // cycle_size
    query_blocks = queries.reshape(block_mask.shape[0], BLK, head_count, head_size)

    def per_block(block_item):
        rows_q, mask_row = block_item
        row_mask = jnp.broadcast_to(mask_row[None, :], (BLK, mask_row.shape[0]))
        return partial_rows(rows_q, row_mask, cache_keys, cache_values, key_counts)

    stacked = lax.map(per_block, (query_blocks, block_mask))
    run_state = tuple((part.reshape((token_count,) + part.shape[2:]) for part in stacked))
    bit_total = cycle_size.bit_length() - 1
    for bit_number in range(bit_total - 1, -1, -1):
        half_rows = run_state[1].shape[0] // 2
        upper_half = jnp.bitwise_and(jnp.right_shift(cycle_index, bit_number), 1)
        kept = tuple(
            (
                lax.dynamic_slice_in_dim(part, upper_half * half_rows, half_rows, 0)
                for part in run_state
            )
        )
        outgoing = tuple(
            (
                lax.dynamic_slice_in_dim(part, (1 - upper_half) * half_rows, half_rows, 0)
                for part in run_state
            )
        )
        received = partner_of((outgoing[0], outgoing[1], outgoing[2]), "ctx", bit_number)
        run_state = combine(kept, received)
    out_sum, top_score, weight_sum = run_state
    attended = (
        (out_sum / weight_sum[..., None])
        .astype(jnp.bfloat16)
        .reshape(segment, head_count * head_size)
    )
    partial_value = jnp.dot(
        lax.all_gather(attended, "ctx", axis=0, tiled=True),
        out_weight,
        preferred_element_type=jnp.float32,
    )
    return lax.psum_scatter(partial_value, "kv", scatter_dimension=0, tiled=True)


def body(queries, cache_keys, cache_values, block_mask, key_counts, out_weight):
    devices = lax.axis_size("ctx")
    token_count, head_count, d = queries.shape
    kv_count = cache_keys.shape[1]
    group_size = head_count // kv_count
    suits = (
        lax.axis_size("kv") == 1
        and devices == 32
        and token_count == BLK
        and block_mask.shape[0] == 1
        and kv_count % 2 == 0
        and d == LANES
        and group_size == 16
        and token_count * group_size == LANES * (devices // 2)
    )
    run = fast_body if suits else general_body
    return run(queries, cache_keys, cache_values, block_mask, key_counts, out_weight)


def solution(mesh):
    placed = (
        P("groups", "kv", None),
        P(("groups", "ctx"), "kv", None),
        P(("groups", "ctx"), "kv", None),
        P("groups", "ctx"),
        P(("groups", "ctx")),
        P("kv", "ctx"),
    )
    return jax.shard_map(
        body, mesh=mesh, in_specs=placed, out_specs=P(("groups", "kv"), "ctx"), check_vma=False
    )
```

```python
import functools
import math

import jax
import jax.numpy as jnp
from jax import lax
from jax.experimental import pallas as pl
from jax.experimental.pallas import tpu as pltpu
from jax.sharding import PartitionSpec as P

BLK = 128
LANES = 128
STAT = 16
very_low = -1e30
lowest_top = -(2.0**99)
bf16 = jnp.bfloat16
f32 = jnp.float32


def pack_state(out, top, total):
    high = total.astype(bf16).astype(f32)
    low = total - high
    row = lax.broadcasted_iota(jnp.int32, (STAT, LANES), 0)
    stats = jnp.where(row == 0, top, jnp.where(row == 1, high, jnp.where(row == 2, low, 0.0)))
    return out.astype(bf16), stats.astype(bf16)


def attention_kernel(
    chunk, scale2, meta, q_hbm, k_hbm, v_hbm, send_ref, keep_ref, *scratch
):
    listed, kept_counts, q_ref, k_ref, v_ref, kd, vt, spread, sems = scratch
    core = meta[0]
    d = k_hbm.shape[1]
    kv_count = spread.shape[0] // BLK
    rows = send_ref.shape[0] * LANES
    group_size = q_ref.shape[2]
    block_count = (meta.shape[0] - 2) // 2

    copies = [
        pltpu.make_async_copy(k_hbm, k_ref, sems.at[0]),
        pltpu.make_async_copy(v_hbm, v_ref, sems.at[1]),
    ]
    for g in range(2):
        heads = pl.ds((2 * chunk + g) * group_size, group_size)
        copies.append(pltpu.make_async_copy(q_hbm.at[:, heads, :], q_ref.at[g], sems.at[2 + g]))
    for copy in copies:
        copy.start()

    def note(block, found):
        listed[found] = block
        kept_counts[found] = meta[2 + block_count + block]
        return found + (meta[2 + block] > 0).astype(jnp.int32)

    active = lax.fori_loop(0, block_count, note, jnp.int32(0))
    place = lax.broadcasted_iota(jnp.int32, (BLK, LANES), 0)
    across = lax.broadcasted_iota(jnp.int32, (STAT, LANES), 1)

    def split(source, position):
        start = pl.multiple_of(listed[position] * (BLK * kv_count), BLK * kv_count)
        spread[...] = source[pl.ds(start, BLK * kv_count), :].astype(f32)
        return [spread[pl.ds(2 * chunk + g, BLK, stride=kv_count), :] for g in range(2)]

    def fetch_keys(position, carry):
        at = pl.ds(pl.multiple_of(position * BLK, BLK), BLK)
        valid = place < kept_counts[position]
        for g, key in enumerate(split(k_ref, position)):
            kd[g, at, :] = jnp.where(valid, key, key[0:1]).astype(bf16)
        return carry

    def fetch_values(position, carry):
        at = pl.ds(pl.multiple_of(position * BLK, BLK), BLK)
        count = kept_counts[position]
        for g, value in enumerate(split(v_ref, position)):
            vt[g, 0:d, at] = jnp.where(place < count, value, 0.0).T.astype(bf16)
            vt[g, d:, at] = (across < count).astype(f32).astype(bf16)
        return carry

    copies[0].wait()
    lax.fori_loop(0, active, fetch_keys, 0)
    copies[1].wait()
    lax.fori_loop(0, active, fetch_values, 0)

    @pl.when(active % 2 == 1)
    def _():
        at = pl.ds(pl.multiple_of(active * BLK, BLK), BLK)
        before = pl.ds(pl.multiple_of((active - 1) * BLK, BLK), BLK)
        for g in range(2):
            kd[g, at, :] = kd[g, before, :]
            vt[g, :, at] = jnp.zeros((d + STAT, BLK), bf16)

    copies[2].wait()
    copies[3].wait()
    pairs = (active + 1) // 2
    row = lax.broadcasted_iota(jnp.int32, (STAT, rows), 0)

    def attend(width, role, carry):
        group = jnp.where(role == 0, 1 - core, core)
        q = q_ref[group].reshape(rows, d)
        scores = lax.dot_general(
            kd[group, 0:width, :], q, (((1,), (1,)), ((), ())), preferred_element_type=f32
        )
        top = (jnp.max(scores, axis=0, keepdims=True) * scale2).astype(bf16).astype(f32)
        weights = jnp.exp2(scores * scale2 - top).astype(bf16)
        sums = jnp.dot(vt[group, :, 0:width], weights, preferred_element_type=f32)
        total = sums[d:]
        high = total.astype(bf16).astype(f32)
        stats = jnp.where(row == 0, top, jnp.where(row == 1, high, total - high)).astype(bf16)
        out = sums[:d].astype(bf16)
        for ref, its_role in ((send_ref, 0), (keep_ref, 1)):

            @pl.when(role == its_role)
            def _():
                for piece in range(rows // LANES):
                    at = slice(piece * LANES, (piece + 1) * LANES)
                    ref[piece, 0:d] = out[:, at]
                    ref[piece, d:] = stats[:, at]

        return carry

    for n in range(1, block_count // 2 + 1):

        @pl.when(pairs == n)
        def _(n=n):
            lax.fori_loop(0, 2, functools.partial(attend, 2 * BLK * n), 0)

    @pl.when(pairs == 0)
    def _():
        row = lax.broadcasted_iota(jnp.int32, (d + STAT, LANES), 0)
        empty = jnp.where(row == d, lowest_top, 0.0).astype(bf16)
        for ref in (send_ref, keep_ref):
            for piece in range(rows // LANES):
                ref[piece] = empty


def merged(parts, d):
    stats = [part[d : d + STAT, :].astype(f32) for part in parts]
    tops = [stat[0:1] for stat in stats]
    top = functools.reduce(jnp.maximum, tops)
    out, total = 0.0, 0.0
    for part, stat, one in zip(parts, stats, tops):
        factor = jnp.exp2(one - top)
        out = out + part[0:d, :].astype(f32) * factor
        total = total + (stat[1:2] + stat[2:3]) * factor
    return out, top, total


def store_merged(ref, z, parts):
    d = ref.shape[1] - STAT
    out, stats = pack_state(*merged(parts, d))
    ref[z, 0:d, :] = out
    ref[z, d : d + STAT, :] = stats


def core_kernel(meta, kept, received, *outs):
    my_xy = meta[1]
    z_size = outs[0].shape[0]
    for j, out in enumerate(outs):
        for z in range(z_size):
            piece = (my_xy ^ j) * z_size + z
            store_merged(out, z, [kept[piece], received[piece]])


def plane_kernel(*refs):
    ins, out = refs[:-1], refs[-1]
    for z in range(out.shape[0]):
        store_merged(out, z, [ref[z] for ref in ins])


def last_kernel(*refs):
    ins, out_ref, turned = refs[:-2], refs[-2], refs[-1]
    d = ins[0].shape[1] - STAT
    tokens = out_ref.shape[1]
    heads = LANES // tokens
    for z in range(out_ref.shape[0]):
        out, _, total = merged([ref[z] for ref in ins], d)
        turned[z] = (out / total).T
        for h in range(heads):
            picked = turned[z, pl.ds(h, tokens, stride=heads), :]
            out_ref[z, :, h * d : (h + 1) * d] = picked.astype(bf16)


def project_kernel(chunk, last, meta, weight, *refs):
    own, other, refs = refs[:4], refs[4:8], refs[8:]
    z_size, tokens, depth = own[0].shape
    total = None
    for parts, core in ((own, meta[0]), (other, 1 - meta[0])):
        left = jnp.concatenate(
            [part[...].reshape(z_size * tokens, depth) for part in parts], axis=0
        )
        at = pl.ds(pl.multiple_of((2 * chunk + core) * depth, depth), depth)
        product = jnp.dot(left, weight[at, :], preferred_element_type=f32)
        total = product if total is None else total + product
    if not last:
        refs[0][...] = total
        return
    earlier, out_ref = refs
    total = total + earlier[...]
    my_xy = meta[1]
    size = z_size * tokens
    for j in range(4):
        to = pl.ds(pl.multiple_of((my_xy ^ j) * size, size), size)
        out_ref[to, :] = total[j * size : (j + 1) * size]


def hop(value, mask):
    pairs = [(source, source ^ mask) for source in range(lax.axis_size("ctx"))]
    return lax.ppermute(value, "ctx", pairs)


VMEM = pl.BlockSpec(memory_space=pltpu.VMEM)
SMEM = pl.BlockSpec(memory_space=pltpu.SMEM)
HBM = pl.BlockSpec(memory_space=pltpu.HBM)
SMALL = pltpu.CompilerParams(vmem_limit_bytes=4 << 20)


def fast_body(queries, cache_keys, cache_values, block_mask, key_counts, out_weight):
    index = lax.axis_index("ctx")
    z_size = lax.axis_size("ctx") // 8
    token_count, head_count, d = queries.shape
    kv_count = cache_keys.shape[1]
    group_size = head_count // kv_count
    rows = token_count * group_size
    pieces = rows // LANES
    positions = cache_keys.shape[0]
    features = out_weight.shape[1]
    core = index & 1
    my_xy = (index >> 1) & 3
    tall = d + STAT
    scale2 = math.log2(math.e) / math.sqrt(d)
    keys = cache_keys.reshape(positions * kv_count, d)
    values = cache_values.reshape(positions * kv_count, d)
    place = jnp.concatenate(
        [jnp.stack([core, my_xy]).astype(jnp.int32), block_mask[0], key_counts]
    )
    kept_in_hbm = functools.partial(pltpu.with_memory_space_constraint, memory_space=pltpu.HBM)
    queries, keys, values = kept_in_hbm(queries), kept_in_hbm(keys), kept_in_hbm(values)
    state = jax.ShapeDtypeStruct((z_size, tall, LANES), bf16)

    def attend(chunk):
        blocks = positions // BLK
        return pl.pallas_call(
            functools.partial(attention_kernel, chunk, scale2),
            in_specs=[SMEM] + [HBM] * 3,
            out_specs=[VMEM] * 2,
            scratch_shapes=[
                pltpu.SMEM((blocks + 1,), jnp.int32),
                pltpu.SMEM((blocks + 1,), jnp.int32),
                pltpu.VMEM((2, token_count, group_size, d), bf16),
                pltpu.VMEM((positions * kv_count, d), bf16),
                pltpu.VMEM((positions * kv_count, d), bf16),
                pltpu.VMEM((2, positions, d), bf16),
                pltpu.VMEM((2, tall, positions), bf16),
                pltpu.VMEM((BLK * kv_count, d), f32),
                pltpu.SemaphoreType.DMA((4,)),
            ],
            out_shape=[jax.ShapeDtypeStruct((pieces, tall, LANES), bf16)] * 2,
            compiler_params=pltpu.CompilerParams(vmem_limit_bytes=40 << 20),
            cost_estimate=pl.CostEstimate(
                flops=8 * rows * positions * d,
                transcendentals=2 * rows * positions,
                bytes_accessed=4 * positions * d * kv_count,
            ),
            name="attention",
        )(place, queries, keys, values)

    def merge_cores(kept, received):
        return pl.pallas_call(
            core_kernel,
            in_specs=[SMEM] + [VMEM] * 2,
            out_specs=[VMEM] * 4,
            out_shape=[state] * 4,
            compiler_params=SMALL,
            name="merge_cores",
        )(place, kept, received)

    def merge_chips(parts):
        return pl.pallas_call(
            plane_kernel,
            in_specs=[VMEM] * len(parts),
            out_specs=VMEM,
            out_shape=state,
            compiler_params=SMALL,
            name="merge_chips",
        )(*parts)

    def finish(parts):
        tokens = LANES // group_size
        return pl.pallas_call(
            last_kernel,
            in_specs=[VMEM] * len(parts),
            out_specs=VMEM,
            out_shape=jax.ShapeDtypeStruct((z_size, tokens, group_size * d), bf16),
            scratch_shapes=[pltpu.VMEM((z_size, LANES, d), f32)],
            compiler_params=SMALL,
            name="finish",
        )(*parts)

    def project(chunk, own, other, earlier):
        depth = group_size * d
        more = [] if earlier is None else [earlier]
        return pl.pallas_call(
            functools.partial(project_kernel, chunk, earlier is not None),
            in_specs=[SMEM] + [VMEM] * (1 + len(own + other + more)),
            out_specs=VMEM,
            out_shape=jax.ShapeDtypeStruct((token_count, features), f32),
            compiler_params=pltpu.CompilerParams(vmem_limit_bytes=8 << 20),
            cost_estimate=pl.CostEstimate(
                flops=4 * token_count * depth * features,
                transcendentals=0,
                bytes_accessed=4 * depth * features,
            ),
            name="project",
        )(place, out_weight, *own, *other, *more)

    chunks = kv_count // 2
    partials = []
    for c in range(chunks):
        sent, kept = attend(c)
        partials.append((kept, hop(sent, 1)))
    total = None
    for c in range(chunks):
        parts = merge_cores(*partials[c])
        parts = [parts[0]] + [hop(parts[j], 2 * j) for j in (1, 2, 3)]
        part = merge_chips(parts)
        reach = 1
        while 2 * reach < z_size:
            part = merge_chips([part, hop(part, 8 * reach)])
            reach *= 2
        attended = finish([part, hop(part, 8 * reach)])
        own = [attended] + [hop(attended, 2 * j) for j in (1, 2, 3)]
        other = [hop(part, 1) for part in own]
        total = project(c, own, other, total)
    return total


def partner_of(value, axis, distance):
    mask = 2**distance
    pairs = [(source, source ^ mask) for source in range(lax.axis_size(axis))]
    return lax.ppermute(value, axis, pairs)


def combine(earlier, later):
    out_one, top_one, sum_one = earlier
    out_two, top_two, sum_two = later
    new_top = jnp.maximum(top_one, top_two)
    factor_one = jnp.exp(top_one - new_top)
    factor_two = jnp.exp(top_two - new_top)
    new_out = out_one * factor_one[..., None] + out_two * factor_two[..., None]
    return (new_out, new_top, sum_one * factor_one + sum_two * factor_two)


def keep_state(key_block, run_state):
    return run_state


def partial_rows(rows_q, row_mask, cache_keys, cache_values, key_counts):
    row_count, head_count, head_size = rows_q.shape
    kv_count = cache_keys.shape[1]
    group_size = head_count // kv_count
    grouped = rows_q.reshape(row_count, kv_count, group_size, head_size)
    block_count = cache_keys.shape[0] // BLK
    score_scale = 1.0 / math.sqrt(head_size)
    offsets = jnp.arange(BLK, dtype=jnp.int32)

    def update(key_block, run_state):
        out_sum, top_score, weight_sum = run_state
        key_part = lax.dynamic_slice_in_dim(cache_keys, key_block * BLK, BLK, 0)
        value_part = lax.dynamic_slice_in_dim(cache_values, key_block * BLK, BLK, 0)
        scores = (
            jnp.einsum("rgqd,kgd->rgqk", grouped, key_part, preferred_element_type=jnp.float32)
            * score_scale
        )
        active_rows = lax.dynamic_slice_in_dim(row_mask, key_block, 1, 1)[:, 0] > 0
        valid_count = lax.dynamic_slice_in_dim(key_counts, key_block, 1, 0)[0]
        valid = active_rows[:, None, None, None] & (offsets < valid_count)[None, None, None, :]
        scores = jnp.where(valid, scores, very_low)
        new_top = jnp.maximum(top_score, jnp.max(scores, axis=-1))
        weights = jnp.where(valid, jnp.exp(scores - new_top[..., None]), 0.0)
        factor = jnp.exp(top_score - new_top)
        new_sum = weight_sum * factor + jnp.sum(weights, axis=-1)
        new_out = out_sum * factor[..., None] + jnp.einsum(
            "rgqk,kgd->rgqd",
            weights.astype(jnp.bfloat16),
            value_part,
            preferred_element_type=jnp.float32,
        )
        return (new_out, new_top, new_sum)

    def visit_block(key_block, run_state):
        active = jnp.any(lax.dynamic_slice_in_dim(row_mask, key_block, 1, 1) > 0)
        return lax.cond(active, update, keep_state, key_block, run_state)

    initial = (
        jnp.zeros((row_count, kv_count, group_size, head_size), jnp.float32),
        jnp.full((row_count, kv_count, group_size), very_low, jnp.float32),
        jnp.zeros((row_count, kv_count, group_size), jnp.float32),
    )
    return lax.fori_loop(0, block_count, visit_block, initial)


def general_body(queries, cache_keys, cache_values, block_mask, key_counts, out_weight):
    cycle_size = lax.axis_size("ctx")
    cycle_index = lax.axis_index("ctx")
    token_count, head_count, head_size = queries.shape
    segment = token_count // cycle_size
    query_blocks = queries.reshape(block_mask.shape[0], BLK, head_count, head_size)

    def per_block(block_item):
        rows_q, mask_row = block_item
        row_mask = jnp.broadcast_to(mask_row[None, :], (BLK, mask_row.shape[0]))
        return partial_rows(rows_q, row_mask, cache_keys, cache_values, key_counts)

    stacked = lax.map(per_block, (query_blocks, block_mask))
    run_state = tuple((part.reshape((token_count,) + part.shape[2:]) for part in stacked))
    bit_total = cycle_size.bit_length() - 1
    for bit_number in range(bit_total - 1, -1, -1):
        half_rows = run_state[1].shape[0] // 2
        upper_half = jnp.bitwise_and(jnp.right_shift(cycle_index, bit_number), 1)
        kept = tuple(
            (
                lax.dynamic_slice_in_dim(part, upper_half * half_rows, half_rows, 0)
                for part in run_state
            )
        )
        outgoing = tuple(
            (
                lax.dynamic_slice_in_dim(part, (1 - upper_half) * half_rows, half_rows, 0)
                for part in run_state
            )
        )
        received = partner_of((outgoing[0], outgoing[1], outgoing[2]), "ctx", bit_number)
        run_state = combine(kept, received)
    out_sum, top_score, weight_sum = run_state
    attended = (
        (out_sum / weight_sum[..., None])
        .astype(jnp.bfloat16)
        .reshape(segment, head_count * head_size)
    )
    partial_value = jnp.dot(
        lax.all_gather(attended, "ctx", axis=0, tiled=True),
        out_weight,
        preferred_element_type=jnp.float32,
    )
    return lax.psum_scatter(partial_value, "kv", scatter_dimension=0, tiled=True)


def body(queries, cache_keys, cache_values, block_mask, key_counts, out_weight):
    devices = lax.axis_size("ctx")
    token_count, head_count, d = queries.shape
    kv_count = cache_keys.shape[1]
    group_size = head_count // kv_count
    suits = (
        lax.axis_size("kv") == 1
        and devices == 32
        and token_count == BLK
        and block_mask.shape[0] == 1
        and kv_count % 2 == 0
        and d == LANES
        and group_size == 16
        and token_count * group_size == LANES * (devices // 2)
    )
    run = fast_body if suits else general_body
    return run(queries, cache_keys, cache_values, block_mask, key_counts, out_weight)


def solution(mesh):
    placed = (
        P("groups", "kv", None),
        P(("groups", "ctx"), "kv", None),
        P(("groups", "ctx"), "kv", None),
        P("groups", "ctx"),
        P(("groups", "ctx")),
        P("kv", "ctx"),
    )
    return jax.shard_map(
        body, mesh=mesh, in_specs=placed, out_specs=P(("groups", "kv"), "ctx"), check_vma=False
    )
```

```python
import functools
import math

import jax
import jax.numpy as jnp
from jax import lax
from jax.experimental import pallas as pl
from jax.experimental.pallas import tpu as pltpu
from jax.sharding import PartitionSpec as P

BLK = 128
LANES = 128
STAT = 16
very_low = -1e30
lowest_top = -(2.0**99)
bf16 = jnp.bfloat16
f32 = jnp.float32


def pack_state(out, top, total):
    high = total.astype(bf16).astype(f32)
    low = total - high
    row = lax.broadcasted_iota(jnp.int32, (STAT, LANES), 0)
    stats = jnp.where(row == 0, top, jnp.where(row == 1, high, jnp.where(row == 2, low, 0.0)))
    return out.astype(bf16), stats.astype(bf16)


def active_count(meta):
    block_count = (meta.shape[0] - 2) // 2
    return sum((meta[2 + block] > 0).astype(jnp.int32) for block in range(block_count))


def split_kernel(meta, k_hbm, v_hbm, q_hbm, kd, vt, sent_ref, *scratch):
    listed, kept_counts, q_ref, k_ref, v_ref, spread, sems = scratch
    d = k_hbm.shape[1]
    kv_count = kd.shape[0]
    group_size = q_ref.shape[1]
    block_count = (meta.shape[0] - 2) // 2
    group = 1 - meta[0]

    heads = pl.ds(pl.multiple_of(group * group_size, group_size), group_size)
    copies = [
        pltpu.make_async_copy(k_hbm, k_ref, sems.at[0]),
        pltpu.make_async_copy(v_hbm, v_ref, sems.at[1]),
        pltpu.make_async_copy(q_hbm.at[:, heads, :], q_ref, sems.at[2]),
    ]
    for copy in copies:
        copy.start()

    def note(block, found):
        listed[found] = block
        kept_counts[found] = meta[2 + block_count + block]
        return found + (meta[2 + block] > 0).astype(jnp.int32)

    active = lax.fori_loop(0, block_count, note, jnp.int32(0))
    place = lax.broadcasted_iota(jnp.int32, (BLK, LANES), 0)
    across = lax.broadcasted_iota(jnp.int32, (STAT, LANES), 1)

    def split(source, position):
        start = pl.multiple_of(listed[position] * (BLK * kv_count), BLK * kv_count)
        spread[...] = source[pl.ds(start, BLK * kv_count), :].astype(f32)
        return [spread[pl.ds(g, BLK, stride=kv_count), :] for g in range(kv_count)]

    def fetch_keys(position, carry):
        at = pl.ds(pl.multiple_of(position * BLK, BLK), BLK)
        valid = place < kept_counts[position]
        for g, key in enumerate(split(k_ref, position)):
            kd[g, at, :] = jnp.where(valid, key, key[0:1]).astype(bf16)
        return carry

    def fetch_values(position, carry):
        at = pl.ds(pl.multiple_of(position * BLK, BLK), BLK)
        count = kept_counts[position]
        for g, value in enumerate(split(v_ref, position)):
            vt[g, 0:d, at] = jnp.where(place < count, value, 0.0).T.astype(bf16)
            vt[g, d:, at] = (across < count).astype(f32).astype(bf16)
        return carry

    copies[0].wait()
    lax.fori_loop(0, active, fetch_keys, 0)
    copies[1].wait()
    lax.fori_loop(0, active, fetch_values, 0)

    @pl.when(active % 2 == 1)
    def _():
        at = pl.ds(pl.multiple_of(active * BLK, BLK), BLK)
        before = pl.ds(pl.multiple_of((active - 1) * BLK, BLK), BLK)
        for g in range(kv_count):
            kd[g, at, :] = kd[g, before, :]
            vt[g, :, at] = jnp.zeros((d + STAT, BLK), bf16)

    copies[2].wait()
    attend_all(active, [(sent_ref, group, lambda: q_ref[...])], kd, vt)


def attention_kernel(chunk_roles, meta, kd, vt, q_ref, *outs):
    group_size = q_ref.shape[1] // kd.shape[0]
    todo = []
    for out, (chunk, is_other) in zip(outs, chunk_roles):
        group = 2 * chunk + (1 - meta[0] if is_other else meta[0])

        def read(group=group):
            heads = pl.ds(pl.multiple_of(group * group_size, group_size), group_size)
            return q_ref[:, heads, :]

        todo.append((out, group, read))
    attend_all(active_count(meta), todo, kd, vt)


def attend_all(active, todo, kd, vt):
    d = kd.shape[2]
    scale2 = math.log2(math.e) / math.sqrt(d)
    rows = todo[0][0].shape[0] * LANES
    pairs = (active + 1) // 2

    def attend(width, out, group, read):
        q = read().reshape(rows, d)
        scores = lax.dot_general(
            kd[group, 0:width, :], q, (((1,), (1,)), ((), ())), preferred_element_type=f32
        )
        top = (jnp.max(scores, axis=0, keepdims=True) * scale2).astype(bf16).astype(f32)
        weights = jnp.exp2(scores * scale2 - top).astype(bf16)
        sums = jnp.dot(vt[group, :, 0:width], weights, preferred_element_type=f32)
        total = sums[d:]
        high = total.astype(bf16).astype(f32)
        row = lax.broadcasted_iota(jnp.int32, (STAT, rows), 0)
        stats = jnp.where(row == 0, top, jnp.where(row == 1, high, total - high)).astype(bf16)
        value = sums[:d].astype(bf16)
        for piece in range(rows // LANES):
            at = slice(piece * LANES, (piece + 1) * LANES)
            out[piece, 0:d] = value[:, at]
            out[piece, d:] = stats[:, at]

    for n in range(1, kd.shape[1] // (2 * BLK) + 1):

        @pl.when(pairs == n)
        def _(n=n):
            for out, group, read in todo:
                attend(2 * BLK * n, out, group, read)

    @pl.when(pairs == 0)
    def _():
        row = lax.broadcasted_iota(jnp.int32, (d + STAT, LANES), 0)
        empty = jnp.where(row == d, lowest_top, 0.0).astype(bf16)
        for out, _, _ in todo:
            for piece in range(rows // LANES):
                out[piece] = empty


def merged(parts, d):
    stats = [part[d : d + STAT, :].astype(f32) for part in parts]
    tops = [stat[0:1] for stat in stats]
    top = functools.reduce(jnp.maximum, tops)
    out, total = 0.0, 0.0
    for part, stat, one in zip(parts, stats, tops):
        factor = jnp.exp2(one - top)
        out = out + part[0:d, :].astype(f32) * factor
        total = total + (stat[1:2] + stat[2:3]) * factor
    return out, top, total


def store_merged(ref, z, parts):
    d = ref.shape[1] - STAT
    out, stats = pack_state(*merged(parts, d))
    ref[z, 0:d, :] = out
    ref[z, d : d + STAT, :] = stats


def core_kernel(meta, kept, received, *outs):
    my_xy = meta[1]
    z_size = outs[0].shape[0]
    for j, out in enumerate(outs):
        for z in range(z_size):
            piece = (my_xy ^ j) * z_size + z
            store_merged(out, z, [kept[piece], received[piece]])


def plane_kernel(*refs):
    ins, out = refs[:-1], refs[-1]
    for z in range(out.shape[0]):
        store_merged(out, z, [ref[z] for ref in ins])


def last_kernel(*refs):
    ins, out_ref, turned = refs[:-2], refs[-2], refs[-1]
    d = ins[0].shape[1] - STAT
    tokens = out_ref.shape[1]
    heads = LANES // tokens
    for z in range(out_ref.shape[0]):
        out, _, total = merged([ref[z] for ref in ins], d)
        turned[z] = (out / total).T
        for h in range(heads):
            picked = turned[z, pl.ds(h, tokens, stride=heads), :]
            out_ref[z, :, h * d : (h + 1) * d] = picked.astype(bf16)


def project_kernel(terms, has_earlier, last, meta, weight, *refs):
    z_size, tokens, depth = refs[0].shape
    total = refs[4 * len(terms)][...] if has_earlier else None
    out_ref = refs[-1]
    for i, (chunk, is_other) in enumerate(terms):
        left = jnp.concatenate(
            [part[...].reshape(z_size * tokens, depth) for part in refs[4 * i : 4 * i + 4]], axis=0
        )
        group = 2 * chunk + (1 - meta[0] if is_other else meta[0])
        at = pl.ds(pl.multiple_of(group * depth, depth), depth)
        product = jnp.dot(left, weight[at, :], preferred_element_type=f32)
        total = product if total is None else total + product
    if not last:
        out_ref[...] = total
        return
    my_xy = meta[1]
    size = z_size * tokens
    for j in range(4):
        to = pl.ds(pl.multiple_of((my_xy ^ j) * size, size), size)
        out_ref[to, :] = total[j * size : (j + 1) * size]


def hop(value, mask):
    pairs = [(source, source ^ mask) for source in range(lax.axis_size("ctx"))]
    return lax.ppermute(value, "ctx", pairs)


VMEM = pl.BlockSpec(memory_space=pltpu.VMEM)
SMEM = pl.BlockSpec(memory_space=pltpu.SMEM)
HBM = pl.BlockSpec(memory_space=pltpu.HBM)
SMALL = pltpu.CompilerParams(vmem_limit_bytes=4 << 20)


def fast_body(queries, cache_keys, cache_values, block_mask, key_counts, out_weight):
    index = lax.axis_index("ctx")
    z_size = lax.axis_size("ctx") // 8
    token_count, head_count, d = queries.shape
    kv_count = cache_keys.shape[1]
    group_size = head_count // kv_count
    rows = token_count * group_size
    pieces = rows // LANES
    positions = cache_keys.shape[0]
    features = out_weight.shape[1]
    core = index & 1
    my_xy = (index >> 1) & 3
    tall = d + STAT
    keys = cache_keys.reshape(positions * kv_count, d)
    values = cache_values.reshape(positions * kv_count, d)
    place = jnp.concatenate(
        [jnp.stack([core, my_xy]).astype(jnp.int32), block_mask[0], key_counts]
    )
    kept_in_hbm = functools.partial(pltpu.with_memory_space_constraint, memory_space=pltpu.HBM)
    state = jax.ShapeDtypeStruct((z_size, tall, LANES), bf16)

    partial = jax.ShapeDtypeStruct((pieces, tall, LANES), bf16)
    blocks = positions // BLK

    def split_and_attend():
        return pl.pallas_call(
            split_kernel,
            in_specs=[SMEM] + [HBM] * 3,
            out_specs=[VMEM] * 3,
            scratch_shapes=[
                pltpu.SMEM((blocks + 1,), jnp.int32),
                pltpu.SMEM((blocks + 1,), jnp.int32),
                pltpu.VMEM((token_count, group_size, d), bf16),
                pltpu.VMEM((positions * kv_count, d), bf16),
                pltpu.VMEM((positions * kv_count, d), bf16),
                pltpu.VMEM((BLK * kv_count, d), f32),
                pltpu.SemaphoreType.DMA((3,)),
            ],
            out_shape=[
                jax.ShapeDtypeStruct((kv_count, positions, d), bf16),
                jax.ShapeDtypeStruct((kv_count, tall, positions), bf16),
                partial,
            ],
            compiler_params=pltpu.CompilerParams(vmem_limit_bytes=32 << 20),
            cost_estimate=pl.CostEstimate(
                flops=4 * rows * positions * d,
                transcendentals=rows * positions,
                bytes_accessed=4 * positions * d * kv_count,
            ),
            name="split_and_attend",
        )(place, kept_in_hbm(keys), kept_in_hbm(values), kept_in_hbm(queries))

    def attend(chunk_roles, kd, vt):
        count = len(chunk_roles)
        return pl.pallas_call(
            functools.partial(attention_kernel, chunk_roles),
            in_specs=[SMEM] + [VMEM] * 3,
            out_specs=[VMEM] * count,
            out_shape=[partial] * count,
            compiler_params=pltpu.CompilerParams(vmem_limit_bytes=32 << 20),
            cost_estimate=pl.CostEstimate(
                flops=4 * count * rows * positions * d,
                transcendentals=count * rows * positions,
                bytes_accessed=4 * positions * d * count,
            ),
            name="attend",
        )(place, kd, vt, queries)

    def merge_cores(kept, received):
        return pl.pallas_call(
            core_kernel,
            in_specs=[SMEM] + [VMEM] * 2,
            out_specs=[VMEM] * 4,
            out_shape=[state] * 4,
            compiler_params=SMALL,
            name="merge_cores",
        )(place, kept, received)

    def merge_chips(parts):
        return pl.pallas_call(
            plane_kernel,
            in_specs=[VMEM] * len(parts),
            out_specs=VMEM,
            out_shape=state,
            compiler_params=SMALL,
            name="merge_chips",
        )(*parts)

    def finish(parts):
        tokens = LANES // group_size
        return pl.pallas_call(
            last_kernel,
            in_specs=[VMEM] * len(parts),
            out_specs=VMEM,
            out_shape=jax.ShapeDtypeStruct((z_size, tokens, group_size * d), bf16),
            scratch_shapes=[pltpu.VMEM((z_size, LANES, d), f32)],
            compiler_params=SMALL,
            name="finish",
        )(*parts)

    def project(terms, parts, earlier, last=False):
        depth = group_size * d
        more = [] if earlier is None else [earlier]
        return pl.pallas_call(
            functools.partial(project_kernel, terms, bool(more), last),
            in_specs=[SMEM] + [VMEM] * (1 + len(parts) + len(more)),
            out_specs=VMEM,
            out_shape=jax.ShapeDtypeStruct((token_count, features), f32),
            compiler_params=pltpu.CompilerParams(vmem_limit_bytes=8 << 20),
            cost_estimate=pl.CostEstimate(
                flops=2 * len(terms) * token_count * depth * features,
                transcendentals=0,
                bytes_accessed=2 * len(terms) * depth * features,
            ),
            name="project",
        )(place, out_weight, *parts, *more)

    def exchange_plane(kept, received):
        parts = merge_cores(kept, received)
        return [parts[0]] + [hop(parts[j], 2 * j) for j in (1, 2, 3)]

    def exchange_line(parts):
        part = merge_chips(parts)
        reach = 1
        while 2 * reach < z_size:
            part = merge_chips([part, hop(part, 8 * reach)])
            reach *= 2
        return finish([part, hop(part, 8 * reach)])

    def gather_plane(attended):
        return [attended] + [hop(attended, 2 * j) for j in (1, 2, 3)]

    kd, vt, sent = split_and_attend()
    received = hop(sent, 1)
    kept, sent = attend([(0, False), (1, True)], kd, vt)
    next_received = hop(sent, 1)
    parts = merge_cores(kept, received)
    parts, kd = lax.optimization_barrier((parts, kd))
    first = [parts[0]] + [hop(parts[j], 2 * j) for j in (1, 2, 3)]
    (kept,) = attend([(1, False)], kd, vt)
    second = exchange_plane(kept, next_received)
    own = gather_plane(exchange_line(first))
    other = [hop(part, 1) for part in own]
    next_own = gather_plane(exchange_line(second))
    total = project([(0, False), (0, True)], own + other, None)
    next_own[3], total = lax.optimization_barrier((next_own[3], total))
    next_other = [hop(part, 1) for part in next_own]
    total = project([(1, False)], next_own, total)
    return project([(1, True)], next_other, total, last=True)


def partner_of(value, axis, distance):
    mask = 2**distance
    pairs = [(source, source ^ mask) for source in range(lax.axis_size(axis))]
    return lax.ppermute(value, axis, pairs)


def combine(earlier, later):
    out_one, top_one, sum_one = earlier
    out_two, top_two, sum_two = later
    new_top = jnp.maximum(top_one, top_two)
    factor_one = jnp.exp(top_one - new_top)
    factor_two = jnp.exp(top_two - new_top)
    new_out = out_one * factor_one[..., None] + out_two * factor_two[..., None]
    return (new_out, new_top, sum_one * factor_one + sum_two * factor_two)


def keep_state(key_block, run_state):
    return run_state


def partial_rows(rows_q, row_mask, cache_keys, cache_values, key_counts):
    row_count, head_count, head_size = rows_q.shape
    kv_count = cache_keys.shape[1]
    group_size = head_count // kv_count
    grouped = rows_q.reshape(row_count, kv_count, group_size, head_size)
    block_count = cache_keys.shape[0] // BLK
    score_scale = 1.0 / math.sqrt(head_size)
    offsets = jnp.arange(BLK, dtype=jnp.int32)

    def update(key_block, run_state):
        out_sum, top_score, weight_sum = run_state
        key_part = lax.dynamic_slice_in_dim(cache_keys, key_block * BLK, BLK, 0)
        value_part = lax.dynamic_slice_in_dim(cache_values, key_block * BLK, BLK, 0)
        scores = (
            jnp.einsum("rgqd,kgd->rgqk", grouped, key_part, preferred_element_type=jnp.float32)
            * score_scale
        )
        active_rows = lax.dynamic_slice_in_dim(row_mask, key_block, 1, 1)[:, 0] > 0
        valid_count = lax.dynamic_slice_in_dim(key_counts, key_block, 1, 0)[0]
        valid = active_rows[:, None, None, None] & (offsets < valid_count)[None, None, None, :]
        scores = jnp.where(valid, scores, very_low)
        new_top = jnp.maximum(top_score, jnp.max(scores, axis=-1))
        weights = jnp.where(valid, jnp.exp(scores - new_top[..., None]), 0.0)
        factor = jnp.exp(top_score - new_top)
        new_sum = weight_sum * factor + jnp.sum(weights, axis=-1)
        new_out = out_sum * factor[..., None] + jnp.einsum(
            "rgqk,kgd->rgqd",
            weights.astype(jnp.bfloat16),
            value_part,
            preferred_element_type=jnp.float32,
        )
        return (new_out, new_top, new_sum)

    def visit_block(key_block, run_state):
        active = jnp.any(lax.dynamic_slice_in_dim(row_mask, key_block, 1, 1) > 0)
        return lax.cond(active, update, keep_state, key_block, run_state)

    initial = (
        jnp.zeros((row_count, kv_count, group_size, head_size), jnp.float32),
        jnp.full((row_count, kv_count, group_size), very_low, jnp.float32),
        jnp.zeros((row_count, kv_count, group_size), jnp.float32),
    )
    return lax.fori_loop(0, block_count, visit_block, initial)


def general_body(queries, cache_keys, cache_values, block_mask, key_counts, out_weight):
    cycle_size = lax.axis_size("ctx")
    cycle_index = lax.axis_index("ctx")
    token_count, head_count, head_size = queries.shape
    segment = token_count // cycle_size
    query_blocks = queries.reshape(block_mask.shape[0], BLK, head_count, head_size)

    def per_block(block_item):
        rows_q, mask_row = block_item
        row_mask = jnp.broadcast_to(mask_row[None, :], (BLK, mask_row.shape[0]))
        return partial_rows(rows_q, row_mask, cache_keys, cache_values, key_counts)

    stacked = lax.map(per_block, (query_blocks, block_mask))
    run_state = tuple((part.reshape((token_count,) + part.shape[2:]) for part in stacked))
    bit_total = cycle_size.bit_length() - 1
    for bit_number in range(bit_total - 1, -1, -1):
        half_rows = run_state[1].shape[0] // 2
        upper_half = jnp.bitwise_and(jnp.right_shift(cycle_index, bit_number), 1)
        kept = tuple(
            (
                lax.dynamic_slice_in_dim(part, upper_half * half_rows, half_rows, 0)
                for part in run_state
            )
        )
        outgoing = tuple(
            (
                lax.dynamic_slice_in_dim(part, (1 - upper_half) * half_rows, half_rows, 0)
                for part in run_state
            )
        )
        received = partner_of((outgoing[0], outgoing[1], outgoing[2]), "ctx", bit_number)
        run_state = combine(kept, received)
    out_sum, top_score, weight_sum = run_state
    attended = (
        (out_sum / weight_sum[..., None])
        .astype(jnp.bfloat16)
        .reshape(segment, head_count * head_size)
    )
    partial_value = jnp.dot(
        lax.all_gather(attended, "ctx", axis=0, tiled=True),
        out_weight,
        preferred_element_type=jnp.float32,
    )
    return lax.psum_scatter(partial_value, "kv", scatter_dimension=0, tiled=True)


def body(queries, cache_keys, cache_values, block_mask, key_counts, out_weight):
    devices = lax.axis_size("ctx")
    token_count, head_count, d = queries.shape
    kv_count = cache_keys.shape[1]
    group_size = head_count // kv_count
    suits = (
        lax.axis_size("kv") == 1
        and devices == 32
        and token_count == BLK
        and block_mask.shape[0] == 1
        and kv_count == 4
        and d == LANES
        and group_size == 16
        and token_count * group_size == LANES * (devices // 2)
    )
    run = fast_body if suits else general_body
    return run(queries, cache_keys, cache_values, block_mask, key_counts, out_weight)


def solution(mesh):
    placed = (
        P("groups", "kv", None),
        P(("groups", "ctx"), "kv", None),
        P(("groups", "ctx"), "kv", None),
        P("groups", "ctx"),
        P(("groups", "ctx")),
        P("kv", "ctx"),
    )
    return jax.shard_map(
        body, mesh=mesh, in_specs=placed, out_specs=P(("groups", "kv"), "ctx"), check_vma=False
    )
```

```python
import functools
import math

import jax
import jax.numpy as jnp
from jax import lax
from jax.experimental import pallas as pl
from jax.experimental.pallas import tpu as pltpu
from jax.sharding import PartitionSpec as P

BLK = 128
LANES = 128
STAT = 16
PLACE = 3
very_low = -1e30
lowest_top = -(2.0**99)
bf16 = jnp.bfloat16
f32 = jnp.float32


def pack_state(out, top, total):
    high = total.astype(bf16).astype(f32)
    low = total - high
    row = lax.broadcasted_iota(jnp.int32, (STAT, LANES), 0)
    stats = jnp.where(row == 0, top, jnp.where(row == 1, high, jnp.where(row == 2, low, 0.0)))
    return out.astype(bf16), stats.astype(bf16)


def active_count(meta):
    block_count = (meta.shape[0] - PLACE) // 2
    return sum((meta[PLACE + block] > 0).astype(jnp.int32) for block in range(block_count))


def split_kernel(meta, k_hbm, v_hbm, q_hbm, kd, vt, sent_ref, *scratch):
    listed, kept_counts, q_ref, k_ref, v_ref, spread, sems = scratch
    d = k_hbm.shape[1]
    kv_count = kd.shape[0]
    group_size = q_ref.shape[1]
    block_count = (meta.shape[0] - PLACE) // 2
    group = 1 - meta[0]

    heads = pl.ds(pl.multiple_of(group * group_size, group_size), group_size)
    copies = [
        pltpu.make_async_copy(k_hbm, k_ref, sems.at[0]),
        pltpu.make_async_copy(v_hbm, v_ref, sems.at[1]),
        pltpu.make_async_copy(q_hbm.at[:, heads, :], q_ref, sems.at[2]),
    ]
    for copy in copies:
        copy.start()

    def note(block, found):
        listed[found] = block
        kept_counts[found] = meta[PLACE + block_count + block]
        return found + (meta[PLACE + block] > 0).astype(jnp.int32)

    active = lax.fori_loop(0, block_count, note, jnp.int32(0))
    place = lax.broadcasted_iota(jnp.int32, (BLK, LANES), 0)
    across = lax.broadcasted_iota(jnp.int32, (STAT, LANES), 1)

    def split(source, position):
        start = pl.multiple_of(listed[position] * (BLK * kv_count), BLK * kv_count)
        spread[...] = source[pl.ds(start, BLK * kv_count), :].astype(f32)
        return [spread[pl.ds(g, BLK, stride=kv_count), :] for g in range(kv_count)]

    def fetch_keys(position, carry):
        at = pl.ds(pl.multiple_of(position * BLK, BLK), BLK)
        valid = place < kept_counts[position]
        for g, key in enumerate(split(k_ref, position)):
            kd[g, at, :] = jnp.where(valid, key, key[0:1]).astype(bf16)
        return carry

    def fetch_values(position, carry):
        at = pl.ds(pl.multiple_of(position * BLK, BLK), BLK)
        count = kept_counts[position]
        for g, value in enumerate(split(v_ref, position)):
            vt[g, 0:d, at] = jnp.where(place < count, value, 0.0).T.astype(bf16)
            vt[g, d:, at] = (across < count).astype(f32).astype(bf16)
        return carry

    copies[0].wait()
    lax.fori_loop(0, active, fetch_keys, 0)
    copies[1].wait()
    lax.fori_loop(0, active, fetch_values, 0)

    @pl.when(active % 2 == 1)
    def _():
        at = pl.ds(pl.multiple_of(active * BLK, BLK), BLK)
        before = pl.ds(pl.multiple_of((active - 1) * BLK, BLK), BLK)
        for g in range(kv_count):
            kd[g, at, :] = kd[g, before, :]
            vt[g, :, at] = jnp.zeros((d + STAT, BLK), bf16)

    copies[2].wait()
    attend_all(active, [(sent_ref, group, lambda: q_ref[...])], kd, vt)


def attention_kernel(chunk_roles, meta, kd, vt, q_ref, *outs):
    group_size = q_ref.shape[1] // kd.shape[0]
    todo = []
    for out, (chunk, is_other) in zip(outs, chunk_roles):
        group = 2 * chunk + (1 - meta[0] if is_other else meta[0])

        def read(group=group):
            heads = pl.ds(pl.multiple_of(group * group_size, group_size), group_size)
            return q_ref[:, heads, :]

        todo.append((out, group, read))
    attend_all(active_count(meta), todo, kd, vt)


def attend_all(active, todo, kd, vt):
    d = kd.shape[2]
    scale2 = math.log2(math.e) / math.sqrt(d)
    rows = todo[0][0].shape[0] * LANES
    pairs = (active + 1) // 2

    def attend(width, out, group, read):
        q = read().reshape(rows, d)
        scores = lax.dot_general(
            kd[group, 0:width, :], q, (((1,), (1,)), ((), ())), preferred_element_type=f32
        )
        top = (jnp.max(scores, axis=0, keepdims=True) * scale2).astype(bf16).astype(f32)
        weights = jnp.exp2(scores * scale2 - top).astype(bf16)
        sums = jnp.dot(vt[group, :, 0:width], weights, preferred_element_type=f32)
        total = sums[d:]
        high = total.astype(bf16).astype(f32)
        row = lax.broadcasted_iota(jnp.int32, (STAT, rows), 0)
        stats = jnp.where(row == 0, top, jnp.where(row == 1, high, total - high)).astype(bf16)
        value = sums[:d].astype(bf16)
        for piece in range(rows // LANES):
            at = slice(piece * LANES, (piece + 1) * LANES)
            out[piece, 0:d] = value[:, at]
            out[piece, d:] = stats[:, at]

    for n in range(1, kd.shape[1] // (2 * BLK) + 1):

        @pl.when(pairs == n)
        def _(n=n):
            for out, group, read in todo:
                attend(2 * BLK * n, out, group, read)

    @pl.when(pairs == 0)
    def _():
        row = lax.broadcasted_iota(jnp.int32, (d + STAT, LANES), 0)
        empty = jnp.where(row == d, lowest_top, 0.0).astype(bf16)
        for out, _, _ in todo:
            for piece in range(rows // LANES):
                out[piece] = empty


def merged(parts, d):
    stats = [part[d : d + STAT, :].astype(f32) for part in parts]
    tops = [stat[0:1] for stat in stats]
    top = functools.reduce(jnp.maximum, tops)
    out, total = 0.0, 0.0
    for part, stat, one in zip(parts, stats, tops):
        factor = jnp.exp2(one - top)
        out = out + part[0:d, :].astype(f32) * factor
        total = total + (stat[1:2] + stat[2:3]) * factor
    return out, top, total


def store_merged(ref, z, parts):
    d = ref.shape[1] - STAT
    out, stats = pack_state(*merged(parts, d))
    ref[z, 0:d, :] = out
    ref[z, d : d + STAT, :] = stats


def core_kernel(meta, kept, received, *outs):
    my_xy = meta[1]
    z_size = outs[0].shape[0]
    for j, out in enumerate(outs):
        for z in range(z_size):
            piece = (my_xy ^ j) * z_size + z
            store_merged(out, z, [kept[piece], received[piece]])


def plane_kernel(meta, *refs):
    ins, kept, sent = refs[:-2], refs[-2], refs[-1]
    parity = meta[2] & 1
    for out, first in ((sent, 1 - parity), (kept, parity)):
        for i in range(out.shape[0]):
            store_merged(out, i, [ref[first + 2 * i] for ref in ins])


def line_kernel(*refs):
    ins, out = refs[:-1], refs[-1]
    for i in range(out.shape[0]):
        store_merged(out, i, [ref[i] for ref in ins])


def join_kernel(meta, own, other, out):
    parity = meta[2] & 1
    for ref, first in ((own, parity), (other, 1 - parity)):
        for i in range(ref.shape[0]):
            out[first + 2 * i] = ref[i]


def last_kernel(*refs):
    ins, out_ref, turned = refs[:-2], refs[-2], refs[-1]
    d = ins[0].shape[1] - STAT
    tokens = out_ref.shape[1]
    heads = LANES // tokens
    for z in range(out_ref.shape[0]):
        out, _, total = merged([ref[z] for ref in ins], d)
        turned[z] = (out / total).T
        for h in range(heads):
            picked = turned[z, pl.ds(h, tokens, stride=heads), :]
            out_ref[z, :, h * d : (h + 1) * d] = picked.astype(bf16)


def project_kernel(terms, has_earlier, last, meta, weight, *refs):
    z_size, tokens, depth = refs[0].shape
    total = refs[4 * len(terms)][...] if has_earlier else None
    out_ref = refs[-1]
    for i, (chunk, is_other) in enumerate(terms):
        left = jnp.concatenate(
            [part[...].reshape(z_size * tokens, depth) for part in refs[4 * i : 4 * i + 4]], axis=0
        )
        group = 2 * chunk + (1 - meta[0] if is_other else meta[0])
        at = pl.ds(pl.multiple_of(group * depth, depth), depth)
        product = jnp.dot(left, weight[at, :], preferred_element_type=f32)
        total = product if total is None else total + product
    if not last:
        out_ref[...] = total
        return
    my_xy = meta[1]
    size = z_size * tokens
    for j in range(4):
        to = pl.ds(pl.multiple_of((my_xy ^ j) * size, size), size)
        out_ref[to, :] = total[j * size : (j + 1) * size]


def hop(value, mask):
    pairs = [(source, source ^ mask) for source in range(lax.axis_size("ctx"))]
    return lax.ppermute(value, "ctx", pairs)


VMEM = pl.BlockSpec(memory_space=pltpu.VMEM)
SMEM = pl.BlockSpec(memory_space=pltpu.SMEM)
HBM = pl.BlockSpec(memory_space=pltpu.HBM)
SMALL = pltpu.CompilerParams(vmem_limit_bytes=4 << 20)


def fast_body(queries, cache_keys, cache_values, block_mask, key_counts, out_weight):
    index = lax.axis_index("ctx")
    z_size = lax.axis_size("ctx") // 8
    token_count, head_count, d = queries.shape
    kv_count = cache_keys.shape[1]
    group_size = head_count // kv_count
    rows = token_count * group_size
    pieces = rows // LANES
    positions = cache_keys.shape[0]
    features = out_weight.shape[1]
    core = index & 1
    my_xy = (index >> 1) & 3
    my_z = index >> 3
    tall = d + STAT
    keys = cache_keys.reshape(positions * kv_count, d)
    values = cache_values.reshape(positions * kv_count, d)
    place = jnp.concatenate(
        [jnp.stack([core, my_xy, my_z]).astype(jnp.int32), block_mask[0], key_counts]
    )
    kept_in_hbm = functools.partial(pltpu.with_memory_space_constraint, memory_space=pltpu.HBM)
    state = jax.ShapeDtypeStruct((z_size, tall, LANES), bf16)

    partial = jax.ShapeDtypeStruct((pieces, tall, LANES), bf16)
    blocks = positions // BLK

    def split_and_attend():
        return pl.pallas_call(
            split_kernel,
            in_specs=[SMEM] + [HBM] * 3,
            out_specs=[VMEM] * 3,
            scratch_shapes=[
                pltpu.SMEM((blocks + 1,), jnp.int32),
                pltpu.SMEM((blocks + 1,), jnp.int32),
                pltpu.VMEM((token_count, group_size, d), bf16),
                pltpu.VMEM((positions * kv_count, d), bf16),
                pltpu.VMEM((positions * kv_count, d), bf16),
                pltpu.VMEM((BLK * kv_count, d), f32),
                pltpu.SemaphoreType.DMA((3,)),
            ],
            out_shape=[
                jax.ShapeDtypeStruct((kv_count, positions, d), bf16),
                jax.ShapeDtypeStruct((kv_count, tall, positions), bf16),
                partial,
            ],
            compiler_params=pltpu.CompilerParams(vmem_limit_bytes=32 << 20),
            cost_estimate=pl.CostEstimate(
                flops=4 * rows * positions * d,
                transcendentals=rows * positions,
                bytes_accessed=4 * positions * d * kv_count,
            ),
            name="split_and_attend",
        )(place, kept_in_hbm(keys), kept_in_hbm(values), kept_in_hbm(queries))

    def attend(chunk_roles, kd, vt):
        count = len(chunk_roles)
        return pl.pallas_call(
            functools.partial(attention_kernel, chunk_roles),
            in_specs=[SMEM] + [VMEM] * 3,
            out_specs=[VMEM] * count,
            out_shape=[partial] * count,
            compiler_params=pltpu.CompilerParams(vmem_limit_bytes=32 << 20),
            cost_estimate=pl.CostEstimate(
                flops=4 * count * rows * positions * d,
                transcendentals=count * rows * positions,
                bytes_accessed=4 * positions * d * count,
            ),
            name="attend",
        )(place, kd, vt, queries)

    def merge_cores(kept, received):
        return pl.pallas_call(
            core_kernel,
            in_specs=[SMEM] + [VMEM] * 2,
            out_specs=[VMEM] * 4,
            out_shape=[state] * 4,
            compiler_params=SMALL,
            name="merge_cores",
        )(place, kept, received)

    half = jax.ShapeDtypeStruct((z_size // 2, tall, LANES), bf16)
    tokens = LANES // group_size

    def merge_plane(parts):
        return pl.pallas_call(
            plane_kernel,
            in_specs=[SMEM] + [VMEM] * len(parts),
            out_specs=[VMEM] * 2,
            out_shape=[half] * 2,
            compiler_params=SMALL,
            name="merge_plane",
        )(place, *parts)

    def merge_line(parts):
        return pl.pallas_call(
            line_kernel,
            in_specs=[VMEM] * len(parts),
            out_specs=VMEM,
            out_shape=half,
            compiler_params=SMALL,
            name="merge_line",
        )(*parts)

    def finish(parts):
        return pl.pallas_call(
            last_kernel,
            in_specs=[VMEM] * len(parts),
            out_specs=VMEM,
            out_shape=jax.ShapeDtypeStruct((z_size // 2, tokens, group_size * d), bf16),
            scratch_shapes=[pltpu.VMEM((z_size // 2, LANES, d), f32)],
            compiler_params=SMALL,
            name="finish",
        )(*parts)

    def join(own, other):
        return pl.pallas_call(
            join_kernel,
            in_specs=[SMEM] + [VMEM] * 2,
            out_specs=VMEM,
            out_shape=jax.ShapeDtypeStruct((z_size, tokens, group_size * d), bf16),
            compiler_params=SMALL,
            name="join",
        )(place, own, other)

    def project(terms, parts, earlier, last=False):
        depth = group_size * d
        more = [] if earlier is None else [earlier]
        return pl.pallas_call(
            functools.partial(project_kernel, terms, bool(more), last),
            in_specs=[SMEM] + [VMEM] * (1 + len(parts) + len(more)),
            out_specs=VMEM,
            out_shape=jax.ShapeDtypeStruct((token_count, features), f32),
            compiler_params=pltpu.CompilerParams(vmem_limit_bytes=8 << 20),
            cost_estimate=pl.CostEstimate(
                flops=2 * len(terms) * token_count * depth * features,
                transcendentals=0,
                bytes_accessed=2 * len(terms) * depth * features,
            ),
            name="project",
        )(place, out_weight, *parts, *more)

    def exchange_plane(kept, received):
        parts = merge_cores(kept, received)
        return [parts[0]] + [hop(parts[j], 2 * j) for j in (1, 2, 3)]

    def exchange_line(parts):
        kept, sent = merge_plane(parts)
        part = merge_line([kept, hop(sent, 8)])
        attended = finish([part, hop(part, 16)])
        return join(attended, hop(attended, 8))

    def gather_plane(attended):
        return [attended] + [hop(attended, 2 * j) for j in (1, 2, 3)]

    kd, vt, sent = split_and_attend()
    received = hop(sent, 1)
    kept, sent = attend([(0, False), (1, True)], kd, vt)
    next_received = hop(sent, 1)
    parts = merge_cores(kept, received)
    parts, kd = lax.optimization_barrier((parts, kd))
    first = [parts[0]] + [hop(parts[j], 2 * j) for j in (1, 2, 3)]
    (kept,) = attend([(1, False)], kd, vt)
    second = exchange_plane(kept, next_received)
    own = gather_plane(exchange_line(first))
    other = [hop(part, 1) for part in own]
    next_own = gather_plane(exchange_line(second))
    total = project([(0, False), (0, True)], own + other, None)
    next_own[3], total = lax.optimization_barrier((next_own[3], total))
    next_other = [hop(part, 1) for part in next_own]
    total = project([(1, False)], next_own, total)
    return project([(1, True)], next_other, total, last=True)


def partner_of(value, axis, distance):
    mask = 2**distance
    pairs = [(source, source ^ mask) for source in range(lax.axis_size(axis))]
    return lax.ppermute(value, axis, pairs)


def combine(earlier, later):
    out_one, top_one, sum_one = earlier
    out_two, top_two, sum_two = later
    new_top = jnp.maximum(top_one, top_two)
    factor_one = jnp.exp(top_one - new_top)
    factor_two = jnp.exp(top_two - new_top)
    new_out = out_one * factor_one[..., None] + out_two * factor_two[..., None]
    return (new_out, new_top, sum_one * factor_one + sum_two * factor_two)


def keep_state(key_block, run_state):
    return run_state


def partial_rows(rows_q, row_mask, cache_keys, cache_values, key_counts):
    row_count, head_count, head_size = rows_q.shape
    kv_count = cache_keys.shape[1]
    group_size = head_count // kv_count
    grouped = rows_q.reshape(row_count, kv_count, group_size, head_size)
    block_count = cache_keys.shape[0] // BLK
    score_scale = 1.0 / math.sqrt(head_size)
    offsets = jnp.arange(BLK, dtype=jnp.int32)

    def update(key_block, run_state):
        out_sum, top_score, weight_sum = run_state
        key_part = lax.dynamic_slice_in_dim(cache_keys, key_block * BLK, BLK, 0)
        value_part = lax.dynamic_slice_in_dim(cache_values, key_block * BLK, BLK, 0)
        scores = (
            jnp.einsum("rgqd,kgd->rgqk", grouped, key_part, preferred_element_type=jnp.float32)
            * score_scale
        )
        active_rows = lax.dynamic_slice_in_dim(row_mask, key_block, 1, 1)[:, 0] > 0
        valid_count = lax.dynamic_slice_in_dim(key_counts, key_block, 1, 0)[0]
        valid = active_rows[:, None, None, None] & (offsets < valid_count)[None, None, None, :]
        scores = jnp.where(valid, scores, very_low)
        new_top = jnp.maximum(top_score, jnp.max(scores, axis=-1))
        weights = jnp.where(valid, jnp.exp(scores - new_top[..., None]), 0.0)
        factor = jnp.exp(top_score - new_top)
        new_sum = weight_sum * factor + jnp.sum(weights, axis=-1)
        new_out = out_sum * factor[..., None] + jnp.einsum(
            "rgqk,kgd->rgqd",
            weights.astype(jnp.bfloat16),
            value_part,
            preferred_element_type=jnp.float32,
        )
        return (new_out, new_top, new_sum)

    def visit_block(key_block, run_state):
        active = jnp.any(lax.dynamic_slice_in_dim(row_mask, key_block, 1, 1) > 0)
        return lax.cond(active, update, keep_state, key_block, run_state)

    initial = (
        jnp.zeros((row_count, kv_count, group_size, head_size), jnp.float32),
        jnp.full((row_count, kv_count, group_size), very_low, jnp.float32),
        jnp.zeros((row_count, kv_count, group_size), jnp.float32),
    )
    return lax.fori_loop(0, block_count, visit_block, initial)


def general_body(queries, cache_keys, cache_values, block_mask, key_counts, out_weight):
    cycle_size = lax.axis_size("ctx")
    cycle_index = lax.axis_index("ctx")
    token_count, head_count, head_size = queries.shape
    segment = token_count // cycle_size
    query_blocks = queries.reshape(block_mask.shape[0], BLK, head_count, head_size)

    def per_block(block_item):
        rows_q, mask_row = block_item
        row_mask = jnp.broadcast_to(mask_row[None, :], (BLK, mask_row.shape[0]))
        return partial_rows(rows_q, row_mask, cache_keys, cache_values, key_counts)

    stacked = lax.map(per_block, (query_blocks, block_mask))
    run_state = tuple((part.reshape((token_count,) + part.shape[2:]) for part in stacked))
    bit_total = cycle_size.bit_length() - 1
    for bit_number in range(bit_total - 1, -1, -1):
        half_rows = run_state[1].shape[0] // 2
        upper_half = jnp.bitwise_and(jnp.right_shift(cycle_index, bit_number), 1)
        kept = tuple(
            (
                lax.dynamic_slice_in_dim(part, upper_half * half_rows, half_rows, 0)
                for part in run_state
            )
        )
        outgoing = tuple(
            (
                lax.dynamic_slice_in_dim(part, (1 - upper_half) * half_rows, half_rows, 0)
                for part in run_state
            )
        )
        received = partner_of((outgoing[0], outgoing[1], outgoing[2]), "ctx", bit_number)
        run_state = combine(kept, received)
    out_sum, top_score, weight_sum = run_state
    attended = (
        (out_sum / weight_sum[..., None])
        .astype(jnp.bfloat16)
        .reshape(segment, head_count * head_size)
    )
    partial_value = jnp.dot(
        lax.all_gather(attended, "ctx", axis=0, tiled=True),
        out_weight,
        preferred_element_type=jnp.float32,
    )
    return lax.psum_scatter(partial_value, "kv", scatter_dimension=0, tiled=True)


def body(queries, cache_keys, cache_values, block_mask, key_counts, out_weight):
    devices = lax.axis_size("ctx")
    token_count, head_count, d = queries.shape
    kv_count = cache_keys.shape[1]
    group_size = head_count // kv_count
    suits = (
        lax.axis_size("kv") == 1
        and devices == 32
        and token_count == BLK
        and block_mask.shape[0] == 1
        and kv_count == 4
        and d == LANES
        and group_size == 16
        and token_count * group_size == LANES * (devices // 2)
    )
    run = fast_body if suits else general_body
    return run(queries, cache_keys, cache_values, block_mask, key_counts, out_weight)


def solution(mesh):
    placed = (
        P("groups", "kv", None),
        P(("groups", "ctx"), "kv", None),
        P(("groups", "ctx"), "kv", None),
        P("groups", "ctx"),
        P(("groups", "ctx")),
        P("kv", "ctx"),
    )
    return jax.shard_map(
        body, mesh=mesh, in_specs=placed, out_specs=P(("groups", "kv"), "ctx"), check_vma=False
    )
```

```python
import functools
import math

import jax
import jax.numpy as jnp
from jax import lax
from jax.experimental import pallas as pl
from jax.experimental.pallas import tpu as pltpu
from jax.sharding import PartitionSpec as P

BLK = 128
LANES = 128
STAT = 16
very_low = -1e30
lowest_top = -(2.0**99)
bf16 = jnp.bfloat16
f32 = jnp.float32


def pack_state(out, top, total):
    high = total.astype(bf16).astype(f32)
    low = total - high
    row = lax.broadcasted_iota(jnp.int32, (STAT, LANES), 0)
    stats = jnp.where(row == 0, top, jnp.where(row == 1, high, jnp.where(row == 2, low, 0.0)))
    return out.astype(bf16), stats.astype(bf16)


def active_count(meta):
    block_count = (meta.shape[0] - 2) // 2
    return sum((meta[2 + block] > 0).astype(jnp.int32) for block in range(block_count))


def split_kernel(meta, k_hbm, v_hbm, q_hbm, kd, vt, sent_ref, *scratch):
    listed, kept_counts, q_ref, k_ref, v_ref, spread, sems = scratch
    d = k_hbm.shape[1]
    kv_count = kd.shape[0]
    group_size = q_ref.shape[1]
    block_count = (meta.shape[0] - 2) // 2
    group = 1 - meta[0]

    heads = pl.ds(pl.multiple_of(group * group_size, group_size), group_size)
    copies = [
        pltpu.make_async_copy(k_hbm, k_ref, sems.at[0]),
        pltpu.make_async_copy(v_hbm, v_ref, sems.at[1]),
        pltpu.make_async_copy(q_hbm.at[:, heads, :], q_ref, sems.at[2]),
    ]
    for copy in copies:
        copy.start()

    def note(block, found):
        listed[found] = block
        kept_counts[found] = meta[2 + block_count + block]
        return found + (meta[2 + block] > 0).astype(jnp.int32)

    active = lax.fori_loop(0, block_count, note, jnp.int32(0))
    place = lax.broadcasted_iota(jnp.int32, (BLK, LANES), 0)
    across = lax.broadcasted_iota(jnp.int32, (STAT, LANES), 1)

    def split(source, position):
        start = pl.multiple_of(listed[position] * (BLK * kv_count), BLK * kv_count)
        spread[...] = source[pl.ds(start, BLK * kv_count), :].astype(f32)
        return [spread[pl.ds(g, BLK, stride=kv_count), :] for g in range(kv_count)]

    def fetch_keys(position, carry):
        at = pl.ds(pl.multiple_of(position * BLK, BLK), BLK)
        valid = place < kept_counts[position]
        for g, key in enumerate(split(k_ref, position)):
            kd[g, at, :] = jnp.where(valid, key, key[0:1]).astype(bf16)
        return carry

    def fetch_values(position, carry):
        at = pl.ds(pl.multiple_of(position * BLK, BLK), BLK)
        count = kept_counts[position]
        for g, value in enumerate(split(v_ref, position)):
            vt[g, 0:d, at] = jnp.where(place < count, value, 0.0).T.astype(bf16)
            vt[g, d:, at] = (across < count).astype(f32).astype(bf16)
        return carry

    copies[0].wait()
    lax.fori_loop(0, active, fetch_keys, 0)
    copies[1].wait()
    lax.fori_loop(0, active, fetch_values, 0)

    @pl.when(active % 2 == 1)
    def _():
        at = pl.ds(pl.multiple_of(active * BLK, BLK), BLK)
        before = pl.ds(pl.multiple_of((active - 1) * BLK, BLK), BLK)
        for g in range(kv_count):
            kd[g, at, :] = kd[g, before, :]
            vt[g, :, at] = jnp.zeros((d + STAT, BLK), bf16)

    copies[2].wait()
    attend_all(active, [(sent_ref, group, lambda: q_ref[...])], kd, vt)


def attention_kernel(chunk_roles, meta, kd, vt, q_ref, *outs):
    group_size = q_ref.shape[1] // kd.shape[0]
    todo = []
    for out, (chunk, is_other) in zip(outs, chunk_roles):
        group = 2 * chunk + (1 - meta[0] if is_other else meta[0])

        def read(group=group):
            heads = pl.ds(pl.multiple_of(group * group_size, group_size), group_size)
            return q_ref[:, heads, :]

        todo.append((out, group, read))
    attend_all(active_count(meta), todo, kd, vt)


def attend_all(active, todo, kd, vt):
    d = kd.shape[2]
    scale2 = math.log2(math.e) / math.sqrt(d)
    rows = todo[0][0].shape[0] * LANES
    pairs = (active + 1) // 2

    def attend(width, out, group, read):
        q = read().reshape(rows, d)
        scores = lax.dot_general(
            kd[group, 0:width, :], q, (((1,), (1,)), ((), ())), preferred_element_type=f32
        )
        top = (jnp.max(scores, axis=0, keepdims=True) * scale2).astype(bf16).astype(f32)
        weights = jnp.exp2(scores * scale2 - top).astype(bf16)
        sums = jnp.dot(vt[group, :, 0:width], weights, preferred_element_type=f32)
        total = sums[d:]
        high = total.astype(bf16).astype(f32)
        row = lax.broadcasted_iota(jnp.int32, (STAT, rows), 0)
        stats = jnp.where(row == 0, top, jnp.where(row == 1, high, total - high)).astype(bf16)
        value = sums[:d].astype(bf16)
        for piece in range(rows // LANES):
            at = slice(piece * LANES, (piece + 1) * LANES)
            out[piece, 0:d] = value[:, at]
            out[piece, d:] = stats[:, at]

    for n in range(1, kd.shape[1] // (2 * BLK) + 1):

        @pl.when(pairs == n)
        def _(n=n):
            for out, group, read in todo:
                attend(2 * BLK * n, out, group, read)

    @pl.when(pairs == 0)
    def _():
        row = lax.broadcasted_iota(jnp.int32, (d + STAT, LANES), 0)
        empty = jnp.where(row == d, lowest_top, 0.0).astype(bf16)
        for out, _, _ in todo:
            for piece in range(rows // LANES):
                out[piece] = empty


def merged(parts, d):
    stats = [part[d : d + STAT, :].astype(f32) for part in parts]
    tops = [stat[0:1] for stat in stats]
    top = functools.reduce(jnp.maximum, tops)
    out, total = 0.0, 0.0
    for part, stat, one in zip(parts, stats, tops):
        factor = jnp.exp2(one - top)
        out = out + part[0:d, :].astype(f32) * factor
        total = total + (stat[1:2] + stat[2:3]) * factor
    return out, top, total


def store_merged(ref, z, parts):
    d = ref.shape[1] - STAT
    out, stats = pack_state(*merged(parts, d))
    ref[z, 0:d, :] = out
    ref[z, d : d + STAT, :] = stats


def plane_chips(meta):
    core, my_xy = meta[0], meta[1]
    return [my_xy, my_xy ^ (1 + core), my_xy ^ (2 - core), my_xy ^ 3]


def core_kernel(meta, kept, received, *outs):
    z_size = outs[0].shape[0]
    for chip, out in zip(plane_chips(meta), outs):
        for z in range(z_size):
            piece = chip * z_size + z
            store_merged(out, z, [kept[piece], received[piece]])


def plane_kernel(*refs):
    ins, out = refs[:-1], refs[-1]
    for z in range(out.shape[0]):
        store_merged(out, z, [ref[z] for ref in ins])


def last_kernel(*refs):
    ins, out_ref, turned = refs[:-2], refs[-2], refs[-1]
    d = ins[0].shape[1] - STAT
    tokens = out_ref.shape[1]
    heads = LANES // tokens
    for z in range(out_ref.shape[0]):
        out, _, total = merged([ref[z] for ref in ins], d)
        turned[z] = (out / total).T
        for h in range(heads):
            picked = turned[z, pl.ds(h, tokens, stride=heads), :]
            out_ref[z, :, h * d : (h + 1) * d] = picked.astype(bf16)


def project_kernel(terms, has_earlier, last, meta, weight, *refs):
    z_size, tokens, depth = refs[0].shape
    total = refs[4 * len(terms)][...] if has_earlier else None
    out_ref = refs[-1]
    for i, (chunk, is_other) in enumerate(terms):
        left = jnp.concatenate(
            [part[...].reshape(z_size * tokens, depth) for part in refs[4 * i : 4 * i + 4]], axis=0
        )
        group = 2 * chunk + (1 - meta[0] if is_other else meta[0])
        at = pl.ds(pl.multiple_of(group * depth, depth), depth)
        product = jnp.dot(left, weight[at, :], preferred_element_type=f32)
        total = product if total is None else total + product
    if not last:
        out_ref[...] = total
        return
    size = z_size * tokens
    for j, chip in enumerate(plane_chips(meta)):
        to = pl.ds(pl.multiple_of(chip * size, size), size)
        out_ref[to, :] = total[j * size : (j + 1) * size]


def hop(value, mask):
    pairs = [(source, source ^ mask) for source in range(lax.axis_size("ctx"))]
    return lax.ppermute(value, "ctx", pairs)


def plane_hop(value, number):
    masks = {1: (2, 4), 2: (4, 2), 3: (6, 6)}[number]
    pairs = [(source, source ^ masks[source % 2]) for source in range(lax.axis_size("ctx"))]
    return lax.ppermute(value, "ctx", pairs)


VMEM = pl.BlockSpec(memory_space=pltpu.VMEM)
SMEM = pl.BlockSpec(memory_space=pltpu.SMEM)
HBM = pl.BlockSpec(memory_space=pltpu.HBM)
SMALL = pltpu.CompilerParams(vmem_limit_bytes=4 << 20)


def fast_body(queries, cache_keys, cache_values, block_mask, key_counts, out_weight):
    index = lax.axis_index("ctx")
    z_size = lax.axis_size("ctx") // 8
    token_count, head_count, d = queries.shape
    kv_count = cache_keys.shape[1]
    group_size = head_count // kv_count
    rows = token_count * group_size
    pieces = rows // LANES
    positions = cache_keys.shape[0]
    features = out_weight.shape[1]
    core = index & 1
    my_xy = (index >> 1) & 3
    tall = d + STAT
    keys = cache_keys.reshape(positions * kv_count, d)
    values = cache_values.reshape(positions * kv_count, d)
    place = jnp.concatenate(
        [jnp.stack([core, my_xy]).astype(jnp.int32), block_mask[0], key_counts]
    )
    kept_in_hbm = functools.partial(pltpu.with_memory_space_constraint, memory_space=pltpu.HBM)
    state = jax.ShapeDtypeStruct((z_size, tall, LANES), bf16)

    partial = jax.ShapeDtypeStruct((pieces, tall, LANES), bf16)
    blocks = positions // BLK

    def split_and_attend():
        return pl.pallas_call(
            split_kernel,
            in_specs=[SMEM] + [HBM] * 3,
            out_specs=[VMEM] * 3,
            scratch_shapes=[
                pltpu.SMEM((blocks + 1,), jnp.int32),
                pltpu.SMEM((blocks + 1,), jnp.int32),
                pltpu.VMEM((token_count, group_size, d), bf16),
                pltpu.VMEM((positions * kv_count, d), bf16),
                pltpu.VMEM((positions * kv_count, d), bf16),
                pltpu.VMEM((BLK * kv_count, d), f32),
                pltpu.SemaphoreType.DMA((3,)),
            ],
            out_shape=[
                jax.ShapeDtypeStruct((kv_count, positions, d), bf16),
                jax.ShapeDtypeStruct((kv_count, tall, positions), bf16),
                partial,
            ],
            compiler_params=pltpu.CompilerParams(vmem_limit_bytes=32 << 20),
            cost_estimate=pl.CostEstimate(
                flops=4 * rows * positions * d,
                transcendentals=rows * positions,
                bytes_accessed=4 * positions * d * kv_count,
            ),
            name="split_and_attend",
        )(place, kept_in_hbm(keys), kept_in_hbm(values), kept_in_hbm(queries))

    def attend(chunk_roles, kd, vt):
        count = len(chunk_roles)
        return pl.pallas_call(
            functools.partial(attention_kernel, chunk_roles),
            in_specs=[SMEM] + [VMEM] * 3,
            out_specs=[VMEM] * count,
            out_shape=[partial] * count,
            compiler_params=pltpu.CompilerParams(vmem_limit_bytes=32 << 20),
            cost_estimate=pl.CostEstimate(
                flops=4 * count * rows * positions * d,
                transcendentals=count * rows * positions,
                bytes_accessed=4 * positions * d * count,
            ),
            name="attend",
        )(place, kd, vt, queries)

    def merge_cores(kept, received):
        return pl.pallas_call(
            core_kernel,
            in_specs=[SMEM] + [VMEM] * 2,
            out_specs=[VMEM] * 4,
            out_shape=[state] * 4,
            compiler_params=SMALL,
            name="merge_cores",
        )(place, kept, received)

    def merge_chips(parts):
        return pl.pallas_call(
            plane_kernel,
            in_specs=[VMEM] * len(parts),
            out_specs=VMEM,
            out_shape=state,
            compiler_params=SMALL,
            name="merge_chips",
        )(*parts)

    def finish(parts):
        tokens = LANES // group_size
        return pl.pallas_call(
            last_kernel,
            in_specs=[VMEM] * len(parts),
            out_specs=VMEM,
            out_shape=jax.ShapeDtypeStruct((z_size, tokens, group_size * d), bf16),
            scratch_shapes=[pltpu.VMEM((z_size, LANES, d), f32)],
            compiler_params=SMALL,
            name="finish",
        )(*parts)

    def project(terms, parts, earlier, last=False):
        depth = group_size * d
        more = [] if earlier is None else [earlier]
        return pl.pallas_call(
            functools.partial(project_kernel, terms, bool(more), last),
            in_specs=[SMEM] + [VMEM] * (1 + len(parts) + len(more)),
            out_specs=VMEM,
            out_shape=jax.ShapeDtypeStruct((token_count, features), f32),
            compiler_params=pltpu.CompilerParams(vmem_limit_bytes=8 << 20),
            cost_estimate=pl.CostEstimate(
                flops=2 * len(terms) * token_count * depth * features,
                transcendentals=0,
                bytes_accessed=2 * len(terms) * depth * features,
            ),
            name="project",
        )(place, out_weight, *parts, *more)

    def exchange_plane(kept, received):
        parts = merge_cores(kept, received)
        return [parts[0]] + [plane_hop(parts[j], j) for j in (1, 2, 3)]

    def exchange_line(parts):
        part = merge_chips(parts)
        reach = 1
        while 2 * reach < z_size:
            part = merge_chips([part, hop(part, 8 * reach)])
            reach *= 2
        return finish([part, hop(part, 8 * reach)])

    def gather_plane(attended):
        return [attended] + [plane_hop(attended, j) for j in (1, 2, 3)]

    kd, vt, sent = split_and_attend()
    received = hop(sent, 1)
    kept, sent = attend([(0, False), (1, True)], kd, vt)
    next_received = hop(sent, 1)
    parts = merge_cores(kept, received)
    parts, kd = lax.optimization_barrier((parts, kd))
    first = [parts[0]] + [plane_hop(parts[j], j) for j in (1, 2, 3)]
    (kept,) = attend([(1, False)], kd, vt)
    second = exchange_plane(kept, next_received)
    own = gather_plane(exchange_line(first))
    other = [hop(own[j], 1) for j in (0, 2, 1, 3)]
    next_own = gather_plane(exchange_line(second))
    total = project([(0, False), (0, True)], own + other, None)
    next_own[3], total = lax.optimization_barrier((next_own[3], total))
    next_other = [hop(next_own[j], 1) for j in (0, 2, 1, 3)]
    total = project([(1, False)], next_own, total)
    return project([(1, True)], next_other, total, last=True)


def partner_of(value, axis, distance):
    mask = 2**distance
    pairs = [(source, source ^ mask) for source in range(lax.axis_size(axis))]
    return lax.ppermute(value, axis, pairs)


def combine(earlier, later):
    out_one, top_one, sum_one = earlier
    out_two, top_two, sum_two = later
    new_top = jnp.maximum(top_one, top_two)
    factor_one = jnp.exp(top_one - new_top)
    factor_two = jnp.exp(top_two - new_top)
    new_out = out_one * factor_one[..., None] + out_two * factor_two[..., None]
    return (new_out, new_top, sum_one * factor_one + sum_two * factor_two)


def keep_state(key_block, run_state):
    return run_state


def partial_rows(rows_q, row_mask, cache_keys, cache_values, key_counts):
    row_count, head_count, head_size = rows_q.shape
    kv_count = cache_keys.shape[1]
    group_size = head_count // kv_count
    grouped = rows_q.reshape(row_count, kv_count, group_size, head_size)
    block_count = cache_keys.shape[0] // BLK
    score_scale = 1.0 / math.sqrt(head_size)
    offsets = jnp.arange(BLK, dtype=jnp.int32)

    def update(key_block, run_state):
        out_sum, top_score, weight_sum = run_state
        key_part = lax.dynamic_slice_in_dim(cache_keys, key_block * BLK, BLK, 0)
        value_part = lax.dynamic_slice_in_dim(cache_values, key_block * BLK, BLK, 0)
        scores = (
            jnp.einsum("rgqd,kgd->rgqk", grouped, key_part, preferred_element_type=jnp.float32)
            * score_scale
        )
        active_rows = lax.dynamic_slice_in_dim(row_mask, key_block, 1, 1)[:, 0] > 0
        valid_count = lax.dynamic_slice_in_dim(key_counts, key_block, 1, 0)[0]
        valid = active_rows[:, None, None, None] & (offsets < valid_count)[None, None, None, :]
        scores = jnp.where(valid, scores, very_low)
        new_top = jnp.maximum(top_score, jnp.max(scores, axis=-1))
        weights = jnp.where(valid, jnp.exp(scores - new_top[..., None]), 0.0)
        factor = jnp.exp(top_score - new_top)
        new_sum = weight_sum * factor + jnp.sum(weights, axis=-1)
        new_out = out_sum * factor[..., None] + jnp.einsum(
            "rgqk,kgd->rgqd",
            weights.astype(jnp.bfloat16),
            value_part,
            preferred_element_type=jnp.float32,
        )
        return (new_out, new_top, new_sum)

    def visit_block(key_block, run_state):
        active = jnp.any(lax.dynamic_slice_in_dim(row_mask, key_block, 1, 1) > 0)
        return lax.cond(active, update, keep_state, key_block, run_state)

    initial = (
        jnp.zeros((row_count, kv_count, group_size, head_size), jnp.float32),
        jnp.full((row_count, kv_count, group_size), very_low, jnp.float32),
        jnp.zeros((row_count, kv_count, group_size), jnp.float32),
    )
    return lax.fori_loop(0, block_count, visit_block, initial)


def general_body(queries, cache_keys, cache_values, block_mask, key_counts, out_weight):
    cycle_size = lax.axis_size("ctx")
    cycle_index = lax.axis_index("ctx")
    token_count, head_count, head_size = queries.shape
    segment = token_count // cycle_size
    query_blocks = queries.reshape(block_mask.shape[0], BLK, head_count, head_size)

    def per_block(block_item):
        rows_q, mask_row = block_item
        row_mask = jnp.broadcast_to(mask_row[None, :], (BLK, mask_row.shape[0]))
        return partial_rows(rows_q, row_mask, cache_keys, cache_values, key_counts)

    stacked = lax.map(per_block, (query_blocks, block_mask))
    run_state = tuple((part.reshape((token_count,) + part.shape[2:]) for part in stacked))
    bit_total = cycle_size.bit_length() - 1
    for bit_number in range(bit_total - 1, -1, -1):
        half_rows = run_state[1].shape[0] // 2
        upper_half = jnp.bitwise_and(jnp.right_shift(cycle_index, bit_number), 1)
        kept = tuple(
            (
                lax.dynamic_slice_in_dim(part, upper_half * half_rows, half_rows, 0)
                for part in run_state
            )
        )
        outgoing = tuple(
            (
                lax.dynamic_slice_in_dim(part, (1 - upper_half) * half_rows, half_rows, 0)
                for part in run_state
            )
        )
        received = partner_of((outgoing[0], outgoing[1], outgoing[2]), "ctx", bit_number)
        run_state = combine(kept, received)
    out_sum, top_score, weight_sum = run_state
    attended = (
        (out_sum / weight_sum[..., None])
        .astype(jnp.bfloat16)
        .reshape(segment, head_count * head_size)
    )
    partial_value = jnp.dot(
        lax.all_gather(attended, "ctx", axis=0, tiled=True),
        out_weight,
        preferred_element_type=jnp.float32,
    )
    return lax.psum_scatter(partial_value, "kv", scatter_dimension=0, tiled=True)


def body(queries, cache_keys, cache_values, block_mask, key_counts, out_weight):
    devices = lax.axis_size("ctx")
    token_count, head_count, d = queries.shape
    kv_count = cache_keys.shape[1]
    group_size = head_count // kv_count
    suits = (
        lax.axis_size("kv") == 1
        and devices == 32
        and token_count == BLK
        and block_mask.shape[0] == 1
        and kv_count == 4
        and d == LANES
        and group_size == 16
        and token_count * group_size == LANES * (devices // 2)
    )
    run = fast_body if suits else general_body
    return run(queries, cache_keys, cache_values, block_mask, key_counts, out_weight)


def solution(mesh):
    placed = (
        P("groups", "kv", None),
        P(("groups", "ctx"), "kv", None),
        P(("groups", "ctx"), "kv", None),
        P("groups", "ctx"),
        P(("groups", "ctx")),
        P("kv", "ctx"),
    )
    return jax.shard_map(
        body, mesh=mesh, in_specs=placed, out_specs=P(("groups", "kv"), "ctx"), check_vma=False
    )
```

```python
import functools
import math

import jax
import jax.numpy as jnp
from jax import lax
from jax.experimental import pallas as pl
from jax.experimental.pallas import tpu as pltpu
from jax.sharding import PartitionSpec as P

BLK = 128
LANES = 128
STAT = 8
very_low = -1e30
lowest_top = -(2.0**99)
bf16 = jnp.bfloat16
f32 = jnp.float32


def pack_state(out, top, total):
    high = total.astype(bf16).astype(f32)
    low = total - high
    row = lax.broadcasted_iota(jnp.int32, (STAT, LANES), 0)
    stats = jnp.where(row == 0, top, jnp.where(row == 1, high, jnp.where(row == 2, low, 0.0)))
    return out.astype(bf16), stats.astype(bf16)


def active_count(meta):
    block_count = (meta.shape[0] - 2) // 2
    return sum((meta[2 + block] > 0).astype(jnp.int32) for block in range(block_count))


def split_kernel(meta, k_hbm, v_hbm, q_hbm, kd, vt, sent_ref, *scratch):
    listed, kept_counts, q_ref, k_ref, v_ref, spread, sems = scratch
    d = k_hbm.shape[1]
    kv_count = kd.shape[0]
    group_size = q_ref.shape[1]
    block_count = (meta.shape[0] - 2) // 2
    group = 1 - meta[0]

    heads = pl.ds(pl.multiple_of(group * group_size, group_size), group_size)
    copies = [
        pltpu.make_async_copy(k_hbm, k_ref, sems.at[0]),
        pltpu.make_async_copy(v_hbm, v_ref, sems.at[1]),
        pltpu.make_async_copy(q_hbm.at[:, heads, :], q_ref, sems.at[2]),
    ]
    for copy in copies:
        copy.start()

    def note(block, found):
        listed[found] = block
        kept_counts[found] = meta[2 + block_count + block]
        return found + (meta[2 + block] > 0).astype(jnp.int32)

    active = lax.fori_loop(0, block_count, note, jnp.int32(0))
    place = lax.broadcasted_iota(jnp.int32, (BLK, LANES), 0)
    across = lax.broadcasted_iota(jnp.int32, (STAT, LANES), 1)

    def split(source, position):
        start = pl.multiple_of(listed[position] * (BLK * kv_count), BLK * kv_count)
        spread[...] = source[pl.ds(start, BLK * kv_count), :].astype(f32)
        return [spread[pl.ds(g, BLK, stride=kv_count), :] for g in range(kv_count)]

    def fetch_keys(position, carry):
        at = pl.ds(pl.multiple_of(position * BLK, BLK), BLK)
        valid = place < kept_counts[position]
        for g, key in enumerate(split(k_ref, position)):
            kd[g, at, :] = jnp.where(valid, key, key[0:1]).astype(bf16)
        return carry

    def fetch_values(position, carry):
        at = pl.ds(pl.multiple_of(position * BLK, BLK), BLK)
        count = kept_counts[position]
        for g, value in enumerate(split(v_ref, position)):
            vt[g, 0:d, at] = jnp.where(place < count, value, 0.0).T.astype(bf16)
            vt[g, d:, at] = (across < count).astype(f32).astype(bf16)
        return carry

    copies[0].wait()
    lax.fori_loop(0, active, fetch_keys, 0)
    copies[1].wait()
    lax.fori_loop(0, active, fetch_values, 0)

    @pl.when(active % 2 == 1)
    def _():
        at = pl.ds(pl.multiple_of(active * BLK, BLK), BLK)
        before = pl.ds(pl.multiple_of((active - 1) * BLK, BLK), BLK)
        for g in range(kv_count):
            kd[g, at, :] = kd[g, before, :]
            vt[g, :, at] = jnp.zeros((d + STAT, BLK), bf16)

    copies[2].wait()
    attend_all(active, [(sent_ref, group, lambda: q_ref[...])], kd, vt)


def attention_kernel(chunk_roles, meta, kd, vt, q_ref, *outs):
    group_size = q_ref.shape[1] // kd.shape[0]
    todo = []
    for out, (chunk, is_other) in zip(outs, chunk_roles):
        group = 2 * chunk + (1 - meta[0] if is_other else meta[0])

        def read(group=group):
            heads = pl.ds(pl.multiple_of(group * group_size, group_size), group_size)
            return q_ref[:, heads, :]

        todo.append((out, group, read))
    attend_all(active_count(meta), todo, kd, vt)


def attend_all(active, todo, kd, vt):
    d = kd.shape[2]
    scale2 = math.log2(math.e) / math.sqrt(d)
    rows = todo[0][0].shape[0] * LANES
    pairs = (active + 1) // 2

    def attend(width, out, group, read):
        q = read().reshape(rows, d)
        scores = lax.dot_general(
            kd[group, 0:width, :], q, (((1,), (1,)), ((), ())), preferred_element_type=f32
        )
        top = (jnp.max(scores, axis=0, keepdims=True) * scale2).astype(bf16).astype(f32)
        weights = jnp.exp2(scores * scale2 - top).astype(bf16)
        sums = jnp.dot(vt[group, :, 0:width], weights, preferred_element_type=f32)
        total = sums[d:]
        high = total.astype(bf16).astype(f32)
        row = lax.broadcasted_iota(jnp.int32, (STAT, rows), 0)
        stats = jnp.where(row == 0, top, jnp.where(row == 1, high, total - high)).astype(bf16)
        value = sums[:d].astype(bf16)
        for piece in range(rows // LANES):
            at = slice(piece * LANES, (piece + 1) * LANES)
            out[piece, 0:d] = value[:, at]
            out[piece, d:] = stats[:, at]

    for n in range(1, kd.shape[1] // (2 * BLK) + 1):

        @pl.when(pairs == n)
        def _(n=n):
            for out, group, read in todo:
                attend(2 * BLK * n, out, group, read)

    @pl.when(pairs == 0)
    def _():
        row = lax.broadcasted_iota(jnp.int32, (d + STAT, LANES), 0)
        empty = jnp.where(row == d, lowest_top, 0.0).astype(bf16)
        for out, _, _ in todo:
            for piece in range(rows // LANES):
                out[piece] = empty


def merged(parts, d):
    stats = [part[d : d + STAT, :].astype(f32) for part in parts]
    tops = [stat[0:1] for stat in stats]
    top = functools.reduce(jnp.maximum, tops)
    out, total = 0.0, 0.0
    for part, stat, one in zip(parts, stats, tops):
        factor = jnp.exp2(one - top)
        out = out + part[0:d, :].astype(f32) * factor
        total = total + (stat[1:2] + stat[2:3]) * factor
    return out, top, total


def store_merged(ref, z, parts):
    d = ref.shape[1] - STAT
    out, stats = pack_state(*merged(parts, d))
    ref[z, 0:d, :] = out
    ref[z, d : d + STAT, :] = stats


def plane_chips(meta):
    core, my_xy = meta[0], meta[1]
    return [my_xy, my_xy ^ (1 + core), my_xy ^ (2 - core), my_xy ^ 3]


def core_kernel(meta, kept, received, *outs):
    z_size = outs[0].shape[0]
    for chip, out in zip(plane_chips(meta), outs):
        for z in range(z_size):
            piece = chip * z_size + z
            store_merged(out, z, [kept[piece], received[piece]])


def plane_kernel(*refs):
    ins, out = refs[:-1], refs[-1]
    for z in range(out.shape[0]):
        store_merged(out, z, [ref[z] for ref in ins])


def last_kernel(*refs):
    ins, out_ref, turned = refs[:-2], refs[-2], refs[-1]
    d = ins[0].shape[1] - STAT
    tokens = out_ref.shape[1]
    heads = LANES // tokens
    for z in range(out_ref.shape[0]):
        out, _, total = merged([ref[z] for ref in ins], d)
        turned[z] = (out / total).T
        for h in range(heads):
            picked = turned[z, pl.ds(h, tokens, stride=heads), :]
            out_ref[z, :, h * d : (h + 1) * d] = picked.astype(bf16)


def project_kernel(terms, has_earlier, last, meta, weight, *refs):
    z_size, tokens, depth = refs[0].shape
    total = refs[4 * len(terms)][...] if has_earlier else None
    out_ref = refs[-1]
    for i, (chunk, is_other) in enumerate(terms):
        left = jnp.concatenate(
            [part[...].reshape(z_size * tokens, depth) for part in refs[4 * i : 4 * i + 4]], axis=0
        )
        group = 2 * chunk + (1 - meta[0] if is_other else meta[0])
        at = pl.ds(pl.multiple_of(group * depth, depth), depth)
        product = jnp.dot(left, weight[at, :], preferred_element_type=f32)
        total = product if total is None else total + product
    if not last:
        out_ref[...] = total
        return
    size = z_size * tokens
    for j, chip in enumerate(plane_chips(meta)):
        to = pl.ds(pl.multiple_of(chip * size, size), size)
        out_ref[to, :] = total[j * size : (j + 1) * size]


def hop(value, mask):
    pairs = [(source, source ^ mask) for source in range(lax.axis_size("ctx"))]
    return lax.ppermute(value, "ctx", pairs)


def plane_hop(value, number):
    masks = {1: (2, 4), 2: (4, 2), 3: (6, 6)}[number]
    pairs = [(source, source ^ masks[source % 2]) for source in range(lax.axis_size("ctx"))]
    return lax.ppermute(value, "ctx", pairs)


def line_hop(value, reach, z_size):
    masks = (8 * reach, 4 * z_size // reach)
    pairs = [(source, source ^ masks[source % 2]) for source in range(lax.axis_size("ctx"))]
    return lax.ppermute(value, "ctx", pairs)


VMEM = pl.BlockSpec(memory_space=pltpu.VMEM)
SMEM = pl.BlockSpec(memory_space=pltpu.SMEM)
HBM = pl.BlockSpec(memory_space=pltpu.HBM)
SMALL = pltpu.CompilerParams(vmem_limit_bytes=4 << 20)


def fast_body(queries, cache_keys, cache_values, block_mask, key_counts, out_weight):
    index = lax.axis_index("ctx")
    z_size = lax.axis_size("ctx") // 8
    token_count, head_count, d = queries.shape
    kv_count = cache_keys.shape[1]
    group_size = head_count // kv_count
    rows = token_count * group_size
    pieces = rows // LANES
    positions = cache_keys.shape[0]
    features = out_weight.shape[1]
    core = index & 1
    my_xy = (index >> 1) & 3
    tall = d + STAT
    keys = cache_keys.reshape(positions * kv_count, d)
    values = cache_values.reshape(positions * kv_count, d)
    place = jnp.concatenate(
        [jnp.stack([core, my_xy]).astype(jnp.int32), block_mask[0], key_counts]
    )
    kept_in_hbm = functools.partial(pltpu.with_memory_space_constraint, memory_space=pltpu.HBM)
    state = jax.ShapeDtypeStruct((z_size, tall, LANES), bf16)

    partial = jax.ShapeDtypeStruct((pieces, tall, LANES), bf16)
    blocks = positions // BLK

    def split_and_attend():
        return pl.pallas_call(
            split_kernel,
            in_specs=[SMEM] + [HBM] * 3,
            out_specs=[VMEM] * 3,
            scratch_shapes=[
                pltpu.SMEM((blocks + 1,), jnp.int32),
                pltpu.SMEM((blocks + 1,), jnp.int32),
                pltpu.VMEM((token_count, group_size, d), bf16),
                pltpu.VMEM((positions * kv_count, d), bf16),
                pltpu.VMEM((positions * kv_count, d), bf16),
                pltpu.VMEM((BLK * kv_count, d), f32),
                pltpu.SemaphoreType.DMA((3,)),
            ],
            out_shape=[
                jax.ShapeDtypeStruct((kv_count, positions, d), bf16),
                jax.ShapeDtypeStruct((kv_count, tall, positions), bf16),
                partial,
            ],
            compiler_params=pltpu.CompilerParams(vmem_limit_bytes=32 << 20),
            cost_estimate=pl.CostEstimate(
                flops=4 * rows * positions * d,
                transcendentals=rows * positions,
                bytes_accessed=4 * positions * d * kv_count,
            ),
            name="split_and_attend",
        )(place, kept_in_hbm(keys), kept_in_hbm(values), kept_in_hbm(queries))

    def attend(chunk_roles, kd, vt):
        count = len(chunk_roles)
        return pl.pallas_call(
            functools.partial(attention_kernel, chunk_roles),
            in_specs=[SMEM] + [VMEM] * 3,
            out_specs=[VMEM] * count,
            out_shape=[partial] * count,
            compiler_params=pltpu.CompilerParams(vmem_limit_bytes=32 << 20),
            cost_estimate=pl.CostEstimate(
                flops=4 * count * rows * positions * d,
                transcendentals=count * rows * positions,
                bytes_accessed=4 * positions * d * count,
            ),
            name="attend",
        )(place, kd, vt, queries)

    def merge_cores(kept, received):
        return pl.pallas_call(
            core_kernel,
            in_specs=[SMEM] + [VMEM] * 2,
            out_specs=[VMEM] * 4,
            out_shape=[state] * 4,
            compiler_params=SMALL,
            name="merge_cores",
        )(place, kept, received)

    def merge_chips(parts):
        return pl.pallas_call(
            plane_kernel,
            in_specs=[VMEM] * len(parts),
            out_specs=VMEM,
            out_shape=state,
            compiler_params=SMALL,
            name="merge_chips",
        )(*parts)

    def finish(parts):
        tokens = LANES // group_size
        return pl.pallas_call(
            last_kernel,
            in_specs=[VMEM] * len(parts),
            out_specs=VMEM,
            out_shape=jax.ShapeDtypeStruct((z_size, tokens, group_size * d), bf16),
            scratch_shapes=[pltpu.VMEM((z_size, LANES, d), f32)],
            compiler_params=SMALL,
            name="finish",
        )(*parts)

    def project(terms, parts, earlier, last=False):
        depth = group_size * d
        more = [] if earlier is None else [earlier]
        return pl.pallas_call(
            functools.partial(project_kernel, terms, bool(more), last),
            in_specs=[SMEM] + [VMEM] * (1 + len(parts) + len(more)),
            out_specs=VMEM,
            out_shape=jax.ShapeDtypeStruct((token_count, features), f32),
            compiler_params=pltpu.CompilerParams(vmem_limit_bytes=8 << 20),
            cost_estimate=pl.CostEstimate(
                flops=2 * len(terms) * token_count * depth * features,
                transcendentals=0,
                bytes_accessed=2 * len(terms) * depth * features,
            ),
            name="project",
        )(place, out_weight, *parts, *more)

    def exchange_plane(kept, received):
        parts = merge_cores(kept, received)
        return [parts[0]] + [plane_hop(parts[j], j) for j in (1, 2, 3)]

    def exchange_line(parts):
        part = merge_chips(parts)
        reach = 1
        while 2 * reach < z_size:
            part = merge_chips([part, line_hop(part, reach, z_size)])
            reach *= 2
        return finish([part, line_hop(part, reach, z_size)])

    def gather_plane(attended):
        return [attended] + [plane_hop(attended, j) for j in (1, 2, 3)]

    kd, vt, sent = split_and_attend()
    received = hop(sent, 1)
    kept, sent = attend([(0, False), (1, True)], kd, vt)
    next_received = hop(sent, 1)
    parts = merge_cores(kept, received)
    parts, kd = lax.optimization_barrier((parts, kd))
    first = [parts[0]] + [plane_hop(parts[j], j) for j in (1, 2, 3)]
    (kept,) = attend([(1, False)], kd, vt)
    second = exchange_plane(kept, next_received)
    own = gather_plane(exchange_line(first))
    other = [hop(own[j], 1) for j in (0, 2, 1, 3)]
    next_own = gather_plane(exchange_line(second))
    total = project([(0, False), (0, True)], own + other, None)
    next_own[3], total = lax.optimization_barrier((next_own[3], total))
    next_other = [hop(next_own[j], 1) for j in (0, 2, 1, 3)]
    total = project([(1, False)], next_own, total)
    return project([(1, True)], next_other, total, last=True)


def partner_of(value, axis, distance):
    mask = 2**distance
    pairs = [(source, source ^ mask) for source in range(lax.axis_size(axis))]
    return lax.ppermute(value, axis, pairs)


def combine(earlier, later):
    out_one, top_one, sum_one = earlier
    out_two, top_two, sum_two = later
    new_top = jnp.maximum(top_one, top_two)
    factor_one = jnp.exp(top_one - new_top)
    factor_two = jnp.exp(top_two - new_top)
    new_out = out_one * factor_one[..., None] + out_two * factor_two[..., None]
    return (new_out, new_top, sum_one * factor_one + sum_two * factor_two)


def keep_state(key_block, run_state):
    return run_state


def partial_rows(rows_q, row_mask, cache_keys, cache_values, key_counts):
    row_count, head_count, head_size = rows_q.shape
    kv_count = cache_keys.shape[1]
    group_size = head_count // kv_count
    grouped = rows_q.reshape(row_count, kv_count, group_size, head_size)
    block_count = cache_keys.shape[0] // BLK
    score_scale = 1.0 / math.sqrt(head_size)
    offsets = jnp.arange(BLK, dtype=jnp.int32)

    def update(key_block, run_state):
        out_sum, top_score, weight_sum = run_state
        key_part = lax.dynamic_slice_in_dim(cache_keys, key_block * BLK, BLK, 0)
        value_part = lax.dynamic_slice_in_dim(cache_values, key_block * BLK, BLK, 0)
        scores = (
            jnp.einsum("rgqd,kgd->rgqk", grouped, key_part, preferred_element_type=jnp.float32)
            * score_scale
        )
        active_rows = lax.dynamic_slice_in_dim(row_mask, key_block, 1, 1)[:, 0] > 0
        valid_count = lax.dynamic_slice_in_dim(key_counts, key_block, 1, 0)[0]
        valid = active_rows[:, None, None, None] & (offsets < valid_count)[None, None, None, :]
        scores = jnp.where(valid, scores, very_low)
        new_top = jnp.maximum(top_score, jnp.max(scores, axis=-1))
        weights = jnp.where(valid, jnp.exp(scores - new_top[..., None]), 0.0)
        factor = jnp.exp(top_score - new_top)
        new_sum = weight_sum * factor + jnp.sum(weights, axis=-1)
        new_out = out_sum * factor[..., None] + jnp.einsum(
            "rgqk,kgd->rgqd",
            weights.astype(jnp.bfloat16),
            value_part,
            preferred_element_type=jnp.float32,
        )
        return (new_out, new_top, new_sum)

    def visit_block(key_block, run_state):
        active = jnp.any(lax.dynamic_slice_in_dim(row_mask, key_block, 1, 1) > 0)
        return lax.cond(active, update, keep_state, key_block, run_state)

    initial = (
        jnp.zeros((row_count, kv_count, group_size, head_size), jnp.float32),
        jnp.full((row_count, kv_count, group_size), very_low, jnp.float32),
        jnp.zeros((row_count, kv_count, group_size), jnp.float32),
    )
    return lax.fori_loop(0, block_count, visit_block, initial)


def general_body(queries, cache_keys, cache_values, block_mask, key_counts, out_weight):
    cycle_size = lax.axis_size("ctx")
    cycle_index = lax.axis_index("ctx")
    token_count, head_count, head_size = queries.shape
    segment = token_count // cycle_size
    query_blocks = queries.reshape(block_mask.shape[0], BLK, head_count, head_size)

    def per_block(block_item):
        rows_q, mask_row = block_item
        row_mask = jnp.broadcast_to(mask_row[None, :], (BLK, mask_row.shape[0]))
        return partial_rows(rows_q, row_mask, cache_keys, cache_values, key_counts)

    stacked = lax.map(per_block, (query_blocks, block_mask))
    run_state = tuple((part.reshape((token_count,) + part.shape[2:]) for part in stacked))
    bit_total = cycle_size.bit_length() - 1
    for bit_number in range(bit_total - 1, -1, -1):
        half_rows = run_state[1].shape[0] // 2
        upper_half = jnp.bitwise_and(jnp.right_shift(cycle_index, bit_number), 1)
        kept = tuple(
            (
                lax.dynamic_slice_in_dim(part, upper_half * half_rows, half_rows, 0)
                for part in run_state
            )
        )
        outgoing = tuple(
            (
                lax.dynamic_slice_in_dim(part, (1 - upper_half) * half_rows, half_rows, 0)
                for part in run_state
            )
        )
        received = partner_of((outgoing[0], outgoing[1], outgoing[2]), "ctx", bit_number)
        run_state = combine(kept, received)
    out_sum, top_score, weight_sum = run_state
    attended = (
        (out_sum / weight_sum[..., None])
        .astype(jnp.bfloat16)
        .reshape(segment, head_count * head_size)
    )
    partial_value = jnp.dot(
        lax.all_gather(attended, "ctx", axis=0, tiled=True),
        out_weight,
        preferred_element_type=jnp.float32,
    )
    return lax.psum_scatter(partial_value, "kv", scatter_dimension=0, tiled=True)


def body(queries, cache_keys, cache_values, block_mask, key_counts, out_weight):
    devices = lax.axis_size("ctx")
    token_count, head_count, d = queries.shape
    kv_count = cache_keys.shape[1]
    group_size = head_count // kv_count
    suits = (
        lax.axis_size("kv") == 1
        and devices == 32
        and token_count == BLK
        and block_mask.shape[0] == 1
        and kv_count == 4
        and d == LANES
        and group_size == 16
        and token_count * group_size == LANES * (devices // 2)
    )
    run = fast_body if suits else general_body
    return run(queries, cache_keys, cache_values, block_mask, key_counts, out_weight)


def solution(mesh):
    placed = (
        P("groups", "kv", None),
        P(("groups", "ctx"), "kv", None),
        P(("groups", "ctx"), "kv", None),
        P("groups", "ctx"),
        P(("groups", "ctx")),
        P("kv", "ctx"),
    )
    return jax.shard_map(
        body, mesh=mesh, in_specs=placed, out_specs=P(("groups", "kv"), "ctx"), check_vma=False
    )
```

```python
import functools
import math

import jax
import jax.numpy as jnp
from jax import lax
from jax.experimental import pallas as pl
from jax.experimental.pallas import tpu as pltpu
from jax.sharding import PartitionSpec as P

BLK = 128
LANES = 128
STAT = 8
very_low = -1e30
lowest_top = -(2.0**99)
bf16 = jnp.bfloat16
f32 = jnp.float32


def pack_state(out, top, total):
    high = total.astype(bf16).astype(f32)
    low = total - high
    row = lax.broadcasted_iota(jnp.int32, (STAT, LANES), 0)
    stats = jnp.where(row == 0, top, jnp.where(row == 1, high, jnp.where(row == 2, low, 0.0)))
    return out.astype(bf16), stats.astype(bf16)


def active_count(meta):
    block_count = (meta.shape[0] - 2) // 2
    return sum((meta[2 + block] > 0).astype(jnp.int32) for block in range(block_count))


def split_kernel(meta, k_hbm, v_hbm, q_hbm, kd, vt, sent_ref, *scratch):
    listed, kept_counts, q_ref, k_ref, v_ref, spread, sems = scratch
    d = k_hbm.shape[1]
    kv_count = kd.shape[0]
    group_size = q_ref.shape[1]
    block_count = (meta.shape[0] - 2) // 2
    group = 1 - meta[0]

    heads = pl.ds(pl.multiple_of(group * group_size, group_size), group_size)
    copies = [
        pltpu.make_async_copy(k_hbm, k_ref, sems.at[0]),
        pltpu.make_async_copy(v_hbm, v_ref, sems.at[1]),
        pltpu.make_async_copy(q_hbm.at[:, heads, :], q_ref, sems.at[2]),
    ]
    for copy in copies:
        copy.start()

    def note(block, found):
        listed[found] = block
        kept_counts[found] = meta[2 + block_count + block]
        return found + (meta[2 + block] > 0).astype(jnp.int32)

    active = lax.fori_loop(0, block_count, note, jnp.int32(0))
    place = lax.broadcasted_iota(jnp.int32, (BLK, LANES), 0)
    across = lax.broadcasted_iota(jnp.int32, (STAT, LANES), 1)

    def split(source, position):
        start = pl.multiple_of(listed[position] * (BLK * kv_count), BLK * kv_count)
        spread[...] = source[pl.ds(start, BLK * kv_count), :].astype(f32)
        return [spread[pl.ds(g, BLK, stride=kv_count), :] for g in range(kv_count)]

    def fetch_keys(position, carry):
        at = pl.ds(pl.multiple_of(position * BLK, BLK), BLK)
        valid = place < kept_counts[position]
        for g, key in enumerate(split(k_ref, position)):
            kd[g, at, :] = jnp.where(valid, key, key[0:1]).astype(bf16)
        return carry

    def fetch_values(position, carry):
        at = pl.ds(pl.multiple_of(position * BLK, BLK), BLK)
        count = kept_counts[position]
        for g, value in enumerate(split(v_ref, position)):
            vt[g, 0:d, at] = jnp.where(place < count, value, 0.0).T.astype(bf16)
            vt[g, d:, at] = (across < count).astype(f32).astype(bf16)
        return carry

    copies[0].wait()
    lax.fori_loop(0, active, fetch_keys, 0)
    copies[1].wait()
    lax.fori_loop(0, active, fetch_values, 0)

    @pl.when(active % 2 == 1)
    def _():
        at = pl.ds(pl.multiple_of(active * BLK, BLK), BLK)
        before = pl.ds(pl.multiple_of((active - 1) * BLK, BLK), BLK)
        for g in range(kv_count):
            kd[g, at, :] = kd[g, before, :]
            vt[g, :, at] = jnp.zeros((d + STAT, BLK), bf16)

    copies[2].wait()
    attend_all(active, [(sent_ref, group, lambda: q_ref[...])], kd, vt)


def attention_kernel(chunk_roles, meta, kd, vt, q_ref, *outs):
    group_size = q_ref.shape[1] // kd.shape[0]
    todo = []
    for out, (chunk, is_other) in zip(outs, chunk_roles):
        group = 2 * chunk + (1 - meta[0] if is_other else meta[0])

        def read(group=group):
            heads = pl.ds(pl.multiple_of(group * group_size, group_size), group_size)
            return q_ref[:, heads, :]

        todo.append((out, group, read))
    attend_all(active_count(meta), todo, kd, vt)


def attend_all(active, todo, kd, vt):
    d = kd.shape[2]
    scale2 = math.log2(math.e) / math.sqrt(d)
    rows = todo[0][0].shape[0] * LANES
    pairs = (active + 1) // 2

    def attend(width, out, group, read):
        q = read().reshape(rows, d)
        scores = lax.dot_general(
            kd[group, 0:width, :], q, (((1,), (1,)), ((), ())), preferred_element_type=f32
        )
        top = (jnp.max(scores, axis=0, keepdims=True) * scale2).astype(bf16).astype(f32)
        weights = jnp.exp2(scores * scale2 - top).astype(bf16)
        sums = jnp.dot(vt[group, :, 0:width], weights, preferred_element_type=f32)
        total = sums[d:]
        high = total.astype(bf16).astype(f32)
        row = lax.broadcasted_iota(jnp.int32, (STAT, rows), 0)
        stats = jnp.where(row == 0, top, jnp.where(row == 1, high, total - high)).astype(bf16)
        value = sums[:d].astype(bf16)
        for piece in range(rows // LANES):
            at = slice(piece * LANES, (piece + 1) * LANES)
            out[piece, 0:d] = value[:, at]
            out[piece, d:] = stats[:, at]

    for n in range(1, kd.shape[1] // (2 * BLK) + 1):

        @pl.when(pairs == n)
        def _(n=n):
            for out, group, read in todo:
                attend(2 * BLK * n, out, group, read)

    @pl.when(pairs == 0)
    def _():
        row = lax.broadcasted_iota(jnp.int32, (d + STAT, LANES), 0)
        empty = jnp.where(row == d, lowest_top, 0.0).astype(bf16)
        for out, _, _ in todo:
            for piece in range(rows // LANES):
                out[piece] = empty


def merged(parts, d):
    stats = [part[d : d + STAT, :].astype(f32) for part in parts]
    tops = [stat[0:1] for stat in stats]
    top = functools.reduce(jnp.maximum, tops)
    out, total = 0.0, 0.0
    for part, stat, one in zip(parts, stats, tops):
        factor = jnp.exp2(one - top)
        out = out + part[0:d, :].astype(f32) * factor
        total = total + (stat[1:2] + stat[2:3]) * factor
    return out, top, total


def store_merged(ref, z, parts):
    d = ref.shape[1] - STAT
    out, stats = pack_state(*merged(parts, d))
    ref[z, 0:d, :] = out
    ref[z, d : d + STAT, :] = stats


def plane_chips(meta):
    core, my_xy = meta[0], meta[1]
    return [my_xy, my_xy ^ (1 + core), my_xy ^ (2 - core), my_xy ^ 3]


def core_kernel(meta, kept, received, *outs):
    z_size = outs[0].shape[0]
    for chip, out in zip(plane_chips(meta), outs):
        for z in range(z_size):
            piece = chip * z_size + z
            store_merged(out, z, [kept[piece], received[piece]])


def plane_kernel(*refs):
    ins, out = refs[:-1], refs[-1]
    for z in range(out.shape[0]):
        store_merged(out, z, [ref[z] for ref in ins])


def last_kernel(*refs):
    ins, out_ref, turned = refs[:-2], refs[-2], refs[-1]
    d = ins[0].shape[1] - STAT
    tokens = out_ref.shape[1]
    heads = LANES // tokens
    for z in range(out_ref.shape[0]):
        out, _, total = merged([ref[z] for ref in ins], d)
        turned[z] = (out / total).T
        for h in range(heads):
            picked = turned[z, pl.ds(h, tokens, stride=heads), :]
            out_ref[z, :, h * d : (h + 1) * d] = picked.astype(bf16)


def project_kernel(terms, has_earlier, last, meta, weight, *refs):
    z_size, tokens, depth = refs[0].shape
    total = refs[4 * len(terms)][...] if has_earlier else None
    out_ref = refs[-1]
    for i, (chunk, is_other) in enumerate(terms):
        left = jnp.concatenate(
            [part[...].reshape(z_size * tokens, depth) for part in refs[4 * i : 4 * i + 4]], axis=0
        )
        group = 2 * chunk + (1 - meta[0] if is_other else meta[0])
        at = pl.ds(pl.multiple_of(group * depth, depth), depth)
        product = jnp.dot(left, weight[at, :], preferred_element_type=f32)
        total = product if total is None else total + product
    if not last:
        out_ref[...] = total
        return
    size = z_size * tokens
    for j, chip in enumerate(plane_chips(meta)):
        to = pl.ds(pl.multiple_of(chip * size, size), size)
        out_ref[to, :] = total[j * size : (j + 1) * size]


def hop(value, mask):
    pairs = [(source, source ^ mask) for source in range(lax.axis_size("ctx"))]
    return lax.ppermute(value, "ctx", pairs)


def plane_hop(value, number):
    masks = {1: (2, 4), 2: (4, 2), 3: (6, 6)}[number]
    pairs = [(source, source ^ masks[source % 2]) for source in range(lax.axis_size("ctx"))]
    return lax.ppermute(value, "ctx", pairs)


def line_hop(value, reach, z_size):
    masks = (8 * reach, 4 * z_size // reach)
    pairs = [(source, source ^ masks[source % 2]) for source in range(lax.axis_size("ctx"))]
    return lax.ppermute(value, "ctx", pairs)


VMEM = pl.BlockSpec(memory_space=pltpu.VMEM)
SMEM = pl.BlockSpec(memory_space=pltpu.SMEM)
HBM = pl.BlockSpec(memory_space=pltpu.HBM)
SMALL = pltpu.CompilerParams(vmem_limit_bytes=4 << 20)


def fast_body(queries, cache_keys, cache_values, block_mask, key_counts, out_weight):
    index = lax.axis_index("ctx")
    z_size = lax.axis_size("ctx") // 8
    token_count, head_count, d = queries.shape
    kv_count = cache_keys.shape[1]
    group_size = head_count // kv_count
    rows = token_count * group_size
    pieces = rows // LANES
    positions = cache_keys.shape[0]
    features = out_weight.shape[1]
    core = index & 1
    my_xy = (index >> 1) & 3
    tall = d + STAT
    keys = cache_keys.reshape(positions * kv_count, d)
    values = cache_values.reshape(positions * kv_count, d)
    place = jnp.concatenate(
        [jnp.stack([core, my_xy]).astype(jnp.int32), block_mask[0], key_counts]
    )
    kept_in_hbm = functools.partial(pltpu.with_memory_space_constraint, memory_space=pltpu.HBM)
    state = jax.ShapeDtypeStruct((z_size, tall, LANES), bf16)

    partial = jax.ShapeDtypeStruct((pieces, tall, LANES), bf16)
    blocks = positions // BLK

    def split_and_attend():
        return pl.pallas_call(
            split_kernel,
            in_specs=[SMEM] + [HBM] * 3,
            out_specs=[VMEM] * 3,
            scratch_shapes=[
                pltpu.SMEM((blocks + 1,), jnp.int32),
                pltpu.SMEM((blocks + 1,), jnp.int32),
                pltpu.VMEM((token_count, group_size, d), bf16),
                pltpu.VMEM((positions * kv_count, d), bf16),
                pltpu.VMEM((positions * kv_count, d), bf16),
                pltpu.VMEM((BLK * kv_count, d), f32),
                pltpu.SemaphoreType.DMA((3,)),
            ],
            out_shape=[
                jax.ShapeDtypeStruct((kv_count, positions, d), bf16),
                jax.ShapeDtypeStruct((kv_count, tall, positions), bf16),
                partial,
            ],
            compiler_params=pltpu.CompilerParams(vmem_limit_bytes=32 << 20),
            cost_estimate=pl.CostEstimate(
                flops=4 * rows * positions * d,
                transcendentals=rows * positions,
                bytes_accessed=4 * positions * d * kv_count,
            ),
            name="split_and_attend",
        )(place, kept_in_hbm(keys), kept_in_hbm(values), kept_in_hbm(queries))

    def attend(chunk_roles, kd, vt):
        count = len(chunk_roles)
        return pl.pallas_call(
            functools.partial(attention_kernel, chunk_roles),
            in_specs=[SMEM] + [VMEM] * 3,
            out_specs=[VMEM] * count,
            out_shape=[partial] * count,
            compiler_params=pltpu.CompilerParams(vmem_limit_bytes=32 << 20),
            cost_estimate=pl.CostEstimate(
                flops=4 * count * rows * positions * d,
                transcendentals=count * rows * positions,
                bytes_accessed=4 * positions * d * count,
            ),
            name="attend",
        )(place, kd, vt, queries)

    def merge_cores(kept, received):
        return pl.pallas_call(
            core_kernel,
            in_specs=[SMEM] + [VMEM] * 2,
            out_specs=[VMEM] * 4,
            out_shape=[state] * 4,
            compiler_params=SMALL,
            name="merge_cores",
        )(place, kept, received)

    def merge_chips(parts):
        return pl.pallas_call(
            plane_kernel,
            in_specs=[VMEM] * len(parts),
            out_specs=VMEM,
            out_shape=state,
            compiler_params=SMALL,
            name="merge_chips",
        )(*parts)

    def finish(parts):
        tokens = LANES // group_size
        return pl.pallas_call(
            last_kernel,
            in_specs=[VMEM] * len(parts),
            out_specs=VMEM,
            out_shape=jax.ShapeDtypeStruct((z_size, tokens, group_size * d), bf16),
            scratch_shapes=[pltpu.VMEM((z_size, LANES, d), f32)],
            compiler_params=SMALL,
            name="finish",
        )(*parts)

    def project(terms, parts, earlier, last=False):
        depth = group_size * d
        more = [] if earlier is None else [earlier]
        return pl.pallas_call(
            functools.partial(project_kernel, terms, bool(more), last),
            in_specs=[SMEM] + [VMEM] * (1 + len(parts) + len(more)),
            out_specs=VMEM,
            out_shape=jax.ShapeDtypeStruct((token_count, features), f32),
            compiler_params=pltpu.CompilerParams(vmem_limit_bytes=8 << 20),
            cost_estimate=pl.CostEstimate(
                flops=2 * len(terms) * token_count * depth * features,
                transcendentals=0,
                bytes_accessed=2 * len(terms) * depth * features,
            ),
            name="project",
        )(place, out_weight, *parts, *more)

    def exchange_plane(kept, received):
        parts = merge_cores(kept, received)
        return [parts[0]] + [plane_hop(parts[j], j) for j in (1, 2, 3)]

    def exchange_line(parts):
        part = merge_chips(parts)
        reach = 1
        while 2 * reach < z_size:
            part = merge_chips([part, line_hop(part, reach, z_size)])
            reach *= 2
        return finish([part, line_hop(part, reach, z_size)])

    def gather_plane(attended):
        first, second = plane_hop(attended, 1), plane_hop(attended, 2)
        return [attended, first, second, plane_hop(first, 2)]

    kd, vt, sent = split_and_attend()
    received = hop(sent, 1)
    kept, sent = attend([(0, False), (1, True)], kd, vt)
    next_received = hop(sent, 1)
    parts = merge_cores(kept, received)
    parts, kd = lax.optimization_barrier((parts, kd))
    first = [parts[0]] + [plane_hop(parts[j], j) for j in (1, 2, 3)]
    (kept,) = attend([(1, False)], kd, vt)
    second = exchange_plane(kept, next_received)
    own = gather_plane(exchange_line(first))
    other = [hop(own[j], 1) for j in (0, 2, 1, 3)]
    next_own = gather_plane(exchange_line(second))
    total = project([(0, False), (0, True)], own + other, None)
    next_own[3], total = lax.optimization_barrier((next_own[3], total))
    next_other = [hop(next_own[j], 1) for j in (0, 2, 1, 3)]
    total = project([(1, False)], next_own, total)
    return project([(1, True)], next_other, total, last=True)


def partner_of(value, axis, distance):
    mask = 2**distance
    pairs = [(source, source ^ mask) for source in range(lax.axis_size(axis))]
    return lax.ppermute(value, axis, pairs)


def combine(earlier, later):
    out_one, top_one, sum_one = earlier
    out_two, top_two, sum_two = later
    new_top = jnp.maximum(top_one, top_two)
    factor_one = jnp.exp(top_one - new_top)
    factor_two = jnp.exp(top_two - new_top)
    new_out = out_one * factor_one[..., None] + out_two * factor_two[..., None]
    return (new_out, new_top, sum_one * factor_one + sum_two * factor_two)


def keep_state(key_block, run_state):
    return run_state


def partial_rows(rows_q, row_mask, cache_keys, cache_values, key_counts):
    row_count, head_count, head_size = rows_q.shape
    kv_count = cache_keys.shape[1]
    group_size = head_count // kv_count
    grouped = rows_q.reshape(row_count, kv_count, group_size, head_size)
    block_count = cache_keys.shape[0] // BLK
    score_scale = 1.0 / math.sqrt(head_size)
    offsets = jnp.arange(BLK, dtype=jnp.int32)

    def update(key_block, run_state):
        out_sum, top_score, weight_sum = run_state
        key_part = lax.dynamic_slice_in_dim(cache_keys, key_block * BLK, BLK, 0)
        value_part = lax.dynamic_slice_in_dim(cache_values, key_block * BLK, BLK, 0)
        scores = (
            jnp.einsum("rgqd,kgd->rgqk", grouped, key_part, preferred_element_type=jnp.float32)
            * score_scale
        )
        active_rows = lax.dynamic_slice_in_dim(row_mask, key_block, 1, 1)[:, 0] > 0
        valid_count = lax.dynamic_slice_in_dim(key_counts, key_block, 1, 0)[0]
        valid = active_rows[:, None, None, None] & (offsets < valid_count)[None, None, None, :]
        scores = jnp.where(valid, scores, very_low)
        new_top = jnp.maximum(top_score, jnp.max(scores, axis=-1))
        weights = jnp.where(valid, jnp.exp(scores - new_top[..., None]), 0.0)
        factor = jnp.exp(top_score - new_top)
        new_sum = weight_sum * factor + jnp.sum(weights, axis=-1)
        new_out = out_sum * factor[..., None] + jnp.einsum(
            "rgqk,kgd->rgqd",
            weights.astype(jnp.bfloat16),
            value_part,
            preferred_element_type=jnp.float32,
        )
        return (new_out, new_top, new_sum)

    def visit_block(key_block, run_state):
        active = jnp.any(lax.dynamic_slice_in_dim(row_mask, key_block, 1, 1) > 0)
        return lax.cond(active, update, keep_state, key_block, run_state)

    initial = (
        jnp.zeros((row_count, kv_count, group_size, head_size), jnp.float32),
        jnp.full((row_count, kv_count, group_size), very_low, jnp.float32),
        jnp.zeros((row_count, kv_count, group_size), jnp.float32),
    )
    return lax.fori_loop(0, block_count, visit_block, initial)


def general_body(queries, cache_keys, cache_values, block_mask, key_counts, out_weight):
    cycle_size = lax.axis_size("ctx")
    cycle_index = lax.axis_index("ctx")
    token_count, head_count, head_size = queries.shape
    segment = token_count // cycle_size
    query_blocks = queries.reshape(block_mask.shape[0], BLK, head_count, head_size)

    def per_block(block_item):
        rows_q, mask_row = block_item
        row_mask = jnp.broadcast_to(mask_row[None, :], (BLK, mask_row.shape[0]))
        return partial_rows(rows_q, row_mask, cache_keys, cache_values, key_counts)

    stacked = lax.map(per_block, (query_blocks, block_mask))
    run_state = tuple((part.reshape((token_count,) + part.shape[2:]) for part in stacked))
    bit_total = cycle_size.bit_length() - 1
    for bit_number in range(bit_total - 1, -1, -1):
        half_rows = run_state[1].shape[0] // 2
        upper_half = jnp.bitwise_and(jnp.right_shift(cycle_index, bit_number), 1)
        kept = tuple(
            (
                lax.dynamic_slice_in_dim(part, upper_half * half_rows, half_rows, 0)
                for part in run_state
            )
        )
        outgoing = tuple(
            (
                lax.dynamic_slice_in_dim(part, (1 - upper_half) * half_rows, half_rows, 0)
                for part in run_state
            )
        )
        received = partner_of((outgoing[0], outgoing[1], outgoing[2]), "ctx", bit_number)
        run_state = combine(kept, received)
    out_sum, top_score, weight_sum = run_state
    attended = (
        (out_sum / weight_sum[..., None])
        .astype(jnp.bfloat16)
        .reshape(segment, head_count * head_size)
    )
    partial_value = jnp.dot(
        lax.all_gather(attended, "ctx", axis=0, tiled=True),
        out_weight,
        preferred_element_type=jnp.float32,
    )
    return lax.psum_scatter(partial_value, "kv", scatter_dimension=0, tiled=True)


def body(queries, cache_keys, cache_values, block_mask, key_counts, out_weight):
    devices = lax.axis_size("ctx")
    token_count, head_count, d = queries.shape
    kv_count = cache_keys.shape[1]
    group_size = head_count // kv_count
    suits = (
        lax.axis_size("kv") == 1
        and devices == 32
        and token_count == BLK
        and block_mask.shape[0] == 1
        and kv_count == 4
        and d == LANES
        and group_size == 16
        and token_count * group_size == LANES * (devices // 2)
    )
    run = fast_body if suits else general_body
    return run(queries, cache_keys, cache_values, block_mask, key_counts, out_weight)


def solution(mesh):
    placed = (
        P("groups", "kv", None),
        P(("groups", "ctx"), "kv", None),
        P(("groups", "ctx"), "kv", None),
        P("groups", "ctx"),
        P(("groups", "ctx")),
        P("kv", "ctx"),
    )
    return jax.shard_map(
        body, mesh=mesh, in_specs=placed, out_specs=P(("groups", "kv"), "ctx"), check_vma=False
    )
```

```python
import functools
import math

import jax
import jax.numpy as jnp
from jax import lax
from jax.experimental import pallas as pl
from jax.experimental.pallas import tpu as pltpu
from jax.sharding import PartitionSpec as P

BLK = 128
LANES = 128
STAT = 8
very_low = -1e30
lowest_top = -(2.0**99)
bf16 = jnp.bfloat16
f32 = jnp.float32


def pack_state(out, top, total):
    high = total.astype(bf16).astype(f32)
    low = total - high
    row = lax.broadcasted_iota(jnp.int32, (STAT, LANES), 0)
    stats = jnp.where(row == 0, top, jnp.where(row == 1, high, jnp.where(row == 2, low, 0.0)))
    return out.astype(bf16), stats.astype(bf16)


def active_count(meta):
    block_count = (meta.shape[0] - 2) // 2
    return sum((meta[2 + block] > 0).astype(jnp.int32) for block in range(block_count))


def split_kernel(meta, k_hbm, v_hbm, q_hbm, kd, vt, sent_ref, *scratch):
    listed, kept_counts, q_ref, k_ref, v_ref, spread, sems = scratch
    d = k_hbm.shape[1]
    kv_count = kd.shape[0]
    group_size = q_ref.shape[1]
    block_count = (meta.shape[0] - 2) // 2
    group = 1 - meta[0]

    heads = pl.ds(pl.multiple_of(group * group_size, group_size), group_size)
    copies = [
        pltpu.make_async_copy(k_hbm, k_ref, sems.at[0]),
        pltpu.make_async_copy(v_hbm, v_ref, sems.at[1]),
        pltpu.make_async_copy(q_hbm.at[:, heads, :], q_ref, sems.at[2]),
    ]
    for copy in copies:
        copy.start()

    def note(block, found):
        listed[found] = block
        kept_counts[found] = meta[2 + block_count + block]
        return found + (meta[2 + block] > 0).astype(jnp.int32)

    active = lax.fori_loop(0, block_count, note, jnp.int32(0))
    place = lax.broadcasted_iota(jnp.int32, (BLK, LANES), 0)
    across = lax.broadcasted_iota(jnp.int32, (STAT, LANES), 1)

    def split(source, position):
        start = pl.multiple_of(listed[position] * (BLK * kv_count), BLK * kv_count)
        spread[...] = source[pl.ds(start, BLK * kv_count), :].astype(f32)
        return [spread[pl.ds(g, BLK, stride=kv_count), :] for g in range(kv_count)]

    def fetch_keys(position, carry):
        at = pl.ds(pl.multiple_of(position * BLK, BLK), BLK)
        valid = place < kept_counts[position]
        for g, key in enumerate(split(k_ref, position)):
            kd[g, at, :] = jnp.where(valid, key, key[0:1]).astype(bf16)
        return carry

    def fetch_values(position, carry):
        at = pl.ds(pl.multiple_of(position * BLK, BLK), BLK)
        count = kept_counts[position]
        for g, value in enumerate(split(v_ref, position)):
            vt[g, 0:d, at] = jnp.where(place < count, value, 0.0).T.astype(bf16)
            vt[g, d:, at] = (across < count).astype(f32).astype(bf16)
        return carry

    copies[0].wait()
    lax.fori_loop(0, active, fetch_keys, 0)
    copies[1].wait()
    lax.fori_loop(0, active, fetch_values, 0)

    @pl.when(active % 2 == 1)
    def _():
        at = pl.ds(pl.multiple_of(active * BLK, BLK), BLK)
        before = pl.ds(pl.multiple_of((active - 1) * BLK, BLK), BLK)
        for g in range(kv_count):
            kd[g, at, :] = kd[g, before, :]
            vt[g, :, at] = jnp.zeros((d + STAT, BLK), bf16)

    copies[2].wait()
    attend_all(active, [(sent_ref, group, lambda: q_ref[...])], kd, vt)


def attention_kernel(chunk_roles, meta, kd, vt, q_ref, *outs):
    group_size = q_ref.shape[1] // kd.shape[0]
    todo = []
    for out, (chunk, is_other) in zip(outs, chunk_roles):
        group = 2 * chunk + (1 - meta[0] if is_other else meta[0])

        def read(group=group):
            heads = pl.ds(pl.multiple_of(group * group_size, group_size), group_size)
            return q_ref[:, heads, :]

        todo.append((out, group, read))
    attend_all(active_count(meta), todo, kd, vt)


def attend_all(active, todo, kd, vt):
    d = kd.shape[2]
    scale2 = math.log2(math.e) / math.sqrt(d)
    rows = todo[0][0].shape[0] * LANES
    pairs = (active + 1) // 2

    def attend(width, out, group, read):
        q = read().reshape(rows, d)
        scores = lax.dot_general(
            kd[group, 0:width, :], q, (((1,), (1,)), ((), ())), preferred_element_type=f32
        )
        top = (jnp.max(scores, axis=0, keepdims=True) * scale2).astype(bf16).astype(f32)
        weights = jnp.exp2(scores * scale2 - top).astype(bf16)
        sums = jnp.dot(vt[group, :, 0:width], weights, preferred_element_type=f32)
        total = sums[d:]
        high = total.astype(bf16).astype(f32)
        row = lax.broadcasted_iota(jnp.int32, (STAT, rows), 0)
        stats = jnp.where(row == 0, top, jnp.where(row == 1, high, total - high)).astype(bf16)
        value = sums[:d].astype(bf16)
        for piece in range(rows // LANES):
            at = slice(piece * LANES, (piece + 1) * LANES)
            out[piece, 0:d] = value[:, at]
            out[piece, d:] = stats[:, at]

    for n in range(1, kd.shape[1] // (2 * BLK) + 1):

        @pl.when(pairs == n)
        def _(n=n):
            for out, group, read in todo:
                attend(2 * BLK * n, out, group, read)

    @pl.when(pairs == 0)
    def _():
        row = lax.broadcasted_iota(jnp.int32, (d + STAT, LANES), 0)
        empty = jnp.where(row == d, lowest_top, 0.0).astype(bf16)
        for out, _, _ in todo:
            for piece in range(rows // LANES):
                out[piece] = empty


def merged(parts, d):
    stats = [part[d : d + STAT, :].astype(f32) for part in parts]
    tops = [stat[0:1] for stat in stats]
    top = functools.reduce(jnp.maximum, tops)
    out, total = 0.0, 0.0
    for part, stat, one in zip(parts, stats, tops):
        factor = jnp.exp2(one - top)
        out = out + part[0:d, :].astype(f32) * factor
        total = total + (stat[1:2] + stat[2:3]) * factor
    return out, top, total


def store_merged(ref, z, parts):
    d = ref.shape[1] - STAT
    out, stats = pack_state(*merged(parts, d))
    ref[z, 0:d, :] = out
    ref[z, d : d + STAT, :] = stats


def plane_chips(meta):
    core, my_xy = meta[0], meta[1]
    return [my_xy, my_xy ^ (1 + core), my_xy ^ (2 - core), my_xy ^ 3]


def core_kernel(meta, kept, received, *outs):
    z_size = outs[0].shape[0]
    for chip, out in zip(plane_chips(meta), outs):
        for z in range(z_size):
            piece = chip * z_size + z
            store_merged(out, z, [kept[piece], received[piece]])


def plane_kernel(*refs):
    ins, out = refs[:-1], refs[-1]
    for z in range(out.shape[0]):
        store_merged(out, z, [ref[z] for ref in ins])


def last_kernel(*refs):
    ins, out_ref, turned = refs[:-2], refs[-2], refs[-1]
    d = ins[0].shape[1] - STAT
    tokens = out_ref.shape[1]
    heads = LANES // tokens
    for z in range(out_ref.shape[0]):
        out, _, total = merged([ref[z] for ref in ins], d)
        turned[z] = (out / total).T
        for h in range(heads):
            picked = turned[z, pl.ds(h, tokens, stride=heads), :]
            out_ref[z, :, h * d : (h + 1) * d] = picked.astype(bf16)


def project_kernel(terms, has_earlier, last, meta, weight, *refs):
    z_size, tokens, depth = refs[0].shape
    total = refs[4 * len(terms)][...] if has_earlier else None
    out_ref = refs[-1]
    for i, (chunk, is_other) in enumerate(terms):
        left = jnp.concatenate(
            [part[...].reshape(z_size * tokens, depth) for part in refs[4 * i : 4 * i + 4]], axis=0
        )
        group = 2 * chunk + (1 - meta[0] if is_other else meta[0])
        at = pl.ds(pl.multiple_of(group * depth, depth), depth)
        product = jnp.dot(left, weight[at, :], preferred_element_type=f32)
        total = product if total is None else total + product
    if not last:
        out_ref[...] = total
        return
    size = z_size * tokens
    for j, chip in enumerate(plane_chips(meta)):
        to = pl.ds(pl.multiple_of(chip * size, size), size)
        out_ref[to, :] = total[j * size : (j + 1) * size]


def hop(value, mask):
    pairs = [(source, source ^ mask) for source in range(lax.axis_size("ctx"))]
    return lax.ppermute(value, "ctx", pairs)


def plane_hop(value, number):
    masks = {1: (2, 4), 2: (4, 2), 3: (6, 6)}[number]
    pairs = [(source, source ^ masks[source % 2]) for source in range(lax.axis_size("ctx"))]
    return lax.ppermute(value, "ctx", pairs)


def line_hop(value, reach, z_size):
    masks = (8 * reach, 4 * z_size // reach)
    pairs = [(source, source ^ masks[source % 2]) for source in range(lax.axis_size("ctx"))]
    return lax.ppermute(value, "ctx", pairs)


VMEM = pl.BlockSpec(memory_space=pltpu.VMEM)
SMEM = pl.BlockSpec(memory_space=pltpu.SMEM)
HBM = pl.BlockSpec(memory_space=pltpu.HBM)
SMALL = pltpu.CompilerParams(vmem_limit_bytes=4 << 20)


def fast_body(queries, cache_keys, cache_values, block_mask, key_counts, out_weight):
    index = lax.axis_index("ctx")
    z_size = lax.axis_size("ctx") // 8
    token_count, head_count, d = queries.shape
    kv_count = cache_keys.shape[1]
    group_size = head_count // kv_count
    rows = token_count * group_size
    pieces = rows // LANES
    positions = cache_keys.shape[0]
    features = out_weight.shape[1]
    core = index & 1
    my_xy = (index >> 1) & 3
    tall = d + STAT
    keys = cache_keys.reshape(positions * kv_count, d)
    values = cache_values.reshape(positions * kv_count, d)
    place = jnp.concatenate(
        [jnp.stack([core, my_xy]).astype(jnp.int32), block_mask[0], key_counts]
    )
    kept_in_hbm = functools.partial(pltpu.with_memory_space_constraint, memory_space=pltpu.HBM)
    state = jax.ShapeDtypeStruct((z_size, tall, LANES), bf16)

    partial = jax.ShapeDtypeStruct((pieces, tall, LANES), bf16)
    blocks = positions // BLK

    def split_and_attend():
        return pl.pallas_call(
            split_kernel,
            in_specs=[SMEM] + [HBM] * 3,
            out_specs=[VMEM] * 3,
            scratch_shapes=[
                pltpu.SMEM((blocks + 1,), jnp.int32),
                pltpu.SMEM((blocks + 1,), jnp.int32),
                pltpu.VMEM((token_count, group_size, d), bf16),
                pltpu.VMEM((positions * kv_count, d), bf16),
                pltpu.VMEM((positions * kv_count, d), bf16),
                pltpu.VMEM((BLK * kv_count, d), f32),
                pltpu.SemaphoreType.DMA((3,)),
            ],
            out_shape=[
                jax.ShapeDtypeStruct((kv_count, positions, d), bf16),
                jax.ShapeDtypeStruct((kv_count, tall, positions), bf16),
                partial,
            ],
            compiler_params=pltpu.CompilerParams(vmem_limit_bytes=32 << 20),
            cost_estimate=pl.CostEstimate(
                flops=4 * rows * positions * d,
                transcendentals=rows * positions,
                bytes_accessed=4 * positions * d * kv_count,
            ),
            name="split_and_attend",
        )(place, kept_in_hbm(keys), kept_in_hbm(values), kept_in_hbm(queries))

    def attend(chunk_roles, kd, vt):
        count = len(chunk_roles)
        return pl.pallas_call(
            functools.partial(attention_kernel, chunk_roles),
            in_specs=[SMEM] + [VMEM] * 3,
            out_specs=[VMEM] * count,
            out_shape=[partial] * count,
            compiler_params=pltpu.CompilerParams(vmem_limit_bytes=32 << 20),
            cost_estimate=pl.CostEstimate(
                flops=4 * count * rows * positions * d,
                transcendentals=count * rows * positions,
                bytes_accessed=4 * positions * d * count,
            ),
            name="attend",
        )(place, kd, vt, queries)

    def merge_cores(kept, received):
        return pl.pallas_call(
            core_kernel,
            in_specs=[SMEM] + [VMEM] * 2,
            out_specs=[VMEM] * 4,
            out_shape=[state] * 4,
            compiler_params=SMALL,
            name="merge_cores",
        )(place, kept, received)

    def merge_chips(parts):
        return pl.pallas_call(
            plane_kernel,
            in_specs=[VMEM] * len(parts),
            out_specs=VMEM,
            out_shape=state,
            compiler_params=SMALL,
            name="merge_chips",
        )(*parts)

    def finish(parts):
        tokens = LANES // group_size
        return pl.pallas_call(
            last_kernel,
            in_specs=[VMEM] * len(parts),
            out_specs=VMEM,
            out_shape=jax.ShapeDtypeStruct((z_size, tokens, group_size * d), bf16),
            scratch_shapes=[pltpu.VMEM((z_size, LANES, d), f32)],
            compiler_params=SMALL,
            name="finish",
        )(*parts)

    def project(terms, parts, earlier, last=False):
        depth = group_size * d
        more = [] if earlier is None else [earlier]
        return pl.pallas_call(
            functools.partial(project_kernel, terms, bool(more), last),
            in_specs=[SMEM] + [VMEM] * (1 + len(parts) + len(more)),
            out_specs=VMEM,
            out_shape=jax.ShapeDtypeStruct((token_count, features), f32),
            compiler_params=pltpu.CompilerParams(vmem_limit_bytes=8 << 20),
            cost_estimate=pl.CostEstimate(
                flops=2 * len(terms) * token_count * depth * features,
                transcendentals=0,
                bytes_accessed=2 * len(terms) * depth * features,
            ),
            name="project",
        )(place, out_weight, *parts, *more)

    def exchange_plane(parts):
        return [parts[0]] + [plane_hop(parts[j], j) for j in (1, 2, 3)]

    def exchange_line(parts):
        part = merge_chips(parts)
        reach = 1
        while 2 * reach < z_size:
            part = merge_chips([part, line_hop(part, reach, z_size)])
            reach *= 2
        return finish([part, line_hop(part, reach, z_size)])

    def gather_plane(attended):
        first, second = plane_hop(attended, 1), plane_hop(attended, 2)
        return [attended, first, second, plane_hop(first, 2)]

    kd, vt, sent = split_and_attend()
    received = hop(sent, 1)
    kept, sent = attend([(0, False), (1, True)], kd, vt)
    next_received = hop(sent, 1)
    parts = merge_cores(kept, received)
    parts, kd = lax.optimization_barrier((parts, kd))
    first = exchange_plane(parts)
    (kept,) = attend([(1, False)], kd, vt)
    parts = merge_cores(kept, next_received)
    parts, first[0] = lax.optimization_barrier((parts, first[0]))
    second = exchange_plane(parts)
    own = gather_plane(exchange_line(first))
    other = [hop(own[j], 1) for j in (0, 2, 1, 3)]
    next_own = gather_plane(exchange_line(second))
    total = project([(0, False), (0, True)], own + other, None)
    next_own[3], total = lax.optimization_barrier((next_own[3], total))
    next_other = [hop(next_own[j], 1) for j in (0, 2, 1, 3)]
    total = project([(1, False)], next_own, total)
    return project([(1, True)], next_other, total, last=True)


def partner_of(value, axis, distance):
    mask = 2**distance
    pairs = [(source, source ^ mask) for source in range(lax.axis_size(axis))]
    return lax.ppermute(value, axis, pairs)


def combine(earlier, later):
    out_one, top_one, sum_one = earlier
    out_two, top_two, sum_two = later
    new_top = jnp.maximum(top_one, top_two)
    factor_one = jnp.exp(top_one - new_top)
    factor_two = jnp.exp(top_two - new_top)
    new_out = out_one * factor_one[..., None] + out_two * factor_two[..., None]
    return (new_out, new_top, sum_one * factor_one + sum_two * factor_two)


def keep_state(key_block, run_state):
    return run_state


def partial_rows(rows_q, row_mask, cache_keys, cache_values, key_counts):
    row_count, head_count, head_size = rows_q.shape
    kv_count = cache_keys.shape[1]
    group_size = head_count // kv_count
    grouped = rows_q.reshape(row_count, kv_count, group_size, head_size)
    block_count = cache_keys.shape[0] // BLK
    score_scale = 1.0 / math.sqrt(head_size)
    offsets = jnp.arange(BLK, dtype=jnp.int32)

    def update(key_block, run_state):
        out_sum, top_score, weight_sum = run_state
        key_part = lax.dynamic_slice_in_dim(cache_keys, key_block * BLK, BLK, 0)
        value_part = lax.dynamic_slice_in_dim(cache_values, key_block * BLK, BLK, 0)
        scores = (
            jnp.einsum("rgqd,kgd->rgqk", grouped, key_part, preferred_element_type=jnp.float32)
            * score_scale
        )
        active_rows = lax.dynamic_slice_in_dim(row_mask, key_block, 1, 1)[:, 0] > 0
        valid_count = lax.dynamic_slice_in_dim(key_counts, key_block, 1, 0)[0]
        valid = active_rows[:, None, None, None] & (offsets < valid_count)[None, None, None, :]
        scores = jnp.where(valid, scores, very_low)
        new_top = jnp.maximum(top_score, jnp.max(scores, axis=-1))
        weights = jnp.where(valid, jnp.exp(scores - new_top[..., None]), 0.0)
        factor = jnp.exp(top_score - new_top)
        new_sum = weight_sum * factor + jnp.sum(weights, axis=-1)
        new_out = out_sum * factor[..., None] + jnp.einsum(
            "rgqk,kgd->rgqd",
            weights.astype(jnp.bfloat16),
            value_part,
            preferred_element_type=jnp.float32,
        )
        return (new_out, new_top, new_sum)

    def visit_block(key_block, run_state):
        active = jnp.any(lax.dynamic_slice_in_dim(row_mask, key_block, 1, 1) > 0)
        return lax.cond(active, update, keep_state, key_block, run_state)

    initial = (
        jnp.zeros((row_count, kv_count, group_size, head_size), jnp.float32),
        jnp.full((row_count, kv_count, group_size), very_low, jnp.float32),
        jnp.zeros((row_count, kv_count, group_size), jnp.float32),
    )
    return lax.fori_loop(0, block_count, visit_block, initial)


def general_body(queries, cache_keys, cache_values, block_mask, key_counts, out_weight):
    cycle_size = lax.axis_size("ctx")
    cycle_index = lax.axis_index("ctx")
    token_count, head_count, head_size = queries.shape
    segment = token_count // cycle_size
    query_blocks = queries.reshape(block_mask.shape[0], BLK, head_count, head_size)

    def per_block(block_item):
        rows_q, mask_row = block_item
        row_mask = jnp.broadcast_to(mask_row[None, :], (BLK, mask_row.shape[0]))
        return partial_rows(rows_q, row_mask, cache_keys, cache_values, key_counts)

    stacked = lax.map(per_block, (query_blocks, block_mask))
    run_state = tuple((part.reshape((token_count,) + part.shape[2:]) for part in stacked))
    bit_total = cycle_size.bit_length() - 1
    for bit_number in range(bit_total - 1, -1, -1):
        half_rows = run_state[1].shape[0] // 2
        upper_half = jnp.bitwise_and(jnp.right_shift(cycle_index, bit_number), 1)
        kept = tuple(
            (
                lax.dynamic_slice_in_dim(part, upper_half * half_rows, half_rows, 0)
                for part in run_state
            )
        )
        outgoing = tuple(
            (
                lax.dynamic_slice_in_dim(part, (1 - upper_half) * half_rows, half_rows, 0)
                for part in run_state
            )
        )
        received = partner_of((outgoing[0], outgoing[1], outgoing[2]), "ctx", bit_number)
        run_state = combine(kept, received)
    out_sum, top_score, weight_sum = run_state
    attended = (
        (out_sum / weight_sum[..., None])
        .astype(jnp.bfloat16)
        .reshape(segment, head_count * head_size)
    )
    partial_value = jnp.dot(
        lax.all_gather(attended, "ctx", axis=0, tiled=True),
        out_weight,
        preferred_element_type=jnp.float32,
    )
    return lax.psum_scatter(partial_value, "kv", scatter_dimension=0, tiled=True)


def body(queries, cache_keys, cache_values, block_mask, key_counts, out_weight):
    devices = lax.axis_size("ctx")
    token_count, head_count, d = queries.shape
    kv_count = cache_keys.shape[1]
    group_size = head_count // kv_count
    suits = (
        lax.axis_size("kv") == 1
        and devices == 32
        and token_count == BLK
        and block_mask.shape[0] == 1
        and kv_count == 4
        and d == LANES
        and group_size == 16
        and token_count * group_size == LANES * (devices // 2)
    )
    run = fast_body if suits else general_body
    return run(queries, cache_keys, cache_values, block_mask, key_counts, out_weight)


def solution(mesh):
    placed = (
        P("groups", "kv", None),
        P(("groups", "ctx"), "kv", None),
        P(("groups", "ctx"), "kv", None),
        P("groups", "ctx"),
        P(("groups", "ctx")),
        P("kv", "ctx"),
    )
    return jax.shard_map(
        body, mesh=mesh, in_specs=placed, out_specs=P(("groups", "kv"), "ctx"), check_vma=False
    )
```

```python
import functools
import math

import jax
import jax.numpy as jnp
from jax import lax
from jax.experimental import pallas as pl
from jax.experimental.pallas import tpu as pltpu
from jax.sharding import PartitionSpec as P

BLK = 128
LANES = 128
STAT = 8
very_low = -1e30
lowest_top = -(2.0**99)
bf16 = jnp.bfloat16
f32 = jnp.float32


def pack_state(out, top, total):
    high = total.astype(bf16).astype(f32)
    low = total - high
    row = lax.broadcasted_iota(jnp.int32, (STAT, LANES), 0)
    stats = jnp.where(row == 0, top, jnp.where(row == 1, high, jnp.where(row == 2, low, 0.0)))
    return out.astype(bf16), stats.astype(bf16)


def active_count(meta):
    block_count = (meta.shape[0] - 2) // 2
    return sum((meta[2 + block] > 0).astype(jnp.int32) for block in range(block_count))


def split_kernel(meta, k_hbm, v_hbm, q_hbm, kd, vt, sent_ref, *scratch):
    listed, kept_counts, q_ref, k_ref, v_ref, spread, sems = scratch
    d = k_hbm.shape[1]
    kv_count = kd.shape[0]
    group_size = q_ref.shape[1]
    block_count = (meta.shape[0] - 2) // 2
    group = 1 - meta[0]

    heads = pl.ds(pl.multiple_of(group * group_size, group_size), group_size)
    copies = [
        pltpu.make_async_copy(k_hbm, k_ref, sems.at[0]),
        pltpu.make_async_copy(v_hbm, v_ref, sems.at[1]),
        pltpu.make_async_copy(q_hbm.at[:, heads, :], q_ref, sems.at[2]),
    ]
    for copy in copies:
        copy.start()

    def note(block, found):
        listed[found] = block
        kept_counts[found] = meta[2 + block_count + block]
        return found + (meta[2 + block] > 0).astype(jnp.int32)

    active = lax.fori_loop(0, block_count, note, jnp.int32(0))
    place = lax.broadcasted_iota(jnp.int32, (BLK, LANES), 0)
    across = lax.broadcasted_iota(jnp.int32, (STAT, LANES), 1)

    def split(source, position):
        start = pl.multiple_of(listed[position] * (BLK * kv_count), BLK * kv_count)
        spread[...] = source[pl.ds(start, BLK * kv_count), :].astype(f32)
        return [spread[pl.ds(g, BLK, stride=kv_count), :] for g in range(kv_count)]

    def fetch_keys(position, carry):
        at = pl.ds(pl.multiple_of(position * BLK, BLK), BLK)
        valid = place < kept_counts[position]
        for g, key in enumerate(split(k_ref, position)):
            kd[g, at, :] = jnp.where(valid, key, key[0:1]).astype(bf16)
        return carry

    def fetch_values(position, carry):
        at = pl.ds(pl.multiple_of(position * BLK, BLK), BLK)
        count = kept_counts[position]
        for g, value in enumerate(split(v_ref, position)):
            vt[g, 0:d, at] = jnp.where(place < count, value, 0.0).T.astype(bf16)
            vt[g, d:, at] = (across < count).astype(f32).astype(bf16)
        return carry

    copies[0].wait()
    lax.fori_loop(0, active, fetch_keys, 0)
    copies[1].wait()
    lax.fori_loop(0, active, fetch_values, 0)

    @pl.when(active % 2 == 1)
    def _():
        at = pl.ds(pl.multiple_of(active * BLK, BLK), BLK)
        before = pl.ds(pl.multiple_of((active - 1) * BLK, BLK), BLK)
        for g in range(kv_count):
            kd[g, at, :] = kd[g, before, :]
            vt[g, :, at] = jnp.zeros((d + STAT, BLK), bf16)

    copies[2].wait()
    attend_all(active, [(sent_ref, group, lambda: q_ref[...])], kd, vt)


def attention_kernel(chunk_roles, meta, kd, vt, q_ref, *outs):
    group_size = q_ref.shape[1] // kd.shape[0]
    todo = []
    for out, (chunk, is_other) in zip(outs, chunk_roles):
        group = 2 * chunk + (1 - meta[0] if is_other else meta[0])

        def read(group=group):
            heads = pl.ds(pl.multiple_of(group * group_size, group_size), group_size)
            return q_ref[:, heads, :]

        todo.append((out, group, read))
    attend_all(active_count(meta), todo, kd, vt)


def attend_all(active, todo, kd, vt):
    d = kd.shape[2]
    scale2 = math.log2(math.e) / math.sqrt(d)
    rows = todo[0][0].shape[0] * LANES
    pairs = (active + 1) // 2

    def attend(width, out, group, read):
        q = read().reshape(rows, d)
        scores = lax.dot_general(
            kd[group, 0:width, :], q, (((1,), (1,)), ((), ())), preferred_element_type=f32
        )
        top = (jnp.max(scores, axis=0, keepdims=True) * scale2).astype(bf16).astype(f32)
        weights = jnp.exp2(scores * scale2 - top).astype(bf16)
        sums = jnp.dot(vt[group, :, 0:width], weights, preferred_element_type=f32)
        total = sums[d:]
        high = total.astype(bf16).astype(f32)
        row = lax.broadcasted_iota(jnp.int32, (STAT, rows), 0)
        stats = jnp.where(row == 0, top, jnp.where(row == 1, high, total - high)).astype(bf16)
        value = sums[:d].astype(bf16)
        for piece in range(rows // LANES):
            at = slice(piece * LANES, (piece + 1) * LANES)
            out[piece, 0:d] = value[:, at]
            out[piece, d:] = stats[:, at]

    for n in range(1, kd.shape[1] // (2 * BLK) + 1):

        @pl.when(pairs == n)
        def _(n=n):
            for out, group, read in todo:
                attend(2 * BLK * n, out, group, read)

    @pl.when(pairs == 0)
    def _():
        row = lax.broadcasted_iota(jnp.int32, (d + STAT, LANES), 0)
        empty = jnp.where(row == d, lowest_top, 0.0).astype(bf16)
        for out, _, _ in todo:
            for piece in range(rows // LANES):
                out[piece] = empty


def merged(parts, d):
    stats = [part[d : d + STAT, :].astype(f32) for part in parts]
    tops = [stat[0:1] for stat in stats]
    top = functools.reduce(jnp.maximum, tops)
    out, total = 0.0, 0.0
    for part, stat, one in zip(parts, stats, tops):
        factor = jnp.exp2(one - top)
        out = out + part[0:d, :].astype(f32) * factor
        total = total + (stat[1:2] + stat[2:3]) * factor
    return out, top, total


def store_merged(ref, z, parts):
    d = ref.shape[1] - STAT
    out, stats = pack_state(*merged(parts, d))
    ref[z, 0:d, :] = out
    ref[z, d : d + STAT, :] = stats


def plane_chips(meta):
    core, my_xy = meta[0], meta[1]
    return [my_xy, my_xy ^ (1 + core), my_xy ^ (2 - core), my_xy ^ 3]


def core_kernel(meta, kept, received, *outs):
    z_size = outs[0].shape[0]
    for chip, out in zip(plane_chips(meta), outs):
        for z in range(z_size):
            piece = chip * z_size + z
            store_merged(out, z, [kept[piece], received[piece]])


def plane_kernel(*refs):
    ins, out = refs[:-1], refs[-1]
    for z in range(out.shape[0]):
        store_merged(out, z, [ref[z] for ref in ins])


def last_kernel(*refs):
    ins, out_ref, turned = refs[:-2], refs[-2], refs[-1]
    z_size, tall, _ = ins[0].shape
    d = tall - STAT
    tokens = out_ref.shape[1]
    heads = LANES // tokens
    for chunk in range(len(ins) // 2):
        for z in range(z_size):
            at = chunk * z_size + z
            out, _, total = merged([ref[z] for ref in ins[2 * chunk : 2 * chunk + 2]], d)
            turned[at] = (out / total).T
            for h in range(heads):
                picked = turned[at, pl.ds(h, tokens, stride=heads), :]
                out_ref[at, :, h * d : (h + 1) * d] = picked.astype(bf16)


def project_kernel(chunks, is_other, meta, weight, *refs):
    parts, out_ref = refs[:4], refs[-1]
    z_size = parts[0].shape[0] // chunks
    _, tokens, depth = parts[0].shape
    size = z_size * tokens
    total = refs[4][...] if is_other else None
    for chunk in range(chunks):
        at = slice(chunk * z_size, (chunk + 1) * z_size)
        left = jnp.concatenate([part[at].reshape(size, depth) for part in parts], axis=0)
        group = 2 * chunk + (1 - meta[0] if is_other else meta[0])
        rows = pl.ds(pl.multiple_of(group * depth, depth), depth)
        product = jnp.dot(left, weight[rows, :], preferred_element_type=f32)
        total = product if total is None else total + product
    if not is_other:
        out_ref[...] = total
        return
    for j, chip in enumerate(plane_chips(meta)):
        to = pl.ds(pl.multiple_of(chip * size, size), size)
        out_ref[to, :] = total[j * size : (j + 1) * size]


def hop(value, mask):
    pairs = [(source, source ^ mask) for source in range(lax.axis_size("ctx"))]
    return lax.ppermute(value, "ctx", pairs)


def plane_hop(value, number):
    masks = {1: (2, 4), 2: (4, 2), 3: (6, 6)}[number]
    pairs = [(source, source ^ masks[source % 2]) for source in range(lax.axis_size("ctx"))]
    return lax.ppermute(value, "ctx", pairs)


def line_hop(value, reach, z_size):
    masks = (8 * reach, 4 * z_size // reach)
    pairs = [(source, source ^ masks[source % 2]) for source in range(lax.axis_size("ctx"))]
    return lax.ppermute(value, "ctx", pairs)


VMEM = pl.BlockSpec(memory_space=pltpu.VMEM)
SMEM = pl.BlockSpec(memory_space=pltpu.SMEM)
HBM = pl.BlockSpec(memory_space=pltpu.HBM)
SMALL = pltpu.CompilerParams(vmem_limit_bytes=4 << 20)


def fast_body(queries, cache_keys, cache_values, block_mask, key_counts, out_weight):
    index = lax.axis_index("ctx")
    z_size = lax.axis_size("ctx") // 8
    token_count, head_count, d = queries.shape
    kv_count = cache_keys.shape[1]
    group_size = head_count // kv_count
    rows = token_count * group_size
    pieces = rows // LANES
    positions = cache_keys.shape[0]
    features = out_weight.shape[1]
    core = index & 1
    my_xy = (index >> 1) & 3
    tall = d + STAT
    keys = cache_keys.reshape(positions * kv_count, d)
    values = cache_values.reshape(positions * kv_count, d)
    place = jnp.concatenate(
        [jnp.stack([core, my_xy]).astype(jnp.int32), block_mask[0], key_counts]
    )
    kept_in_hbm = functools.partial(pltpu.with_memory_space_constraint, memory_space=pltpu.HBM)
    state = jax.ShapeDtypeStruct((z_size, tall, LANES), bf16)

    partial = jax.ShapeDtypeStruct((pieces, tall, LANES), bf16)
    blocks = positions // BLK

    def split_and_attend():
        return pl.pallas_call(
            split_kernel,
            in_specs=[SMEM] + [HBM] * 3,
            out_specs=[VMEM] * 3,
            scratch_shapes=[
                pltpu.SMEM((blocks + 1,), jnp.int32),
                pltpu.SMEM((blocks + 1,), jnp.int32),
                pltpu.VMEM((token_count, group_size, d), bf16),
                pltpu.VMEM((positions * kv_count, d), bf16),
                pltpu.VMEM((positions * kv_count, d), bf16),
                pltpu.VMEM((BLK * kv_count, d), f32),
                pltpu.SemaphoreType.DMA((3,)),
            ],
            out_shape=[
                jax.ShapeDtypeStruct((kv_count, positions, d), bf16),
                jax.ShapeDtypeStruct((kv_count, tall, positions), bf16),
                partial,
            ],
            compiler_params=pltpu.CompilerParams(vmem_limit_bytes=32 << 20),
            cost_estimate=pl.CostEstimate(
                flops=4 * rows * positions * d,
                transcendentals=rows * positions,
                bytes_accessed=4 * positions * d * kv_count,
            ),
            name="split_and_attend",
        )(place, kept_in_hbm(keys), kept_in_hbm(values), kept_in_hbm(queries))

    def attend(chunk_roles, kd, vt):
        count = len(chunk_roles)
        return pl.pallas_call(
            functools.partial(attention_kernel, chunk_roles),
            in_specs=[SMEM] + [VMEM] * 3,
            out_specs=[VMEM] * count,
            out_shape=[partial] * count,
            compiler_params=pltpu.CompilerParams(vmem_limit_bytes=32 << 20),
            cost_estimate=pl.CostEstimate(
                flops=4 * count * rows * positions * d,
                transcendentals=count * rows * positions,
                bytes_accessed=4 * positions * d * count,
            ),
            name="attend",
        )(place, kd, vt, queries)

    def merge_cores(kept, received):
        return pl.pallas_call(
            core_kernel,
            in_specs=[SMEM] + [VMEM] * 2,
            out_specs=[VMEM] * 4,
            out_shape=[state] * 4,
            compiler_params=SMALL,
            name="merge_cores",
        )(place, kept, received)

    def merge_chips(parts):
        return pl.pallas_call(
            plane_kernel,
            in_specs=[VMEM] * len(parts),
            out_specs=VMEM,
            out_shape=state,
            compiler_params=SMALL,
            name="merge_chips",
        )(*parts)

    def finish(parts):
        tokens = LANES // group_size
        shape = (len(parts) // 2 * z_size, tokens, group_size * d)
        return pl.pallas_call(
            last_kernel,
            in_specs=[VMEM] * len(parts),
            out_specs=VMEM,
            out_shape=jax.ShapeDtypeStruct(shape, bf16),
            scratch_shapes=[pltpu.VMEM((shape[0], LANES, d), f32)],
            compiler_params=SMALL,
            name="finish",
        )(*parts)

    def project(parts, earlier=None):
        chunks = kv_count // 2
        depth = group_size * d
        more = [] if earlier is None else [earlier]
        return pl.pallas_call(
            functools.partial(project_kernel, chunks, bool(more)),
            in_specs=[SMEM] + [VMEM] * (1 + len(parts) + len(more)),
            out_specs=VMEM,
            out_shape=jax.ShapeDtypeStruct((token_count, features), f32),
            compiler_params=pltpu.CompilerParams(vmem_limit_bytes=8 << 20),
            cost_estimate=pl.CostEstimate(
                flops=2 * chunks * token_count * depth * features,
                transcendentals=0,
                bytes_accessed=2 * chunks * depth * features,
            ),
            name="project",
        )(place, out_weight, *parts, *more)

    def exchange_plane(parts):
        return [parts[0]] + [plane_hop(parts[j], j) for j in (1, 2, 3)]

    def exchange_line(parts):
        part = merge_chips(parts)
        reach = 1
        while 2 * reach < z_size:
            part = merge_chips([part, line_hop(part, reach, z_size)])
            reach *= 2
        return [part, line_hop(part, reach, z_size)]

    def gather_plane(attended):
        first, second = plane_hop(attended, 1), plane_hop(attended, 2)
        return [attended, first, second, plane_hop(first, 2)]

    kd, vt, sent = split_and_attend()
    received = hop(sent, 1)
    kept, sent = attend([(0, False), (1, True)], kd, vt)
    next_received = hop(sent, 1)
    parts = merge_cores(kept, received)
    parts, kd = lax.optimization_barrier((parts, kd))
    first = exchange_plane(parts)
    (kept,) = attend([(1, False)], kd, vt)
    parts = merge_cores(kept, next_received)
    parts, first[0] = lax.optimization_barrier((parts, first[0]))
    second = exchange_plane(parts)
    own = gather_plane(finish(exchange_line(first) + exchange_line(second)))
    other = [hop(own[j], 1) for j in (0, 2, 1, 3)]
    return project(other, project(own))


def partner_of(value, axis, distance):
    mask = 2**distance
    pairs = [(source, source ^ mask) for source in range(lax.axis_size(axis))]
    return lax.ppermute(value, axis, pairs)


def combine(earlier, later):
    out_one, top_one, sum_one = earlier
    out_two, top_two, sum_two = later
    new_top = jnp.maximum(top_one, top_two)
    factor_one = jnp.exp(top_one - new_top)
    factor_two = jnp.exp(top_two - new_top)
    new_out = out_one * factor_one[..., None] + out_two * factor_two[..., None]
    return (new_out, new_top, sum_one * factor_one + sum_two * factor_two)


def keep_state(key_block, run_state):
    return run_state


def partial_rows(rows_q, row_mask, cache_keys, cache_values, key_counts):
    row_count, head_count, head_size = rows_q.shape
    kv_count = cache_keys.shape[1]
    group_size = head_count // kv_count
    grouped = rows_q.reshape(row_count, kv_count, group_size, head_size)
    block_count = cache_keys.shape[0] // BLK
    score_scale = 1.0 / math.sqrt(head_size)
    offsets = jnp.arange(BLK, dtype=jnp.int32)

    def update(key_block, run_state):
        out_sum, top_score, weight_sum = run_state
        key_part = lax.dynamic_slice_in_dim(cache_keys, key_block * BLK, BLK, 0)
        value_part = lax.dynamic_slice_in_dim(cache_values, key_block * BLK, BLK, 0)
        scores = (
            jnp.einsum("rgqd,kgd->rgqk", grouped, key_part, preferred_element_type=jnp.float32)
            * score_scale
        )
        active_rows = lax.dynamic_slice_in_dim(row_mask, key_block, 1, 1)[:, 0] > 0
        valid_count = lax.dynamic_slice_in_dim(key_counts, key_block, 1, 0)[0]
        valid = active_rows[:, None, None, None] & (offsets < valid_count)[None, None, None, :]
        scores = jnp.where(valid, scores, very_low)
        new_top = jnp.maximum(top_score, jnp.max(scores, axis=-1))
        weights = jnp.where(valid, jnp.exp(scores - new_top[..., None]), 0.0)
        factor = jnp.exp(top_score - new_top)
        new_sum = weight_sum * factor + jnp.sum(weights, axis=-1)
        new_out = out_sum * factor[..., None] + jnp.einsum(
            "rgqk,kgd->rgqd",
            weights.astype(jnp.bfloat16),
            value_part,
            preferred_element_type=jnp.float32,
        )
        return (new_out, new_top, new_sum)

    def visit_block(key_block, run_state):
        active = jnp.any(lax.dynamic_slice_in_dim(row_mask, key_block, 1, 1) > 0)
        return lax.cond(active, update, keep_state, key_block, run_state)

    initial = (
        jnp.zeros((row_count, kv_count, group_size, head_size), jnp.float32),
        jnp.full((row_count, kv_count, group_size), very_low, jnp.float32),
        jnp.zeros((row_count, kv_count, group_size), jnp.float32),
    )
    return lax.fori_loop(0, block_count, visit_block, initial)


def general_body(queries, cache_keys, cache_values, block_mask, key_counts, out_weight):
    cycle_size = lax.axis_size("ctx")
    cycle_index = lax.axis_index("ctx")
    token_count, head_count, head_size = queries.shape
    segment = token_count // cycle_size
    query_blocks = queries.reshape(block_mask.shape[0], BLK, head_count, head_size)

    def per_block(block_item):
        rows_q, mask_row = block_item
        row_mask = jnp.broadcast_to(mask_row[None, :], (BLK, mask_row.shape[0]))
        return partial_rows(rows_q, row_mask, cache_keys, cache_values, key_counts)

    stacked = lax.map(per_block, (query_blocks, block_mask))
    run_state = tuple((part.reshape((token_count,) + part.shape[2:]) for part in stacked))
    bit_total = cycle_size.bit_length() - 1
    for bit_number in range(bit_total - 1, -1, -1):
        half_rows = run_state[1].shape[0] // 2
        upper_half = jnp.bitwise_and(jnp.right_shift(cycle_index, bit_number), 1)
        kept = tuple(
            (
                lax.dynamic_slice_in_dim(part, upper_half * half_rows, half_rows, 0)
                for part in run_state
            )
        )
        outgoing = tuple(
            (
                lax.dynamic_slice_in_dim(part, (1 - upper_half) * half_rows, half_rows, 0)
                for part in run_state
            )
        )
        received = partner_of((outgoing[0], outgoing[1], outgoing[2]), "ctx", bit_number)
        run_state = combine(kept, received)
    out_sum, top_score, weight_sum = run_state
    attended = (
        (out_sum / weight_sum[..., None])
        .astype(jnp.bfloat16)
        .reshape(segment, head_count * head_size)
    )
    partial_value = jnp.dot(
        lax.all_gather(attended, "ctx", axis=0, tiled=True),
        out_weight,
        preferred_element_type=jnp.float32,
    )
    return lax.psum_scatter(partial_value, "kv", scatter_dimension=0, tiled=True)


def body(queries, cache_keys, cache_values, block_mask, key_counts, out_weight):
    devices = lax.axis_size("ctx")
    token_count, head_count, d = queries.shape
    kv_count = cache_keys.shape[1]
    group_size = head_count // kv_count
    suits = (
        lax.axis_size("kv") == 1
        and devices == 32
        and token_count == BLK
        and block_mask.shape[0] == 1
        and kv_count == 4
        and d == LANES
        and group_size == 16
        and token_count * group_size == LANES * (devices // 2)
    )
    run = fast_body if suits else general_body
    return run(queries, cache_keys, cache_values, block_mask, key_counts, out_weight)


def solution(mesh):
    placed = (
        P("groups", "kv", None),
        P(("groups", "ctx"), "kv", None),
        P(("groups", "ctx"), "kv", None),
        P("groups", "ctx"),
        P(("groups", "ctx")),
        P("kv", "ctx"),
    )
    return jax.shard_map(
        body, mesh=mesh, in_specs=placed, out_specs=P(("groups", "kv"), "ctx"), check_vma=False
    )
```

```python
import functools
import math

import jax
import jax.numpy as jnp
from jax import lax
from jax.experimental import pallas as pl
from jax.experimental.pallas import tpu as pltpu
from jax.sharding import PartitionSpec as P

BLK = 128
LANES = 128
STAT = 8
very_low = -1e30
lowest_top = -(2.0**99)
bf16 = jnp.bfloat16
f32 = jnp.float32


def pack_state(out, top, total):
    high = total.astype(bf16).astype(f32)
    low = total - high
    row = lax.broadcasted_iota(jnp.int32, (STAT, LANES), 0)
    stats = jnp.where(row == 0, top, jnp.where(row == 1, high, jnp.where(row == 2, low, 0.0)))
    return out.astype(bf16), stats.astype(bf16)


def active_count(meta):
    block_count = (meta.shape[0] - 2) // 2
    return sum((meta[2 + block] > 0).astype(jnp.int32) for block in range(block_count))


def split_kernel(meta, k_hbm, v_hbm, q_hbm, kd, vt, sent_ref, *scratch):
    listed, kept_counts, q_ref, k_ref, v_ref, spread, sems = scratch
    d = k_hbm.shape[1]
    kv_count = kd.shape[0]
    group_size = q_ref.shape[1]
    block_count = (meta.shape[0] - 2) // 2
    group = 1 - meta[0]

    heads = pl.ds(pl.multiple_of(group * group_size, group_size), group_size)
    copies = [
        pltpu.make_async_copy(k_hbm, k_ref, sems.at[0]),
        pltpu.make_async_copy(v_hbm, v_ref, sems.at[1]),
        pltpu.make_async_copy(q_hbm.at[:, heads, :], q_ref, sems.at[2]),
    ]
    for copy in copies:
        copy.start()

    def note(block, found):
        listed[found] = block
        kept_counts[found] = meta[2 + block_count + block]
        return found + (meta[2 + block] > 0).astype(jnp.int32)

    active = lax.fori_loop(0, block_count, note, jnp.int32(0))
    place = lax.broadcasted_iota(jnp.int32, (BLK, LANES), 0)
    across = lax.broadcasted_iota(jnp.int32, (STAT, LANES), 1)

    def split(source, position):
        start = pl.multiple_of(listed[position] * (BLK * kv_count), BLK * kv_count)
        spread[...] = source[pl.ds(start, BLK * kv_count), :].astype(f32)
        return [spread[pl.ds(g, BLK, stride=kv_count), :] for g in range(kv_count)]

    def fetch_keys(position, carry):
        at = pl.ds(pl.multiple_of(position * BLK, BLK), BLK)
        valid = place < kept_counts[position]
        for g, key in enumerate(split(k_ref, position)):
            kd[g, at, :] = jnp.where(valid, key, key[0:1]).astype(bf16)
        return carry

    def fetch_values(position, carry):
        at = pl.ds(pl.multiple_of(position * BLK, BLK), BLK)
        count = kept_counts[position]
        for g, value in enumerate(split(v_ref, position)):
            vt[g, 0:d, at] = jnp.where(place < count, value, 0.0).T.astype(bf16)
            vt[g, d:, at] = (across < count).astype(f32).astype(bf16)
        return carry

    copies[0].wait()
    lax.fori_loop(0, active, fetch_keys, 0)
    copies[1].wait()
    lax.fori_loop(0, active, fetch_values, 0)

    @pl.when(active % 2 == 1)
    def _():
        at = pl.ds(pl.multiple_of(active * BLK, BLK), BLK)
        before = pl.ds(pl.multiple_of((active - 1) * BLK, BLK), BLK)
        for g in range(kv_count):
            kd[g, at, :] = kd[g, before, :]
            vt[g, :, at] = jnp.zeros((d + STAT, BLK), bf16)

    copies[2].wait()
    attend_all(active, [(sent_ref, group, lambda: q_ref[...])], kd, vt)


def attention_kernel(chunk_roles, meta, kd, vt, q_ref, *outs):
    group_size = q_ref.shape[1] // kd.shape[0]
    todo = []
    for out, (chunk, is_other) in zip(outs, chunk_roles):
        group = 2 * chunk + (1 - meta[0] if is_other else meta[0])

        def read(group=group):
            heads = pl.ds(pl.multiple_of(group * group_size, group_size), group_size)
            return q_ref[:, heads, :]

        todo.append((out, group, read))
    attend_all(active_count(meta), todo, kd, vt)


def attend_all(active, todo, kd, vt):
    d = kd.shape[2]
    scale2 = math.log2(math.e) / math.sqrt(d)
    rows = todo[0][0].shape[0] * LANES
    pairs = (active + 1) // 2

    def attend(width, out, group, read):
        q = read().reshape(rows, d)
        scores = lax.dot_general(
            kd[group, 0:width, :], q, (((1,), (1,)), ((), ())), preferred_element_type=f32
        )
        top = (jnp.max(scores, axis=0, keepdims=True) * scale2).astype(bf16).astype(f32)
        weights = jnp.exp2(scores * scale2 - top).astype(bf16)
        sums = jnp.dot(vt[group, :, 0:width], weights, preferred_element_type=f32)
        total = sums[d:]
        high = total.astype(bf16).astype(f32)
        row = lax.broadcasted_iota(jnp.int32, (STAT, rows), 0)
        stats = jnp.where(row == 0, top, jnp.where(row == 1, high, total - high)).astype(bf16)
        value = sums[:d].astype(bf16)
        for piece in range(rows // LANES):
            at = slice(piece * LANES, (piece + 1) * LANES)
            out[piece, 0:d] = value[:, at]
            out[piece, d:] = stats[:, at]

    for n in range(1, kd.shape[1] // (2 * BLK) + 1):

        @pl.when(pairs == n)
        def _(n=n):
            for out, group, read in todo:
                attend(2 * BLK * n, out, group, read)

    @pl.when(pairs == 0)
    def _():
        row = lax.broadcasted_iota(jnp.int32, (d + STAT, LANES), 0)
        empty = jnp.where(row == d, lowest_top, 0.0).astype(bf16)
        for out, _, _ in todo:
            for piece in range(rows // LANES):
                out[piece] = empty


def merged(parts, d):
    stats = [part[d : d + STAT, :].astype(f32) for part in parts]
    tops = [stat[0:1] for stat in stats]
    top = functools.reduce(jnp.maximum, tops)
    out, total = 0.0, 0.0
    for part, stat, one in zip(parts, stats, tops):
        factor = jnp.exp2(one - top)
        out = out + part[0:d, :].astype(f32) * factor
        total = total + (stat[1:2] + stat[2:3]) * factor
    return out, top, total


def store_merged(ref, z, parts):
    d = ref.shape[1] - STAT
    out, stats = pack_state(*merged(parts, d))
    ref[z, 0:d, :] = out
    ref[z, d : d + STAT, :] = stats


def plane_chips(meta):
    core, my_xy = meta[0], meta[1]
    return [my_xy, my_xy ^ (1 + core), my_xy ^ (2 - core), my_xy ^ 3]


def core_kernel(meta, kept, received, *outs):
    z_size = outs[0].shape[0]
    for chip, out in zip(plane_chips(meta), outs):
        for z in range(z_size):
            piece = chip * z_size + z
            store_merged(out, z, [kept[piece], received[piece]])


def plane_kernel(*refs):
    ins, out = refs[:-1], refs[-1]
    for z in range(out.shape[0]):
        store_merged(out, z, [ref[z] for ref in ins])


def last_kernel(*refs):
    ins, out_ref, turned = refs[:-2], refs[-2], refs[-1]
    d = ins[0].shape[1] - STAT
    tokens = out_ref.shape[1]
    heads = LANES // tokens
    for z in range(out_ref.shape[0]):
        out, _, total = merged([ref[z] for ref in ins], d)
        turned[z] = (out / total).T
        for h in range(heads):
            picked = turned[z, pl.ds(h, tokens, stride=heads), :]
            out_ref[z, :, h * d : (h + 1) * d] = picked.astype(bf16)


def project_kernel(terms, has_earlier, last, meta, weight, *refs):
    z_size, tokens, depth = refs[0].shape
    total = refs[4 * len(terms)][...] if has_earlier else None
    out_ref = refs[-1]
    for i, (chunk, is_other) in enumerate(terms):
        left = jnp.concatenate(
            [part[...].reshape(z_size * tokens, depth) for part in refs[4 * i : 4 * i + 4]], axis=0
        )
        group = 2 * chunk + (1 - meta[0] if is_other else meta[0])
        at = pl.ds(pl.multiple_of(group * depth, depth), depth)
        product = jnp.dot(left, weight[at, :], preferred_element_type=f32)
        total = product if total is None else total + product
    if not last:
        out_ref[...] = total
        return
    size = z_size * tokens
    for j, chip in enumerate(plane_chips(meta)):
        to = pl.ds(pl.multiple_of(chip * size, size), size)
        out_ref[to, :] = total[j * size : (j + 1) * size]


def hop(value, mask):
    pairs = [(source, source ^ mask) for source in range(lax.axis_size("ctx"))]
    return lax.ppermute(value, "ctx", pairs)


def plane_hop(value, number):
    masks = {1: (2, 4), 2: (4, 2), 3: (6, 6)}[number]
    pairs = [(source, source ^ masks[source % 2]) for source in range(lax.axis_size("ctx"))]
    return lax.ppermute(value, "ctx", pairs)


def line_hop(value, reach, z_size):
    masks = (8 * reach, 4 * z_size // reach)
    pairs = [(source, source ^ masks[source % 2]) for source in range(lax.axis_size("ctx"))]
    return lax.ppermute(value, "ctx", pairs)


VMEM = pl.BlockSpec(memory_space=pltpu.VMEM)
SMEM = pl.BlockSpec(memory_space=pltpu.SMEM)
HBM = pl.BlockSpec(memory_space=pltpu.HBM)
SMALL = pltpu.CompilerParams(vmem_limit_bytes=4 << 20)


def fast_body(queries, cache_keys, cache_values, block_mask, key_counts, out_weight):
    index = lax.axis_index("ctx")
    z_size = lax.axis_size("ctx") // 8
    token_count, head_count, d = queries.shape
    kv_count = cache_keys.shape[1]
    group_size = head_count // kv_count
    rows = token_count * group_size
    pieces = rows // LANES
    positions = cache_keys.shape[0]
    features = out_weight.shape[1]
    core = index & 1
    my_xy = (index >> 1) & 3
    tall = d + STAT
    keys = cache_keys.reshape(positions * kv_count, d)
    values = cache_values.reshape(positions * kv_count, d)
    place = jnp.concatenate(
        [jnp.stack([core, my_xy]).astype(jnp.int32), block_mask[0], key_counts]
    )
    kept_in_hbm = functools.partial(pltpu.with_memory_space_constraint, memory_space=pltpu.HBM)
    state = jax.ShapeDtypeStruct((z_size, tall, LANES), bf16)

    partial = jax.ShapeDtypeStruct((pieces, tall, LANES), bf16)
    blocks = positions // BLK

    def split_and_attend():
        return pl.pallas_call(
            split_kernel,
            in_specs=[SMEM] + [HBM] * 3,
            out_specs=[VMEM] * 3,
            scratch_shapes=[
                pltpu.SMEM((blocks + 1,), jnp.int32),
                pltpu.SMEM((blocks + 1,), jnp.int32),
                pltpu.VMEM((token_count, group_size, d), bf16),
                pltpu.VMEM((positions * kv_count, d), bf16),
                pltpu.VMEM((positions * kv_count, d), bf16),
                pltpu.VMEM((BLK * kv_count, d), f32),
                pltpu.SemaphoreType.DMA((3,)),
            ],
            out_shape=[
                jax.ShapeDtypeStruct((kv_count, positions, d), bf16),
                jax.ShapeDtypeStruct((kv_count, tall, positions), bf16),
                partial,
            ],
            compiler_params=pltpu.CompilerParams(vmem_limit_bytes=32 << 20),
            cost_estimate=pl.CostEstimate(
                flops=4 * rows * positions * d,
                transcendentals=rows * positions,
                bytes_accessed=4 * positions * d * kv_count,
            ),
            name="split_and_attend",
        )(place, kept_in_hbm(keys), kept_in_hbm(values), kept_in_hbm(queries))

    def attend(chunk_roles, kd, vt):
        count = len(chunk_roles)
        return pl.pallas_call(
            functools.partial(attention_kernel, chunk_roles),
            in_specs=[SMEM] + [VMEM] * 3,
            out_specs=[VMEM] * count,
            out_shape=[partial] * count,
            compiler_params=pltpu.CompilerParams(vmem_limit_bytes=32 << 20),
            cost_estimate=pl.CostEstimate(
                flops=4 * count * rows * positions * d,
                transcendentals=count * rows * positions,
                bytes_accessed=4 * positions * d * count,
            ),
            name="attend",
        )(place, kd, vt, queries)

    def merge_cores(kept, received):
        return pl.pallas_call(
            core_kernel,
            in_specs=[SMEM] + [VMEM] * 2,
            out_specs=[VMEM] * 4,
            out_shape=[state] * 4,
            compiler_params=SMALL,
            name="merge_cores",
        )(place, kept, received)

    def merge_chips(parts):
        return pl.pallas_call(
            plane_kernel,
            in_specs=[VMEM] * len(parts),
            out_specs=VMEM,
            out_shape=state,
            compiler_params=SMALL,
            name="merge_chips",
        )(*parts)

    def finish(parts):
        tokens = LANES // group_size
        return pl.pallas_call(
            last_kernel,
            in_specs=[VMEM] * len(parts),
            out_specs=VMEM,
            out_shape=jax.ShapeDtypeStruct((z_size, tokens, group_size * d), bf16),
            scratch_shapes=[pltpu.VMEM((z_size, LANES, d), f32)],
            compiler_params=SMALL,
            name="finish",
        )(*parts)

    def project(terms, parts, earlier, last=False):
        depth = group_size * d
        more = [] if earlier is None else [earlier]
        return pl.pallas_call(
            functools.partial(project_kernel, terms, bool(more), last),
            in_specs=[SMEM] + [VMEM] * (1 + len(parts) + len(more)),
            out_specs=VMEM,
            out_shape=jax.ShapeDtypeStruct((token_count, features), f32),
            compiler_params=pltpu.CompilerParams(vmem_limit_bytes=8 << 20),
            cost_estimate=pl.CostEstimate(
                flops=2 * len(terms) * token_count * depth * features,
                transcendentals=0,
                bytes_accessed=2 * len(terms) * depth * features,
            ),
            name="project",
        )(place, out_weight, *parts, *more)

    def exchange_plane(parts):
        return [parts[0]] + [plane_hop(parts[j], j) for j in (1, 2, 3)]

    def exchange_line(part):
        reach = 1
        while 2 * reach < z_size:
            part = merge_chips([part, line_hop(part, reach, z_size)])
            reach *= 2
        return finish([part, line_hop(part, reach, z_size)])

    def gather_plane(attended):
        first, second = plane_hop(attended, 1), plane_hop(attended, 2)
        return [attended, first, second, plane_hop(first, 2)]

    kd, vt, sent = split_and_attend()
    received = hop(sent, 1)
    kept, sent = attend([(0, False), (1, True)], kd, vt)
    next_received = hop(sent, 1)
    parts = merge_cores(kept, received)
    parts, kd = lax.optimization_barrier((parts, kd))
    first = exchange_plane(parts)
    (kept,) = attend([(1, False)], kd, vt)
    parts = merge_cores(kept, next_received)
    parts, first[0] = lax.optimization_barrier((parts, first[0]))
    merged_first = merge_chips(first)
    parts, merged_first = lax.optimization_barrier((parts, merged_first))
    own = exchange_line(merged_first)
    second = merge_chips(exchange_plane(parts))
    own = gather_plane(own)
    other = [hop(own[j], 1) for j in (0, 2, 1, 3)]
    next_own = gather_plane(exchange_line(second))
    total = project([(0, False), (0, True)], own + other, None)
    next_own[3], total = lax.optimization_barrier((next_own[3], total))
    next_other = [hop(next_own[j], 1) for j in (0, 2, 1, 3)]
    total = project([(1, False)], next_own, total)
    return project([(1, True)], next_other, total, last=True)


def partner_of(value, axis, distance):
    mask = 2**distance
    pairs = [(source, source ^ mask) for source in range(lax.axis_size(axis))]
    return lax.ppermute(value, axis, pairs)


def combine(earlier, later):
    out_one, top_one, sum_one = earlier
    out_two, top_two, sum_two = later
    new_top = jnp.maximum(top_one, top_two)
    factor_one = jnp.exp(top_one - new_top)
    factor_two = jnp.exp(top_two - new_top)
    new_out = out_one * factor_one[..., None] + out_two * factor_two[..., None]
    return (new_out, new_top, sum_one * factor_one + sum_two * factor_two)


def keep_state(key_block, run_state):
    return run_state


def partial_rows(rows_q, row_mask, cache_keys, cache_values, key_counts):
    row_count, head_count, head_size = rows_q.shape
    kv_count = cache_keys.shape[1]
    group_size = head_count // kv_count
    grouped = rows_q.reshape(row_count, kv_count, group_size, head_size)
    block_count = cache_keys.shape[0] // BLK
    score_scale = 1.0 / math.sqrt(head_size)
    offsets = jnp.arange(BLK, dtype=jnp.int32)

    def update(key_block, run_state):
        out_sum, top_score, weight_sum = run_state
        key_part = lax.dynamic_slice_in_dim(cache_keys, key_block * BLK, BLK, 0)
        value_part = lax.dynamic_slice_in_dim(cache_values, key_block * BLK, BLK, 0)
        scores = (
            jnp.einsum("rgqd,kgd->rgqk", grouped, key_part, preferred_element_type=jnp.float32)
            * score_scale
        )
        active_rows = lax.dynamic_slice_in_dim(row_mask, key_block, 1, 1)[:, 0] > 0
        valid_count = lax.dynamic_slice_in_dim(key_counts, key_block, 1, 0)[0]
        valid = active_rows[:, None, None, None] & (offsets < valid_count)[None, None, None, :]
        scores = jnp.where(valid, scores, very_low)
        new_top = jnp.maximum(top_score, jnp.max(scores, axis=-1))
        weights = jnp.where(valid, jnp.exp(scores - new_top[..., None]), 0.0)
        factor = jnp.exp(top_score - new_top)
        new_sum = weight_sum * factor + jnp.sum(weights, axis=-1)
        new_out = out_sum * factor[..., None] + jnp.einsum(
            "rgqk,kgd->rgqd",
            weights.astype(jnp.bfloat16),
            value_part,
            preferred_element_type=jnp.float32,
        )
        return (new_out, new_top, new_sum)

    def visit_block(key_block, run_state):
        active = jnp.any(lax.dynamic_slice_in_dim(row_mask, key_block, 1, 1) > 0)
        return lax.cond(active, update, keep_state, key_block, run_state)

    initial = (
        jnp.zeros((row_count, kv_count, group_size, head_size), jnp.float32),
        jnp.full((row_count, kv_count, group_size), very_low, jnp.float32),
        jnp.zeros((row_count, kv_count, group_size), jnp.float32),
    )
    return lax.fori_loop(0, block_count, visit_block, initial)


def general_body(queries, cache_keys, cache_values, block_mask, key_counts, out_weight):
    cycle_size = lax.axis_size("ctx")
    cycle_index = lax.axis_index("ctx")
    token_count, head_count, head_size = queries.shape
    segment = token_count // cycle_size
    query_blocks = queries.reshape(block_mask.shape[0], BLK, head_count, head_size)

    def per_block(block_item):
        rows_q, mask_row = block_item
        row_mask = jnp.broadcast_to(mask_row[None, :], (BLK, mask_row.shape[0]))
        return partial_rows(rows_q, row_mask, cache_keys, cache_values, key_counts)

    stacked = lax.map(per_block, (query_blocks, block_mask))
    run_state = tuple((part.reshape((token_count,) + part.shape[2:]) for part in stacked))
    bit_total = cycle_size.bit_length() - 1
    for bit_number in range(bit_total - 1, -1, -1):
        half_rows = run_state[1].shape[0] // 2
        upper_half = jnp.bitwise_and(jnp.right_shift(cycle_index, bit_number), 1)
        kept = tuple(
            (
                lax.dynamic_slice_in_dim(part, upper_half * half_rows, half_rows, 0)
                for part in run_state
            )
        )
        outgoing = tuple(
            (
                lax.dynamic_slice_in_dim(part, (1 - upper_half) * half_rows, half_rows, 0)
                for part in run_state
            )
        )
        received = partner_of((outgoing[0], outgoing[1], outgoing[2]), "ctx", bit_number)
        run_state = combine(kept, received)
    out_sum, top_score, weight_sum = run_state
    attended = (
        (out_sum / weight_sum[..., None])
        .astype(jnp.bfloat16)
        .reshape(segment, head_count * head_size)
    )
    partial_value = jnp.dot(
        lax.all_gather(attended, "ctx", axis=0, tiled=True),
        out_weight,
        preferred_element_type=jnp.float32,
    )
    return lax.psum_scatter(partial_value, "kv", scatter_dimension=0, tiled=True)


def body(queries, cache_keys, cache_values, block_mask, key_counts, out_weight):
    devices = lax.axis_size("ctx")
    token_count, head_count, d = queries.shape
    kv_count = cache_keys.shape[1]
    group_size = head_count // kv_count
    suits = (
        lax.axis_size("kv") == 1
        and devices == 32
        and token_count == BLK
        and block_mask.shape[0] == 1
        and kv_count == 4
        and d == LANES
        and group_size == 16
        and token_count * group_size == LANES * (devices // 2)
    )
    run = fast_body if suits else general_body
    return run(queries, cache_keys, cache_values, block_mask, key_counts, out_weight)


def solution(mesh):
    placed = (
        P("groups", "kv", None),
        P(("groups", "ctx"), "kv", None),
        P(("groups", "ctx"), "kv", None),
        P("groups", "ctx"),
        P(("groups", "ctx")),
        P("kv", "ctx"),
    )
    return jax.shard_map(
        body, mesh=mesh, in_specs=placed, out_specs=P(("groups", "kv"), "ctx"), check_vma=False
    )
```

```python
import functools
import math

import jax
import jax.numpy as jnp
from jax import lax
from jax.experimental import pallas as pl
from jax.experimental.pallas import tpu as pltpu
from jax.sharding import PartitionSpec as P

BLK = 128
LANES = 128
STAT = 8
very_low = -1e30
lowest_top = -(2.0**99)
bf16 = jnp.bfloat16
f32 = jnp.float32


def pack_state(out, top, total):
    high = total.astype(bf16).astype(f32)
    low = total - high
    row = lax.broadcasted_iota(jnp.int32, (STAT, LANES), 0)
    stats = jnp.where(row == 0, top, jnp.where(row == 1, high, jnp.where(row == 2, low, 0.0)))
    return out.astype(bf16), stats.astype(bf16)


def active_count(meta):
    block_count = (meta.shape[0] - 2) // 2
    return sum((meta[2 + block] > 0).astype(jnp.int32) for block in range(block_count))


def split_kernel(meta, k_hbm, v_hbm, q_hbm, kd, vt, sent_ref, *scratch):
    listed, kept_counts, q_ref, k_ref, v_ref, spread, sems = scratch
    d = k_hbm.shape[1]
    kv_count = kd.shape[0]
    group_size = q_ref.shape[1]
    block_count = (meta.shape[0] - 2) // 2
    group = 1 - meta[0]

    heads = pl.ds(pl.multiple_of(group * group_size, group_size), group_size)
    copies = [
        pltpu.make_async_copy(k_hbm, k_ref, sems.at[0]),
        pltpu.make_async_copy(v_hbm, v_ref, sems.at[1]),
        pltpu.make_async_copy(q_hbm.at[:, heads, :], q_ref, sems.at[2]),
    ]
    for copy in copies:
        copy.start()

    def note(block, found):
        listed[found] = block
        kept_counts[found] = meta[2 + block_count + block]
        return found + (meta[2 + block] > 0).astype(jnp.int32)

    active = lax.fori_loop(0, block_count, note, jnp.int32(0))
    place = lax.broadcasted_iota(jnp.int32, (BLK, LANES), 0)
    across = lax.broadcasted_iota(jnp.int32, (STAT, LANES), 1)

    def split(source, position):
        start = pl.multiple_of(listed[position] * (BLK * kv_count), BLK * kv_count)
        spread[...] = source[pl.ds(start, BLK * kv_count), :].astype(f32)
        return [spread[pl.ds(g, BLK, stride=kv_count), :] for g in range(kv_count)]

    def fetch_keys(position, carry):
        at = pl.ds(pl.multiple_of(position * BLK, BLK), BLK)
        valid = place < kept_counts[position]
        for g, key in enumerate(split(k_ref, position)):
            kd[g, at, :] = jnp.where(valid, key, key[0:1]).astype(bf16)
        return carry

    def fetch_values(position, carry):
        at = pl.ds(pl.multiple_of(position * BLK, BLK), BLK)
        count = kept_counts[position]
        for g, value in enumerate(split(v_ref, position)):
            vt[g, 0:d, at] = jnp.where(place < count, value, 0.0).T.astype(bf16)
            vt[g, d:, at] = (across < count).astype(f32).astype(bf16)
        return carry

    copies[0].wait()
    lax.fori_loop(0, active, fetch_keys, 0)
    copies[1].wait()
    lax.fori_loop(0, active, fetch_values, 0)

    @pl.when(active % 2 == 1)
    def _():
        at = pl.ds(pl.multiple_of(active * BLK, BLK), BLK)
        before = pl.ds(pl.multiple_of((active - 1) * BLK, BLK), BLK)
        for g in range(kv_count):
            kd[g, at, :] = kd[g, before, :]
            vt[g, :, at] = jnp.zeros((d + STAT, BLK), bf16)

    copies[2].wait()
    attend_all(active, [(sent_ref, group, lambda: q_ref[...])], kd, vt)


def attention_kernel(chunk_roles, meta, kd, vt, q_ref, *outs):
    group_size = q_ref.shape[1] // kd.shape[0]
    todo = []
    for out, (chunk, is_other) in zip(outs, chunk_roles):
        group = 2 * chunk + (1 - meta[0] if is_other else meta[0])

        def read(group=group):
            heads = pl.ds(pl.multiple_of(group * group_size, group_size), group_size)
            return q_ref[:, heads, :]

        todo.append((out, group, read))
    attend_all(active_count(meta), todo, kd, vt)


def attend_all(active, todo, kd, vt):
    d = kd.shape[2]
    scale2 = math.log2(math.e) / math.sqrt(d)
    rows = todo[0][0].shape[0] * LANES
    pairs = (active + 1) // 2

    def attend(width, out, group, read):
        q = read().reshape(rows, d)
        scores = lax.dot_general(
            kd[group, 0:width, :], q, (((1,), (1,)), ((), ())), preferred_element_type=f32
        )
        top = (jnp.max(scores, axis=0, keepdims=True) * scale2).astype(bf16).astype(f32)
        weights = jnp.exp2(scores * scale2 - top).astype(bf16)
        sums = jnp.dot(vt[group, :, 0:width], weights, preferred_element_type=f32)
        total = sums[d:]
        high = total.astype(bf16).astype(f32)
        row = lax.broadcasted_iota(jnp.int32, (STAT, rows), 0)
        stats = jnp.where(row == 0, top, jnp.where(row == 1, high, total - high)).astype(bf16)
        value = sums[:d].astype(bf16)
        for piece in range(rows // LANES):
            at = slice(piece * LANES, (piece + 1) * LANES)
            out[piece, 0:d] = value[:, at]
            out[piece, d:] = stats[:, at]

    for n in range(1, kd.shape[1] // (2 * BLK) + 1):

        @pl.when(pairs == n)
        def _(n=n):
            for out, group, read in todo:
                attend(2 * BLK * n, out, group, read)

    @pl.when(pairs == 0)
    def _():
        row = lax.broadcasted_iota(jnp.int32, (d + STAT, LANES), 0)
        empty = jnp.where(row == d, lowest_top, 0.0).astype(bf16)
        for out, _, _ in todo:
            for piece in range(rows // LANES):
                out[piece] = empty


def merged(parts, d):
    stats = [part[d : d + STAT, :].astype(f32) for part in parts]
    tops = [stat[0:1] for stat in stats]
    top = functools.reduce(jnp.maximum, tops)
    out, total = 0.0, 0.0
    for part, stat, one in zip(parts, stats, tops):
        factor = jnp.exp2(one - top)
        out = out + part[0:d, :].astype(f32) * factor
        total = total + (stat[1:2] + stat[2:3]) * factor
    return out, top, total


def store_merged(ref, z, parts):
    d = ref.shape[1] - STAT
    out, stats = pack_state(*merged(parts, d))
    ref[z, 0:d, :] = out
    ref[z, d : d + STAT, :] = stats


def plane_chips(meta):
    core, my_xy = meta[0], meta[1]
    return [my_xy, my_xy ^ (1 + core), my_xy ^ (2 - core), my_xy ^ 3]


def core_kernel(z_size, choice, meta, kept, received, *outs):
    chips = plane_chips(meta)
    for chosen, out in zip(choice, outs):
        for i, number in enumerate(chosen):
            for z in range(z_size):
                piece = chips[number] * z_size + z
                store_merged(out, i * z_size + z, [kept[piece], received[piece]])


def half_kernel(kept, received, kept_out, sent_out):
    size = kept_out.shape[0]
    for out, first in ((sent_out, size), (kept_out, 0)):
        for i in range(size):
            store_merged(out, i, [kept[first + i], received[first + i]])


def plane_kernel(*refs):
    ins, out = refs[:-1], refs[-1]
    for z in range(out.shape[0]):
        store_merged(out, z, [ref[z] for ref in ins])


def last_kernel(*refs):
    ins, out_ref, turned = refs[:-2], refs[-2], refs[-1]
    d = ins[0].shape[1] - STAT
    tokens = out_ref.shape[1]
    heads = LANES // tokens
    for z in range(out_ref.shape[0]):
        out, _, total = merged([ref[z] for ref in ins], d)
        turned[z] = (out / total).T
        for h in range(heads):
            picked = turned[z, pl.ds(h, tokens, stride=heads), :]
            out_ref[z, :, h * d : (h + 1) * d] = picked.astype(bf16)


def project_kernel(terms, has_earlier, last, meta, weight, *refs):
    z_size, tokens, depth = refs[0].shape
    total = refs[4 * len(terms)][...] if has_earlier else None
    out_ref = refs[-1]
    for i, (chunk, is_other) in enumerate(terms):
        left = jnp.concatenate(
            [part[...].reshape(z_size * tokens, depth) for part in refs[4 * i : 4 * i + 4]], axis=0
        )
        group = 2 * chunk + (1 - meta[0] if is_other else meta[0])
        at = pl.ds(pl.multiple_of(group * depth, depth), depth)
        product = jnp.dot(left, weight[at, :], preferred_element_type=f32)
        total = product if total is None else total + product
    if not last:
        out_ref[...] = total
        return
    size = z_size * tokens
    for j, chip in enumerate(plane_chips(meta)):
        to = pl.ds(pl.multiple_of(chip * size, size), size)
        out_ref[to, :] = total[j * size : (j + 1) * size]


def hop(value, mask):
    pairs = [(source, source ^ mask) for source in range(lax.axis_size("ctx"))]
    return lax.ppermute(value, "ctx", pairs)


def plane_hop(value, number):
    masks = {1: (2, 4), 2: (4, 2), 3: (6, 6)}[number]
    pairs = [(source, source ^ masks[source % 2]) for source in range(lax.axis_size("ctx"))]
    return lax.ppermute(value, "ctx", pairs)


def line_hop(value, reach, z_size):
    masks = (8 * reach, 4 * z_size // reach)
    pairs = [(source, source ^ masks[source % 2]) for source in range(lax.axis_size("ctx"))]
    return lax.ppermute(value, "ctx", pairs)


VMEM = pl.BlockSpec(memory_space=pltpu.VMEM)
SMEM = pl.BlockSpec(memory_space=pltpu.SMEM)
HBM = pl.BlockSpec(memory_space=pltpu.HBM)
SMALL = pltpu.CompilerParams(vmem_limit_bytes=4 << 20)


def fast_body(queries, cache_keys, cache_values, block_mask, key_counts, out_weight):
    index = lax.axis_index("ctx")
    z_size = lax.axis_size("ctx") // 8
    token_count, head_count, d = queries.shape
    kv_count = cache_keys.shape[1]
    group_size = head_count // kv_count
    rows = token_count * group_size
    pieces = rows // LANES
    positions = cache_keys.shape[0]
    features = out_weight.shape[1]
    core = index & 1
    my_xy = (index >> 1) & 3
    tall = d + STAT
    keys = cache_keys.reshape(positions * kv_count, d)
    values = cache_values.reshape(positions * kv_count, d)
    place = jnp.concatenate(
        [jnp.stack([core, my_xy]).astype(jnp.int32), block_mask[0], key_counts]
    )
    kept_in_hbm = functools.partial(pltpu.with_memory_space_constraint, memory_space=pltpu.HBM)
    state = jax.ShapeDtypeStruct((z_size, tall, LANES), bf16)

    partial = jax.ShapeDtypeStruct((pieces, tall, LANES), bf16)
    blocks = positions // BLK

    def split_and_attend():
        return pl.pallas_call(
            split_kernel,
            in_specs=[SMEM] + [HBM] * 3,
            out_specs=[VMEM] * 3,
            scratch_shapes=[
                pltpu.SMEM((blocks + 1,), jnp.int32),
                pltpu.SMEM((blocks + 1,), jnp.int32),
                pltpu.VMEM((token_count, group_size, d), bf16),
                pltpu.VMEM((positions * kv_count, d), bf16),
                pltpu.VMEM((positions * kv_count, d), bf16),
                pltpu.VMEM((BLK * kv_count, d), f32),
                pltpu.SemaphoreType.DMA((3,)),
            ],
            out_shape=[
                jax.ShapeDtypeStruct((kv_count, positions, d), bf16),
                jax.ShapeDtypeStruct((kv_count, tall, positions), bf16),
                partial,
            ],
            compiler_params=pltpu.CompilerParams(vmem_limit_bytes=32 << 20),
            cost_estimate=pl.CostEstimate(
                flops=4 * rows * positions * d,
                transcendentals=rows * positions,
                bytes_accessed=4 * positions * d * kv_count,
            ),
            name="split_and_attend",
        )(place, kept_in_hbm(keys), kept_in_hbm(values), kept_in_hbm(queries))

    def attend(chunk_roles, kd, vt):
        count = len(chunk_roles)
        return pl.pallas_call(
            functools.partial(attention_kernel, chunk_roles),
            in_specs=[SMEM] + [VMEM] * 3,
            out_specs=[VMEM] * count,
            out_shape=[partial] * count,
            compiler_params=pltpu.CompilerParams(vmem_limit_bytes=32 << 20),
            cost_estimate=pl.CostEstimate(
                flops=4 * count * rows * positions * d,
                transcendentals=count * rows * positions,
                bytes_accessed=4 * positions * d * count,
            ),
            name="attend",
        )(place, kd, vt, queries)

    def merge_cores(kept, received, choice):
        return pl.pallas_call(
            functools.partial(core_kernel, z_size, choice),
            in_specs=[SMEM] + [VMEM] * 2,
            out_specs=[VMEM] * len(choice),
            out_shape=[
                jax.ShapeDtypeStruct((len(chosen) * z_size, tall, LANES), bf16)
                for chosen in choice
            ],
            compiler_params=SMALL,
            name="merge_cores",
        )(place, kept, received)

    def merge_half(kept, received):
        return pl.pallas_call(
            half_kernel,
            in_specs=[VMEM] * 2,
            out_specs=[VMEM] * 2,
            out_shape=[state] * 2,
            compiler_params=SMALL,
            name="merge_half",
        )(kept, received)

    def merge_chips(parts):
        return pl.pallas_call(
            plane_kernel,
            in_specs=[VMEM] * len(parts),
            out_specs=VMEM,
            out_shape=state,
            compiler_params=SMALL,
            name="merge_chips",
        )(*parts)

    def finish(parts):
        tokens = LANES // group_size
        return pl.pallas_call(
            last_kernel,
            in_specs=[VMEM] * len(parts),
            out_specs=VMEM,
            out_shape=jax.ShapeDtypeStruct((z_size, tokens, group_size * d), bf16),
            scratch_shapes=[pltpu.VMEM((z_size, LANES, d), f32)],
            compiler_params=SMALL,
            name="finish",
        )(*parts)

    def project(terms, parts, earlier, last=False):
        depth = group_size * d
        more = [] if earlier is None else [earlier]
        return pl.pallas_call(
            functools.partial(project_kernel, terms, bool(more), last),
            in_specs=[SMEM] + [VMEM] * (1 + len(parts) + len(more)),
            out_specs=VMEM,
            out_shape=jax.ShapeDtypeStruct((token_count, features), f32),
            compiler_params=pltpu.CompilerParams(vmem_limit_bytes=8 << 20),
            cost_estimate=pl.CostEstimate(
                flops=2 * len(terms) * token_count * depth * features,
                transcendentals=0,
                bytes_accessed=2 * len(terms) * depth * features,
            ),
            name="project",
        )(place, out_weight, *parts, *more)

    def exchange_plane(parts):
        return [parts[0]] + [plane_hop(parts[j], j) for j in (1, 2, 3)]

    def exchange_line(parts):
        part = merge_chips(parts)
        reach = 1
        while 2 * reach < z_size:
            part = merge_chips([part, line_hop(part, reach, z_size)])
            reach *= 2
        return finish([part, line_hop(part, reach, z_size)])

    def gather_plane(attended):
        first, second = plane_hop(attended, 1), plane_hop(attended, 2)
        return [attended, first, second, plane_hop(first, 2)]

    kd, vt, sent = split_and_attend()
    received = hop(sent, 1)
    kept, sent = attend([(0, False), (1, True)], kd, vt)
    next_received = hop(sent, 1)
    half, sent = merge_cores(kept, received, ((0, 2), (1, 3)))
    sent, kd = lax.optimization_barrier((sent, kd))
    received = plane_hop(sent, 1)
    (kept,) = attend([(1, False)], kd, vt)
    kept, half = lax.optimization_barrier((kept, half))
    first = merge_half(half, received)
    parts = merge_cores(kept, next_received, ((0,), (1,), (2,), (3,)))
    parts, first = lax.optimization_barrier((parts, first))
    first = [first[0], plane_hop(first[1], 2)]
    second = exchange_plane(parts)
    own = gather_plane(exchange_line(first))
    next_own = gather_plane(exchange_line(second))
    other = [hop(own[j], 1) for j in (0, 2, 1, 3)]
    total = project([(0, False), (0, True)], own + other, None)
    next_own[3], total = lax.optimization_barrier((next_own[3], total))
    next_other = [hop(next_own[j], 1) for j in (0, 2, 1, 3)]
    total = project([(1, False)], next_own, total)
    return project([(1, True)], next_other, total, last=True)


def partner_of(value, axis, distance):
    mask = 2**distance
    pairs = [(source, source ^ mask) for source in range(lax.axis_size(axis))]
    return lax.ppermute(value, axis, pairs)


def combine(earlier, later):
    out_one, top_one, sum_one = earlier
    out_two, top_two, sum_two = later
    new_top = jnp.maximum(top_one, top_two)
    factor_one = jnp.exp(top_one - new_top)
    factor_two = jnp.exp(top_two - new_top)
    new_out = out_one * factor_one[..., None] + out_two * factor_two[..., None]
    return (new_out, new_top, sum_one * factor_one + sum_two * factor_two)


def keep_state(key_block, run_state):
    return run_state


def partial_rows(rows_q, row_mask, cache_keys, cache_values, key_counts):
    row_count, head_count, head_size = rows_q.shape
    kv_count = cache_keys.shape[1]
    group_size = head_count // kv_count
    grouped = rows_q.reshape(row_count, kv_count, group_size, head_size)
    block_count = cache_keys.shape[0] // BLK
    score_scale = 1.0 / math.sqrt(head_size)
    offsets = jnp.arange(BLK, dtype=jnp.int32)

    def update(key_block, run_state):
        out_sum, top_score, weight_sum = run_state
        key_part = lax.dynamic_slice_in_dim(cache_keys, key_block * BLK, BLK, 0)
        value_part = lax.dynamic_slice_in_dim(cache_values, key_block * BLK, BLK, 0)
        scores = (
            jnp.einsum("rgqd,kgd->rgqk", grouped, key_part, preferred_element_type=jnp.float32)
            * score_scale
        )
        active_rows = lax.dynamic_slice_in_dim(row_mask, key_block, 1, 1)[:, 0] > 0
        valid_count = lax.dynamic_slice_in_dim(key_counts, key_block, 1, 0)[0]
        valid = active_rows[:, None, None, None] & (offsets < valid_count)[None, None, None, :]
        scores = jnp.where(valid, scores, very_low)
        new_top = jnp.maximum(top_score, jnp.max(scores, axis=-1))
        weights = jnp.where(valid, jnp.exp(scores - new_top[..., None]), 0.0)
        factor = jnp.exp(top_score - new_top)
        new_sum = weight_sum * factor + jnp.sum(weights, axis=-1)
        new_out = out_sum * factor[..., None] + jnp.einsum(
            "rgqk,kgd->rgqd",
            weights.astype(jnp.bfloat16),
            value_part,
            preferred_element_type=jnp.float32,
        )
        return (new_out, new_top, new_sum)

    def visit_block(key_block, run_state):
        active = jnp.any(lax.dynamic_slice_in_dim(row_mask, key_block, 1, 1) > 0)
        return lax.cond(active, update, keep_state, key_block, run_state)

    initial = (
        jnp.zeros((row_count, kv_count, group_size, head_size), jnp.float32),
        jnp.full((row_count, kv_count, group_size), very_low, jnp.float32),
        jnp.zeros((row_count, kv_count, group_size), jnp.float32),
    )
    return lax.fori_loop(0, block_count, visit_block, initial)


def general_body(queries, cache_keys, cache_values, block_mask, key_counts, out_weight):
    cycle_size = lax.axis_size("ctx")
    cycle_index = lax.axis_index("ctx")
    token_count, head_count, head_size = queries.shape
    segment = token_count // cycle_size
    query_blocks = queries.reshape(block_mask.shape[0], BLK, head_count, head_size)

    def per_block(block_item):
        rows_q, mask_row = block_item
        row_mask = jnp.broadcast_to(mask_row[None, :], (BLK, mask_row.shape[0]))
        return partial_rows(rows_q, row_mask, cache_keys, cache_values, key_counts)

    stacked = lax.map(per_block, (query_blocks, block_mask))
    run_state = tuple((part.reshape((token_count,) + part.shape[2:]) for part in stacked))
    bit_total = cycle_size.bit_length() - 1
    for bit_number in range(bit_total - 1, -1, -1):
        half_rows = run_state[1].shape[0] // 2
        upper_half = jnp.bitwise_and(jnp.right_shift(cycle_index, bit_number), 1)
        kept = tuple(
            (
                lax.dynamic_slice_in_dim(part, upper_half * half_rows, half_rows, 0)
                for part in run_state
            )
        )
        outgoing = tuple(
            (
                lax.dynamic_slice_in_dim(part, (1 - upper_half) * half_rows, half_rows, 0)
                for part in run_state
            )
        )
        received = partner_of((outgoing[0], outgoing[1], outgoing[2]), "ctx", bit_number)
        run_state = combine(kept, received)
    out_sum, top_score, weight_sum = run_state
    attended = (
        (out_sum / weight_sum[..., None])
        .astype(jnp.bfloat16)
        .reshape(segment, head_count * head_size)
    )
    partial_value = jnp.dot(
        lax.all_gather(attended, "ctx", axis=0, tiled=True),
        out_weight,
        preferred_element_type=jnp.float32,
    )
    return lax.psum_scatter(partial_value, "kv", scatter_dimension=0, tiled=True)


def body(queries, cache_keys, cache_values, block_mask, key_counts, out_weight):
    devices = lax.axis_size("ctx")
    token_count, head_count, d = queries.shape
    kv_count = cache_keys.shape[1]
    group_size = head_count // kv_count
    suits = (
        lax.axis_size("kv") == 1
        and devices == 32
        and token_count == BLK
        and block_mask.shape[0] == 1
        and kv_count == 4
        and d == LANES
        and group_size == 16
        and token_count * group_size == LANES * (devices // 2)
    )
    run = fast_body if suits else general_body
    return run(queries, cache_keys, cache_values, block_mask, key_counts, out_weight)


def solution(mesh):
    placed = (
        P("groups", "kv", None),
        P(("groups", "ctx"), "kv", None),
        P(("groups", "ctx"), "kv", None),
        P("groups", "ctx"),
        P(("groups", "ctx")),
        P("kv", "ctx"),
    )
    return jax.shard_map(
        body, mesh=mesh, in_specs=placed, out_specs=P(("groups", "kv"), "ctx"), check_vma=False
    )
```

```python
import functools
import math

import jax
import jax.numpy as jnp
from jax import lax
from jax.experimental import pallas as pl
from jax.experimental.pallas import tpu as pltpu
from jax.sharding import PartitionSpec as P

BLK = 128
LANES = 128
STAT = 8
very_low = -1e30
lowest_top = -(2.0**99)
bf16 = jnp.bfloat16
f32 = jnp.float32


def pack_state(out, top, total):
    high = total.astype(bf16).astype(f32)
    low = total - high
    row = lax.broadcasted_iota(jnp.int32, (STAT, LANES), 0)
    stats = jnp.where(row == 0, top, jnp.where(row == 1, high, jnp.where(row == 2, low, 0.0)))
    return out.astype(bf16), stats.astype(bf16)


def active_count(meta):
    block_count = (meta.shape[0] - 2) // 2
    return sum((meta[2 + block] > 0).astype(jnp.int32) for block in range(block_count))


def split_kernel(meta, k_hbm, v_hbm, q_hbm, kd, vt, sent_ref, *scratch):
    listed, kept_counts, q_ref, k_ref, v_ref, spread, sems = scratch
    d = k_hbm.shape[1]
    kv_count = kd.shape[0]
    group_size = q_ref.shape[1]
    block_count = (meta.shape[0] - 2) // 2
    group = 1 - meta[0]

    heads = pl.ds(pl.multiple_of(group * group_size, group_size), group_size)
    copies = [
        pltpu.make_async_copy(k_hbm, k_ref, sems.at[0]),
        pltpu.make_async_copy(v_hbm, v_ref, sems.at[1]),
        pltpu.make_async_copy(q_hbm.at[:, heads, :], q_ref, sems.at[2]),
    ]
    for copy in copies:
        copy.start()

    def note(block, found):
        listed[found] = block
        kept_counts[found] = meta[2 + block_count + block]
        return found + (meta[2 + block] > 0).astype(jnp.int32)

    active = lax.fori_loop(0, block_count, note, jnp.int32(0))
    place = lax.broadcasted_iota(jnp.int32, (BLK, LANES), 0)
    across = lax.broadcasted_iota(jnp.int32, (STAT, LANES), 1)

    def split(source, position):
        start = pl.multiple_of(listed[position] * (BLK * kv_count), BLK * kv_count)
        spread[...] = source[pl.ds(start, BLK * kv_count), :].astype(f32)
        return [spread[pl.ds(g, BLK, stride=kv_count), :] for g in range(kv_count)]

    def fetch_keys(position, carry):
        at = pl.ds(pl.multiple_of(position * BLK, BLK), BLK)
        valid = place < kept_counts[position]
        for g, key in enumerate(split(k_ref, position)):
            kd[g, at, :] = jnp.where(valid, key, key[0:1]).astype(bf16)
        return carry

    def fetch_values(position, carry):
        at = pl.ds(pl.multiple_of(position * BLK, BLK), BLK)
        count = kept_counts[position]
        for g, value in enumerate(split(v_ref, position)):
            vt[g, 0:d, at] = jnp.where(place < count, value, 0.0).T.astype(bf16)
            vt[g, d:, at] = (across < count).astype(f32).astype(bf16)
        return carry

    copies[0].wait()
    lax.fori_loop(0, active, fetch_keys, 0)
    copies[1].wait()
    lax.fori_loop(0, active, fetch_values, 0)

    @pl.when(active % 2 == 1)
    def _():
        at = pl.ds(pl.multiple_of(active * BLK, BLK), BLK)
        before = pl.ds(pl.multiple_of((active - 1) * BLK, BLK), BLK)
        for g in range(kv_count):
            kd[g, at, :] = kd[g, before, :]
            vt[g, :, at] = jnp.zeros((d + STAT, BLK), bf16)

    copies[2].wait()
    attend_all(active, [(sent_ref, group, lambda: q_ref[...])], kd, vt)


def attention_kernel(chunk_roles, meta, kd, vt, q_ref, *outs):
    group_size = q_ref.shape[1] // kd.shape[0]
    todo = []
    for out, (chunk, is_other) in zip(outs, chunk_roles):
        group = 2 * chunk + (1 - meta[0] if is_other else meta[0])

        def read(group=group):
            heads = pl.ds(pl.multiple_of(group * group_size, group_size), group_size)
            return q_ref[:, heads, :]

        todo.append((out, group, read))
    attend_all(active_count(meta), todo, kd, vt)


def attend_all(active, todo, kd, vt):
    d = kd.shape[2]
    scale2 = math.log2(math.e) / math.sqrt(d)
    rows = todo[0][0].shape[0] * LANES
    pairs = (active + 1) // 2

    def attend(width, out, group, read):
        q = read().reshape(rows, d)
        scores = lax.dot_general(
            kd[group, 0:width, :], q, (((1,), (1,)), ((), ())), preferred_element_type=f32
        )
        top = (jnp.max(scores, axis=0, keepdims=True) * scale2).astype(bf16).astype(f32)
        weights = jnp.exp2(scores * scale2 - top).astype(bf16)
        sums = jnp.dot(vt[group, :, 0:width], weights, preferred_element_type=f32)
        total = sums[d:]
        high = total.astype(bf16).astype(f32)
        row = lax.broadcasted_iota(jnp.int32, (STAT, rows), 0)
        stats = jnp.where(row == 0, top, jnp.where(row == 1, high, total - high)).astype(bf16)
        value = sums[:d].astype(bf16)
        for piece in range(rows // LANES):
            at = slice(piece * LANES, (piece + 1) * LANES)
            out[piece, 0:d] = value[:, at]
            out[piece, d:] = stats[:, at]

    for n in range(1, kd.shape[1] // (2 * BLK) + 1):

        @pl.when(pairs == n)
        def _(n=n):
            for out, group, read in todo:
                attend(2 * BLK * n, out, group, read)

    @pl.when(pairs == 0)
    def _():
        row = lax.broadcasted_iota(jnp.int32, (d + STAT, LANES), 0)
        empty = jnp.where(row == d, lowest_top, 0.0).astype(bf16)
        for out, _, _ in todo:
            for piece in range(rows // LANES):
                out[piece] = empty


def merged(parts, d):
    stats = [part[d : d + STAT, :].astype(f32) for part in parts]
    tops = [stat[0:1] for stat in stats]
    top = functools.reduce(jnp.maximum, tops)
    out, total = 0.0, 0.0
    for part, stat, one in zip(parts, stats, tops):
        factor = jnp.exp2(one - top)
        out = out + part[0:d, :].astype(f32) * factor
        total = total + (stat[1:2] + stat[2:3]) * factor
    return out, top, total


def store_merged(ref, z, parts):
    d = ref.shape[1] - STAT
    out, stats = pack_state(*merged(parts, d))
    ref[z, 0:d, :] = out
    ref[z, d : d + STAT, :] = stats


def plane_chips(meta):
    core, my_xy = meta[0], meta[1]
    return [my_xy, my_xy ^ (1 + core), my_xy ^ (2 - core), my_xy ^ 3]


def core_kernel(meta, kept, received, *outs):
    z_size = outs[0].shape[0]
    for chip, out in zip(plane_chips(meta), outs):
        for z in range(z_size):
            piece = chip * z_size + z
            store_merged(out, z, [kept[piece], received[piece]])


def plane_kernel(*refs):
    ins, out = refs[:-1], refs[-1]
    for z in range(out.shape[0]):
        store_merged(out, z, [ref[z] for ref in ins])


def last_kernel(*refs):
    ins, out_ref, turned = refs[:-2], refs[-2], refs[-1]
    d = ins[0].shape[1] - STAT
    tokens = out_ref.shape[1]
    heads = LANES // tokens
    for z in range(out_ref.shape[0]):
        out, _, total = merged([ref[z] for ref in ins], d)
        turned[z] = (out / total).T
        for h in range(heads):
            picked = turned[z, pl.ds(h, tokens, stride=heads), :]
            out_ref[z, :, h * d : (h + 1) * d] = picked.astype(bf16)


def project_kernel(terms, has_earlier, last, meta, weight, *refs):
    z_size, tokens, depth = refs[0].shape
    total = refs[4 * len(terms)][...] if has_earlier else None
    out_ref = refs[-1]
    for i, (chunk, is_other) in enumerate(terms):
        left = jnp.concatenate(
            [part[...].reshape(z_size * tokens, depth) for part in refs[4 * i : 4 * i + 4]], axis=0
        )
        group = 2 * chunk + (1 - meta[0] if is_other else meta[0])
        at = pl.ds(pl.multiple_of(group * depth, depth), depth)
        product = jnp.dot(left, weight[at, :], preferred_element_type=f32)
        total = product if total is None else total + product
    if not last:
        out_ref[...] = total
        return
    size = z_size * tokens
    for j, chip in enumerate(plane_chips(meta)):
        to = pl.ds(pl.multiple_of(chip * size, size), size)
        out_ref[to, :] = total[j * size : (j + 1) * size]


def hop(value, mask):
    pairs = [(source, source ^ mask) for source in range(lax.axis_size("ctx"))]
    return lax.ppermute(value, "ctx", pairs)


def plane_hop(value, number):
    masks = {1: (2, 4), 2: (4, 2), 3: (6, 6)}[number]
    pairs = [(source, source ^ masks[source % 2]) for source in range(lax.axis_size("ctx"))]
    return lax.ppermute(value, "ctx", pairs)


def line_hop(value, reach, z_size):
    masks = (8 * reach, 4 * z_size // reach)
    pairs = [(source, source ^ masks[source % 2]) for source in range(lax.axis_size("ctx"))]
    return lax.ppermute(value, "ctx", pairs)


VMEM = pl.BlockSpec(memory_space=pltpu.VMEM)
SMEM = pl.BlockSpec(memory_space=pltpu.SMEM)
HBM = pl.BlockSpec(memory_space=pltpu.HBM)
SMALL = pltpu.CompilerParams(vmem_limit_bytes=4 << 20)


def fast_body(queries, cache_keys, cache_values, block_mask, key_counts, out_weight):
    index = lax.axis_index("ctx")
    z_size = lax.axis_size("ctx") // 8
    token_count, head_count, d = queries.shape
    kv_count = cache_keys.shape[1]
    group_size = head_count // kv_count
    rows = token_count * group_size
    pieces = rows // LANES
    positions = cache_keys.shape[0]
    features = out_weight.shape[1]
    core = index & 1
    my_xy = (index >> 1) & 3
    tall = d + STAT
    keys = cache_keys.reshape(positions * kv_count, d)
    values = cache_values.reshape(positions * kv_count, d)
    place = jnp.concatenate(
        [jnp.stack([core, my_xy]).astype(jnp.int32), block_mask[0], key_counts]
    )
    kept_in_hbm = functools.partial(pltpu.with_memory_space_constraint, memory_space=pltpu.HBM)
    state = jax.ShapeDtypeStruct((z_size, tall, LANES), bf16)

    partial = jax.ShapeDtypeStruct((pieces, tall, LANES), bf16)
    blocks = positions // BLK

    def split_and_attend():
        return pl.pallas_call(
            split_kernel,
            in_specs=[SMEM] + [HBM] * 3,
            out_specs=[VMEM] * 3,
            scratch_shapes=[
                pltpu.SMEM((blocks + 1,), jnp.int32),
                pltpu.SMEM((blocks + 1,), jnp.int32),
                pltpu.VMEM((token_count, group_size, d), bf16),
                pltpu.VMEM((positions * kv_count, d), bf16),
                pltpu.VMEM((positions * kv_count, d), bf16),
                pltpu.VMEM((BLK * kv_count, d), f32),
                pltpu.SemaphoreType.DMA((3,)),
            ],
            out_shape=[
                jax.ShapeDtypeStruct((kv_count, positions, d), bf16),
                jax.ShapeDtypeStruct((kv_count, tall, positions), bf16),
                partial,
            ],
            compiler_params=pltpu.CompilerParams(vmem_limit_bytes=32 << 20),
            cost_estimate=pl.CostEstimate(
                flops=4 * rows * positions * d,
                transcendentals=rows * positions,
                bytes_accessed=4 * positions * d * kv_count,
            ),
            name="split_and_attend",
        )(place, kept_in_hbm(keys), kept_in_hbm(values), kept_in_hbm(queries))

    def attend(chunk_roles, kd, vt):
        count = len(chunk_roles)
        return pl.pallas_call(
            functools.partial(attention_kernel, chunk_roles),
            in_specs=[SMEM] + [VMEM] * 3,
            out_specs=[VMEM] * count,
            out_shape=[partial] * count,
            compiler_params=pltpu.CompilerParams(vmem_limit_bytes=32 << 20),
            cost_estimate=pl.CostEstimate(
                flops=4 * count * rows * positions * d,
                transcendentals=count * rows * positions,
                bytes_accessed=4 * positions * d * count,
            ),
            name="attend",
        )(place, kd, vt, queries)

    def merge_cores(kept, received):
        return pl.pallas_call(
            core_kernel,
            in_specs=[SMEM] + [VMEM] * 2,
            out_specs=[VMEM] * 4,
            out_shape=[state] * 4,
            compiler_params=SMALL,
            name="merge_cores",
        )(place, kept, received)

    def merge_chips(parts):
        return pl.pallas_call(
            plane_kernel,
            in_specs=[VMEM] * len(parts),
            out_specs=VMEM,
            out_shape=state,
            compiler_params=SMALL,
            name="merge_chips",
        )(*parts)

    def finish(parts):
        tokens = LANES // group_size
        return pl.pallas_call(
            last_kernel,
            in_specs=[VMEM] * len(parts),
            out_specs=VMEM,
            out_shape=jax.ShapeDtypeStruct((z_size, tokens, group_size * d), bf16),
            scratch_shapes=[pltpu.VMEM((z_size, LANES, d), f32)],
            compiler_params=SMALL,
            name="finish",
        )(*parts)

    def project(terms, parts, earlier, last=False):
        depth = group_size * d
        more = [] if earlier is None else [earlier]
        return pl.pallas_call(
            functools.partial(project_kernel, terms, bool(more), last),
            in_specs=[SMEM] + [VMEM] * (1 + len(parts) + len(more)),
            out_specs=VMEM,
            out_shape=jax.ShapeDtypeStruct((token_count, features), f32),
            compiler_params=pltpu.CompilerParams(vmem_limit_bytes=8 << 20),
            cost_estimate=pl.CostEstimate(
                flops=2 * len(terms) * token_count * depth * features,
                transcendentals=0,
                bytes_accessed=2 * len(terms) * depth * features,
            ),
            name="project",
        )(place, out_weight, *parts, *more)

    def exchange_plane(parts):
        return [parts[0]] + [plane_hop(parts[j], j) for j in (1, 2, 3)]

    def exchange_line(parts):
        part = merge_chips(parts)
        reach = 1
        while 2 * reach < z_size:
            part = merge_chips([part, line_hop(part, reach, z_size)])
            reach *= 2
        return finish([part, line_hop(part, reach, z_size)])

    def gather_plane(attended):
        first, second = plane_hop(attended, 1), plane_hop(attended, 2)
        return [attended, first, second, plane_hop(first, 2)]

    kd, vt, sent = split_and_attend()
    received = hop(sent, 1)
    kept, sent = attend([(0, False), (1, True)], kd, vt)
    next_received = hop(sent, 1)
    parts = merge_cores(kept, received)
    parts, kd = lax.optimization_barrier((parts, kd))
    first = exchange_plane(parts)
    (kept,) = attend([(1, False)], kd, vt)
    parts = merge_cores(kept, next_received)
    parts, first[0] = lax.optimization_barrier((parts, first[0]))
    second = exchange_plane(parts)
    own = gather_plane(exchange_line(first))
    other = [hop(own[j], 1) for j in (0, 2, 1, 3)]
    next_own = gather_plane(exchange_line(second))
    next_other = [hop(next_own[j], 1) for j in (0, 2, 1, 3)]
    total = project([(0, False), (0, True), (1, False)], own + other + next_own, None)
    return project([(1, True)], next_other, total, last=True)


def partner_of(value, axis, distance):
    mask = 2**distance
    pairs = [(source, source ^ mask) for source in range(lax.axis_size(axis))]
    return lax.ppermute(value, axis, pairs)


def combine(earlier, later):
    out_one, top_one, sum_one = earlier
    out_two, top_two, sum_two = later
    new_top = jnp.maximum(top_one, top_two)
    factor_one = jnp.exp(top_one - new_top)
    factor_two = jnp.exp(top_two - new_top)
    new_out = out_one * factor_one[..., None] + out_two * factor_two[..., None]
    return (new_out, new_top, sum_one * factor_one + sum_two * factor_two)


def keep_state(key_block, run_state):
    return run_state


def partial_rows(rows_q, row_mask, cache_keys, cache_values, key_counts):
    row_count, head_count, head_size = rows_q.shape
    kv_count = cache_keys.shape[1]
    group_size = head_count // kv_count
    grouped = rows_q.reshape(row_count, kv_count, group_size, head_size)
    block_count = cache_keys.shape[0] // BLK
    score_scale = 1.0 / math.sqrt(head_size)
    offsets = jnp.arange(BLK, dtype=jnp.int32)

    def update(key_block, run_state):
        out_sum, top_score, weight_sum = run_state
        key_part = lax.dynamic_slice_in_dim(cache_keys, key_block * BLK, BLK, 0)
        value_part = lax.dynamic_slice_in_dim(cache_values, key_block * BLK, BLK, 0)
        scores = (
            jnp.einsum("rgqd,kgd->rgqk", grouped, key_part, preferred_element_type=jnp.float32)
            * score_scale
        )
        active_rows = lax.dynamic_slice_in_dim(row_mask, key_block, 1, 1)[:, 0] > 0
        valid_count = lax.dynamic_slice_in_dim(key_counts, key_block, 1, 0)[0]
        valid = active_rows[:, None, None, None] & (offsets < valid_count)[None, None, None, :]
        scores = jnp.where(valid, scores, very_low)
        new_top = jnp.maximum(top_score, jnp.max(scores, axis=-1))
        weights = jnp.where(valid, jnp.exp(scores - new_top[..., None]), 0.0)
        factor = jnp.exp(top_score - new_top)
        new_sum = weight_sum * factor + jnp.sum(weights, axis=-1)
        new_out = out_sum * factor[..., None] + jnp.einsum(
            "rgqk,kgd->rgqd",
            weights.astype(jnp.bfloat16),
            value_part,
            preferred_element_type=jnp.float32,
        )
        return (new_out, new_top, new_sum)

    def visit_block(key_block, run_state):
        active = jnp.any(lax.dynamic_slice_in_dim(row_mask, key_block, 1, 1) > 0)
        return lax.cond(active, update, keep_state, key_block, run_state)

    initial = (
        jnp.zeros((row_count, kv_count, group_size, head_size), jnp.float32),
        jnp.full((row_count, kv_count, group_size), very_low, jnp.float32),
        jnp.zeros((row_count, kv_count, group_size), jnp.float32),
    )
    return lax.fori_loop(0, block_count, visit_block, initial)


def general_body(queries, cache_keys, cache_values, block_mask, key_counts, out_weight):
    cycle_size = lax.axis_size("ctx")
    cycle_index = lax.axis_index("ctx")
    token_count, head_count, head_size = queries.shape
    segment = token_count // cycle_size
    query_blocks = queries.reshape(block_mask.shape[0], BLK, head_count, head_size)

    def per_block(block_item):
        rows_q, mask_row = block_item
        row_mask = jnp.broadcast_to(mask_row[None, :], (BLK, mask_row.shape[0]))
        return partial_rows(rows_q, row_mask, cache_keys, cache_values, key_counts)

    stacked = lax.map(per_block, (query_blocks, block_mask))
    run_state = tuple((part.reshape((token_count,) + part.shape[2:]) for part in stacked))
    bit_total = cycle_size.bit_length() - 1
    for bit_number in range(bit_total - 1, -1, -1):
        half_rows = run_state[1].shape[0] // 2
        upper_half = jnp.bitwise_and(jnp.right_shift(cycle_index, bit_number), 1)
        kept = tuple(
            (
                lax.dynamic_slice_in_dim(part, upper_half * half_rows, half_rows, 0)
                for part in run_state
            )
        )
        outgoing = tuple(
            (
                lax.dynamic_slice_in_dim(part, (1 - upper_half) * half_rows, half_rows, 0)
                for part in run_state
            )
        )
        received = partner_of((outgoing[0], outgoing[1], outgoing[2]), "ctx", bit_number)
        run_state = combine(kept, received)
    out_sum, top_score, weight_sum = run_state
    attended = (
        (out_sum / weight_sum[..., None])
        .astype(jnp.bfloat16)
        .reshape(segment, head_count * head_size)
    )
    partial_value = jnp.dot(
        lax.all_gather(attended, "ctx", axis=0, tiled=True),
        out_weight,
        preferred_element_type=jnp.float32,
    )
    return lax.psum_scatter(partial_value, "kv", scatter_dimension=0, tiled=True)


def body(queries, cache_keys, cache_values, block_mask, key_counts, out_weight):
    devices = lax.axis_size("ctx")
    token_count, head_count, d = queries.shape
    kv_count = cache_keys.shape[1]
    group_size = head_count // kv_count
    suits = (
        lax.axis_size("kv") == 1
        and devices == 32
        and token_count == BLK
        and block_mask.shape[0] == 1
        and kv_count == 4
        and d == LANES
        and group_size == 16
        and token_count * group_size == LANES * (devices // 2)
    )
    run = fast_body if suits else general_body
    return run(queries, cache_keys, cache_values, block_mask, key_counts, out_weight)


def solution(mesh):
    placed = (
        P("groups", "kv", None),
        P(("groups", "ctx"), "kv", None),
        P(("groups", "ctx"), "kv", None),
        P("groups", "ctx"),
        P(("groups", "ctx")),
        P("kv", "ctx"),
    )
    return jax.shard_map(
        body, mesh=mesh, in_specs=placed, out_specs=P(("groups", "kv"), "ctx"), check_vma=False
    )
```

```python
import functools
import math

import jax
import jax.numpy as jnp
from jax import lax
from jax.experimental import pallas as pl
from jax.experimental.pallas import tpu as pltpu
from jax.sharding import PartitionSpec as P

BLK = 128
LANES = 128
STAT = 8
very_low = -1e30
lowest_top = -(2.0**99)
bf16 = jnp.bfloat16
f32 = jnp.float32


def pack_state(out, top, total):
    high = total.astype(bf16).astype(f32)
    low = total - high
    row = lax.broadcasted_iota(jnp.int32, (STAT, LANES), 0)
    stats = jnp.where(row == 0, top, jnp.where(row == 1, high, jnp.where(row == 2, low, 0.0)))
    return out.astype(bf16), stats.astype(bf16)


def active_count(meta):
    block_count = (meta.shape[0] - 2) // 2
    return sum((meta[2 + block] > 0).astype(jnp.int32) for block in range(block_count))


def split_kernel(meta, k_hbm, v_hbm, q_hbm, kd, vt, sent_ref, *scratch):
    listed, kept_counts, q_ref, k_ref, v_ref, spread, sems = scratch
    d = k_hbm.shape[1]
    kv_count = kd.shape[0]
    group_size = q_ref.shape[1]
    block_count = (meta.shape[0] - 2) // 2
    group = 1 - meta[0]

    heads = pl.ds(pl.multiple_of(group * group_size, group_size), group_size)
    copies = [
        pltpu.make_async_copy(k_hbm, k_ref, sems.at[0]),
        pltpu.make_async_copy(v_hbm, v_ref, sems.at[1]),
        pltpu.make_async_copy(q_hbm.at[:, heads, :], q_ref, sems.at[2]),
    ]
    for copy in copies:
        copy.start()

    def note(block, found):
        listed[found] = block
        kept_counts[found] = meta[2 + block_count + block]
        return found + (meta[2 + block] > 0).astype(jnp.int32)

    active = lax.fori_loop(0, block_count, note, jnp.int32(0))
    place = lax.broadcasted_iota(jnp.int32, (BLK, LANES), 0)
    across = lax.broadcasted_iota(jnp.int32, (STAT, LANES), 1)

    def split(source, position):
        start = pl.multiple_of(listed[position] * (BLK * kv_count), BLK * kv_count)
        spread[...] = source[pl.ds(start, BLK * kv_count), :].astype(f32)
        return [spread[pl.ds(g, BLK, stride=kv_count), :] for g in range(kv_count)]

    def fetch_keys(position, carry):
        at = pl.ds(pl.multiple_of(position * BLK, BLK), BLK)
        valid = place < kept_counts[position]
        for g, key in enumerate(split(k_ref, position)):
            kd[g, at, :] = jnp.where(valid, key, key[0:1]).astype(bf16)
        return carry

    def fetch_values(position, carry):
        at = pl.ds(pl.multiple_of(position * BLK, BLK), BLK)
        count = kept_counts[position]
        for g, value in enumerate(split(v_ref, position)):
            vt[g, 0:d, at] = jnp.where(place < count, value, 0.0).T.astype(bf16)
            vt[g, d:, at] = (across < count).astype(f32).astype(bf16)
        return carry

    copies[0].wait()
    lax.fori_loop(0, active, fetch_keys, 0)
    copies[1].wait()
    lax.fori_loop(0, active, fetch_values, 0)

    @pl.when(active % 2 == 1)
    def _():
        at = pl.ds(pl.multiple_of(active * BLK, BLK), BLK)
        before = pl.ds(pl.multiple_of((active - 1) * BLK, BLK), BLK)
        for g in range(kv_count):
            kd[g, at, :] = kd[g, before, :]
            vt[g, :, at] = jnp.zeros((d + STAT, BLK), bf16)

    copies[2].wait()
    attend_all(active, [(sent_ref, group, lambda: q_ref[...])], kd, vt)


def attention_kernel(chunk_roles, meta, kd, vt, q_ref, *outs):
    group_size = q_ref.shape[1] // kd.shape[0]
    todo = []
    for out, (chunk, is_other) in zip(outs, chunk_roles):
        group = 2 * chunk + (1 - meta[0] if is_other else meta[0])

        def read(group=group):
            heads = pl.ds(pl.multiple_of(group * group_size, group_size), group_size)
            return q_ref[:, heads, :]

        todo.append((out, group, read))
    attend_all(active_count(meta), todo, kd, vt)


def attend_all(active, todo, kd, vt):
    d = kd.shape[2]
    scale2 = math.log2(math.e) / math.sqrt(d)
    rows = todo[0][0].shape[0] * LANES
    pairs = (active + 1) // 2

    def attend(width, out, group, read):
        q = read().reshape(rows, d)
        scores = lax.dot_general(
            kd[group, 0:width, :], q, (((1,), (1,)), ((), ())), preferred_element_type=f32
        )
        top = (jnp.max(scores, axis=0, keepdims=True) * scale2).astype(bf16).astype(f32)
        weights = jnp.exp2(scores * scale2 - top).astype(bf16)
        sums = jnp.dot(vt[group, :, 0:width], weights, preferred_element_type=f32)
        total = sums[d:]
        high = total.astype(bf16).astype(f32)
        row = lax.broadcasted_iota(jnp.int32, (STAT, rows), 0)
        stats = jnp.where(row == 0, top, jnp.where(row == 1, high, total - high)).astype(bf16)
        value = sums[:d].astype(bf16)
        for piece in range(rows // LANES):
            at = slice(piece * LANES, (piece + 1) * LANES)
            out[piece, 0:d] = value[:, at]
            out[piece, d:] = stats[:, at]

    for n in range(1, kd.shape[1] // (2 * BLK) + 1):

        @pl.when(pairs == n)
        def _(n=n):
            for out, group, read in todo:
                attend(2 * BLK * n, out, group, read)

    @pl.when(pairs == 0)
    def _():
        row = lax.broadcasted_iota(jnp.int32, (d + STAT, LANES), 0)
        empty = jnp.where(row == d, lowest_top, 0.0).astype(bf16)
        for out, _, _ in todo:
            for piece in range(rows // LANES):
                out[piece] = empty


def merged(parts, d):
    stats = [part[d : d + STAT, :].astype(f32) for part in parts]
    tops = [stat[0:1] for stat in stats]
    top = functools.reduce(jnp.maximum, tops)
    out, total = 0.0, 0.0
    for part, stat, one in zip(parts, stats, tops):
        factor = jnp.exp2(one - top)
        out = out + part[0:d, :].astype(f32) * factor
        total = total + (stat[1:2] + stat[2:3]) * factor
    return out, top, total


def store_merged(ref, z, parts):
    d = ref.shape[1] - STAT
    out, stats = pack_state(*merged(parts, d))
    ref[z, 0:d, :] = out
    ref[z, d : d + STAT, :] = stats


def plane_chips(meta):
    core, my_xy = meta[0], meta[1]
    return [my_xy, my_xy ^ (1 + core), my_xy ^ (2 - core), my_xy ^ 3]


def core_kernel(meta, kept, received, *outs):
    z_size = outs[0].shape[0]
    for chip, out in zip(plane_chips(meta), outs):
        for z in range(z_size):
            piece = chip * z_size + z
            store_merged(out, z, [kept[piece], received[piece]])


def plane_kernel(*refs):
    ins, out = refs[:-1], refs[-1]
    for z in range(out.shape[0]):
        store_merged(out, z, [ref[z] for ref in ins])


def last_kernel(*refs):
    ins, out_ref, turned = refs[:-2], refs[-2], refs[-1]
    d = ins[0].shape[1] - STAT
    tokens = out_ref.shape[1]
    heads = LANES // tokens
    for z in range(out_ref.shape[0]):
        out, _, total = merged([ref[z] for ref in ins], d)
        turned[z] = (out / total).T
        for h in range(heads):
            picked = turned[z, pl.ds(h, tokens, stride=heads), :]
            out_ref[z, :, h * d : (h + 1) * d] = picked.astype(bf16)


def project_kernel(terms, has_earlier, last, meta, weight, *refs):
    z_size, tokens, depth = refs[0].shape
    total = refs[4 * len(terms)][...] if has_earlier else None
    out_ref = refs[-1]
    for i, (chunk, is_other) in enumerate(terms):
        left = jnp.concatenate(
            [part[...].reshape(z_size * tokens, depth) for part in refs[4 * i : 4 * i + 4]], axis=0
        )
        group = 2 * chunk + (1 - meta[0] if is_other else meta[0])
        at = pl.ds(pl.multiple_of(group * depth, depth), depth)
        product = jnp.dot(left, weight[at, :], preferred_element_type=f32)
        total = product if total is None else total + product
    if not last:
        out_ref[...] = total
        return
    size = z_size * tokens
    for j, chip in enumerate(plane_chips(meta)):
        to = pl.ds(pl.multiple_of(chip * size, size), size)
        out_ref[to, :] = total[j * size : (j + 1) * size]


def hop(value, mask):
    pairs = [(source, source ^ mask) for source in range(lax.axis_size("ctx"))]
    return lax.ppermute(value, "ctx", pairs)


def plane_hop(value, number):
    masks = {1: (2, 4), 2: (4, 2), 3: (6, 6)}[number]
    pairs = [(source, source ^ masks[source % 2]) for source in range(lax.axis_size("ctx"))]
    return lax.ppermute(value, "ctx", pairs)


def line_hop(value, reach, z_size):
    masks = (8 * reach, 4 * z_size // reach)
    pairs = [(source, source ^ masks[source % 2]) for source in range(lax.axis_size("ctx"))]
    return lax.ppermute(value, "ctx", pairs)


VMEM = pl.BlockSpec(memory_space=pltpu.VMEM)
SMEM = pl.BlockSpec(memory_space=pltpu.SMEM)
HBM = pl.BlockSpec(memory_space=pltpu.HBM)
SMALL = pltpu.CompilerParams(vmem_limit_bytes=4 << 20)


def fast_body(queries, cache_keys, cache_values, block_mask, key_counts, out_weight):
    index = lax.axis_index("ctx")
    z_size = lax.axis_size("ctx") // 8
    token_count, head_count, d = queries.shape
    kv_count = cache_keys.shape[1]
    group_size = head_count // kv_count
    rows = token_count * group_size
    pieces = rows // LANES
    positions = cache_keys.shape[0]
    features = out_weight.shape[1]
    core = index & 1
    my_xy = (index >> 1) & 3
    tall = d + STAT
    keys = cache_keys.reshape(positions * kv_count, d)
    values = cache_values.reshape(positions * kv_count, d)
    place = jnp.concatenate(
        [jnp.stack([core, my_xy]).astype(jnp.int32), block_mask[0], key_counts]
    )
    kept_in_hbm = functools.partial(pltpu.with_memory_space_constraint, memory_space=pltpu.HBM)
    state = jax.ShapeDtypeStruct((z_size, tall, LANES), bf16)

    partial = jax.ShapeDtypeStruct((pieces, tall, LANES), bf16)
    blocks = positions // BLK

    def split_and_attend():
        return pl.pallas_call(
            split_kernel,
            in_specs=[SMEM] + [HBM] * 3,
            out_specs=[VMEM] * 3,
            scratch_shapes=[
                pltpu.SMEM((blocks + 1,), jnp.int32),
                pltpu.SMEM((blocks + 1,), jnp.int32),
                pltpu.VMEM((token_count, group_size, d), bf16),
                pltpu.VMEM((positions * kv_count, d), bf16),
                pltpu.VMEM((positions * kv_count, d), bf16),
                pltpu.VMEM((BLK * kv_count, d), f32),
                pltpu.SemaphoreType.DMA((3,)),
            ],
            out_shape=[
                jax.ShapeDtypeStruct((kv_count, positions, d), bf16),
                jax.ShapeDtypeStruct((kv_count, tall, positions), bf16),
                partial,
            ],
            compiler_params=pltpu.CompilerParams(vmem_limit_bytes=32 << 20),
            cost_estimate=pl.CostEstimate(
                flops=4 * rows * positions * d,
                transcendentals=rows * positions,
                bytes_accessed=4 * positions * d * kv_count,
            ),
            name="split_and_attend",
        )(place, kept_in_hbm(keys), kept_in_hbm(values), kept_in_hbm(queries))

    def attend(chunk_roles, kd, vt):
        count = len(chunk_roles)
        return pl.pallas_call(
            functools.partial(attention_kernel, chunk_roles),
            in_specs=[SMEM] + [VMEM] * 3,
            out_specs=[VMEM] * count,
            out_shape=[partial] * count,
            compiler_params=pltpu.CompilerParams(vmem_limit_bytes=32 << 20),
            cost_estimate=pl.CostEstimate(
                flops=4 * count * rows * positions * d,
                transcendentals=count * rows * positions,
                bytes_accessed=4 * positions * d * count,
            ),
            name="attend",
        )(place, kd, vt, queries)

    def merge_cores(kept, received):
        return pl.pallas_call(
            core_kernel,
            in_specs=[SMEM] + [VMEM] * 2,
            out_specs=[VMEM] * 4,
            out_shape=[state] * 4,
            compiler_params=SMALL,
            name="merge_cores",
        )(place, kept, received)

    def merge_chips(parts):
        return pl.pallas_call(
            plane_kernel,
            in_specs=[VMEM] * len(parts),
            out_specs=VMEM,
            out_shape=state,
            compiler_params=SMALL,
            name="merge_chips",
        )(*parts)

    def finish(parts):
        tokens = LANES // group_size
        return pl.pallas_call(
            last_kernel,
            in_specs=[VMEM] * len(parts),
            out_specs=VMEM,
            out_shape=jax.ShapeDtypeStruct((z_size, tokens, group_size * d), bf16),
            scratch_shapes=[pltpu.VMEM((z_size, LANES, d), f32)],
            compiler_params=SMALL,
            name="finish",
        )(*parts)

    def project(terms, parts, earlier, last=False):
        depth = group_size * d
        more = [] if earlier is None else [earlier]
        return pl.pallas_call(
            functools.partial(project_kernel, terms, bool(more), last),
            in_specs=[SMEM] + [VMEM] * (1 + len(parts) + len(more)),
            out_specs=VMEM,
            out_shape=jax.ShapeDtypeStruct((token_count, features), f32),
            compiler_params=pltpu.CompilerParams(vmem_limit_bytes=8 << 20),
            cost_estimate=pl.CostEstimate(
                flops=2 * len(terms) * token_count * depth * features,
                transcendentals=0,
                bytes_accessed=2 * len(terms) * depth * features,
            ),
            name="project",
        )(place, out_weight, *parts, *more)

    def exchange_plane(parts):
        return [parts[0]] + [plane_hop(parts[j], j) for j in (1, 2, 3)]

    def near(part):
        return merge_chips([part, line_hop(part, 1, z_size)])

    def far(part):
        return finish([part, line_hop(part, 2, z_size)])

    def gather_plane(attended):
        first, second = plane_hop(attended, 1), plane_hop(attended, 2)
        return [attended, first, second, plane_hop(first, 2)]

    kd, vt, sent = split_and_attend()
    received = hop(sent, 1)
    kept, sent = attend([(0, False), (1, True)], kd, vt)
    next_received = hop(sent, 1)
    parts = merge_cores(kept, received)
    parts, kd = lax.optimization_barrier((parts, kd))
    first = exchange_plane(parts)
    (kept,) = attend([(1, False)], kd, vt)
    parts = merge_cores(kept, next_received)
    parts, first[0] = lax.optimization_barrier((parts, first[0]))
    second = exchange_plane(parts)
    part = near(merge_chips(first))
    next_part = merge_chips(second)
    part, next_part = lax.optimization_barrier((part, next_part))
    attended = far(part)
    next_part = near(next_part)
    attended, next_part = lax.optimization_barrier((attended, next_part))
    own = gather_plane(attended)
    other = [hop(own[j], 1) for j in (0, 2, 1, 3)]
    next_own = gather_plane(far(next_part))
    next_other = [hop(next_own[j], 1) for j in (0, 2, 1, 3)]
    total = project([(0, False), (0, True), (1, False)], own + other + next_own, None)
    return project([(1, True)], next_other, total, last=True)


def partner_of(value, axis, distance):
    mask = 2**distance
    pairs = [(source, source ^ mask) for source in range(lax.axis_size(axis))]
    return lax.ppermute(value, axis, pairs)


def combine(earlier, later):
    out_one, top_one, sum_one = earlier
    out_two, top_two, sum_two = later
    new_top = jnp.maximum(top_one, top_two)
    factor_one = jnp.exp(top_one - new_top)
    factor_two = jnp.exp(top_two - new_top)
    new_out = out_one * factor_one[..., None] + out_two * factor_two[..., None]
    return (new_out, new_top, sum_one * factor_one + sum_two * factor_two)


def keep_state(key_block, run_state):
    return run_state


def partial_rows(rows_q, row_mask, cache_keys, cache_values, key_counts):
    row_count, head_count, head_size = rows_q.shape
    kv_count = cache_keys.shape[1]
    group_size = head_count // kv_count
    grouped = rows_q.reshape(row_count, kv_count, group_size, head_size)
    block_count = cache_keys.shape[0] // BLK
    score_scale = 1.0 / math.sqrt(head_size)
    offsets = jnp.arange(BLK, dtype=jnp.int32)

    def update(key_block, run_state):
        out_sum, top_score, weight_sum = run_state
        key_part = lax.dynamic_slice_in_dim(cache_keys, key_block * BLK, BLK, 0)
        value_part = lax.dynamic_slice_in_dim(cache_values, key_block * BLK, BLK, 0)
        scores = (
            jnp.einsum("rgqd,kgd->rgqk", grouped, key_part, preferred_element_type=jnp.float32)
            * score_scale
        )
        active_rows = lax.dynamic_slice_in_dim(row_mask, key_block, 1, 1)[:, 0] > 0
        valid_count = lax.dynamic_slice_in_dim(key_counts, key_block, 1, 0)[0]
        valid = active_rows[:, None, None, None] & (offsets < valid_count)[None, None, None, :]
        scores = jnp.where(valid, scores, very_low)
        new_top = jnp.maximum(top_score, jnp.max(scores, axis=-1))
        weights = jnp.where(valid, jnp.exp(scores - new_top[..., None]), 0.0)
        factor = jnp.exp(top_score - new_top)
        new_sum = weight_sum * factor + jnp.sum(weights, axis=-1)
        new_out = out_sum * factor[..., None] + jnp.einsum(
            "rgqk,kgd->rgqd",
            weights.astype(jnp.bfloat16),
            value_part,
            preferred_element_type=jnp.float32,
        )
        return (new_out, new_top, new_sum)

    def visit_block(key_block, run_state):
        active = jnp.any(lax.dynamic_slice_in_dim(row_mask, key_block, 1, 1) > 0)
        return lax.cond(active, update, keep_state, key_block, run_state)

    initial = (
        jnp.zeros((row_count, kv_count, group_size, head_size), jnp.float32),
        jnp.full((row_count, kv_count, group_size), very_low, jnp.float32),
        jnp.zeros((row_count, kv_count, group_size), jnp.float32),
    )
    return lax.fori_loop(0, block_count, visit_block, initial)


def general_body(queries, cache_keys, cache_values, block_mask, key_counts, out_weight):
    cycle_size = lax.axis_size("ctx")
    cycle_index = lax.axis_index("ctx")
    token_count, head_count, head_size = queries.shape
    segment = token_count // cycle_size
    query_blocks = queries.reshape(block_mask.shape[0], BLK, head_count, head_size)

    def per_block(block_item):
        rows_q, mask_row = block_item
        row_mask = jnp.broadcast_to(mask_row[None, :], (BLK, mask_row.shape[0]))
        return partial_rows(rows_q, row_mask, cache_keys, cache_values, key_counts)

    stacked = lax.map(per_block, (query_blocks, block_mask))
    run_state = tuple((part.reshape((token_count,) + part.shape[2:]) for part in stacked))
    bit_total = cycle_size.bit_length() - 1
    for bit_number in range(bit_total - 1, -1, -1):
        half_rows = run_state[1].shape[0] // 2
        upper_half = jnp.bitwise_and(jnp.right_shift(cycle_index, bit_number), 1)
        kept = tuple(
            (
                lax.dynamic_slice_in_dim(part, upper_half * half_rows, half_rows, 0)
                for part in run_state
            )
        )
        outgoing = tuple(
            (
                lax.dynamic_slice_in_dim(part, (1 - upper_half) * half_rows, half_rows, 0)
                for part in run_state
            )
        )
        received = partner_of((outgoing[0], outgoing[1], outgoing[2]), "ctx", bit_number)
        run_state = combine(kept, received)
    out_sum, top_score, weight_sum = run_state
    attended = (
        (out_sum / weight_sum[..., None])
        .astype(jnp.bfloat16)
        .reshape(segment, head_count * head_size)
    )
    partial_value = jnp.dot(
        lax.all_gather(attended, "ctx", axis=0, tiled=True),
        out_weight,
        preferred_element_type=jnp.float32,
    )
    return lax.psum_scatter(partial_value, "kv", scatter_dimension=0, tiled=True)


def body(queries, cache_keys, cache_values, block_mask, key_counts, out_weight):
    devices = lax.axis_size("ctx")
    token_count, head_count, d = queries.shape
    kv_count = cache_keys.shape[1]
    group_size = head_count // kv_count
    suits = (
        lax.axis_size("kv") == 1
        and devices == 32
        and token_count == BLK
        and block_mask.shape[0] == 1
        and kv_count == 4
        and d == LANES
        and group_size == 16
        and token_count * group_size == LANES * (devices // 2)
    )
    run = fast_body if suits else general_body
    return run(queries, cache_keys, cache_values, block_mask, key_counts, out_weight)


def solution(mesh):
    placed = (
        P("groups", "kv", None),
        P(("groups", "ctx"), "kv", None),
        P(("groups", "ctx"), "kv", None),
        P("groups", "ctx"),
        P(("groups", "ctx")),
        P("kv", "ctx"),
    )
    return jax.shard_map(
        body, mesh=mesh, in_specs=placed, out_specs=P(("groups", "kv"), "ctx"), check_vma=False
    )
```

```python
import functools
import math

import jax
import jax.numpy as jnp
from jax import lax
from jax.experimental import pallas as pl
from jax.experimental.pallas import tpu as pltpu
from jax.sharding import PartitionSpec as P

BLK = 128
LANES = 128
STAT = 8
very_low = -1e30
lowest_top = -(2.0**99)
bf16 = jnp.bfloat16
f32 = jnp.float32


def pack_state(out, top, total):
    high = total.astype(bf16).astype(f32)
    low = total - high
    row = lax.broadcasted_iota(jnp.int32, (STAT, LANES), 0)
    stats = jnp.where(row == 0, top, jnp.where(row == 1, high, jnp.where(row == 2, low, 0.0)))
    return out.astype(bf16), stats.astype(bf16)


def split_kernel(
    meta, mask_hbm, counts_hbm, k_hbm, v_hbm, q_hbm, kd, vt, sent_ref, active_ref, *scratch
):
    mask, counts, listed, kept_counts, q_ref, k_ref, v_ref, spread, sems = scratch
    d = k_hbm.shape[1]
    kv_count = kd.shape[0]
    group_size = q_ref.shape[1]
    block_count = counts.shape[0]
    group = 1 - meta[0]

    heads = pl.ds(pl.multiple_of(group * group_size, group_size), group_size)
    copies = [
        pltpu.make_async_copy(k_hbm, k_ref, sems.at[0]),
        pltpu.make_async_copy(v_hbm, v_ref, sems.at[1]),
        pltpu.make_async_copy(q_hbm.at[:, heads, :], q_ref, sems.at[2]),
        pltpu.make_async_copy(mask_hbm, mask, sems.at[3]),
        pltpu.make_async_copy(counts_hbm, counts, sems.at[4]),
    ]
    for copy in copies:
        copy.start()

    def note(block, found):
        listed[found] = block
        kept_counts[found] = counts[block]
        return found + (mask[0, block] > 0).astype(jnp.int32)

    copies[3].wait()
    copies[4].wait()
    active = lax.fori_loop(0, block_count, note, jnp.int32(0))
    active_ref[0] = active
    place = lax.broadcasted_iota(jnp.int32, (BLK, LANES), 0)
    across = lax.broadcasted_iota(jnp.int32, (STAT, LANES), 1)

    def split(source, position):
        start = pl.multiple_of(listed[position] * (BLK * kv_count), BLK * kv_count)
        spread[...] = source[pl.ds(start, BLK * kv_count), :].astype(f32)
        return [spread[pl.ds(g, BLK, stride=kv_count), :] for g in range(kv_count)]

    def fetch_keys(position, carry):
        at = pl.ds(pl.multiple_of(position * BLK, BLK), BLK)
        valid = place < kept_counts[position]
        for g, key in enumerate(split(k_ref, position)):
            kd[g, at, :] = jnp.where(valid, key, key[0:1]).astype(bf16)
        return carry

    def fetch_values(position, carry):
        at = pl.ds(pl.multiple_of(position * BLK, BLK), BLK)
        count = kept_counts[position]
        for g, value in enumerate(split(v_ref, position)):
            vt[g, 0:d, at] = jnp.where(place < count, value, 0.0).T.astype(bf16)
            vt[g, d:, at] = (across < count).astype(f32).astype(bf16)
        return carry

    copies[0].wait()
    lax.fori_loop(0, active, fetch_keys, 0)
    copies[1].wait()
    lax.fori_loop(0, active, fetch_values, 0)

    @pl.when(active % 2 == 1)
    def _():
        at = pl.ds(pl.multiple_of(active * BLK, BLK), BLK)
        before = pl.ds(pl.multiple_of((active - 1) * BLK, BLK), BLK)
        for g in range(kv_count):
            kd[g, at, :] = kd[g, before, :]
            vt[g, :, at] = jnp.zeros((d + STAT, BLK), bf16)

    copies[2].wait()
    attend_all(active, [(sent_ref, group, lambda: q_ref[...])], kd, vt)


def attention_kernel(chunk_roles, meta, active_ref, kd, vt, q_ref, *outs):
    group_size = q_ref.shape[1] // kd.shape[0]
    todo = []
    for out, (chunk, is_other) in zip(outs, chunk_roles):
        group = 2 * chunk + (1 - meta[0] if is_other else meta[0])

        def read(group=group):
            heads = pl.ds(pl.multiple_of(group * group_size, group_size), group_size)
            return q_ref[:, heads, :]

        todo.append((out, group, read))
    attend_all(active_ref[0], todo, kd, vt)


def attend_all(active, todo, kd, vt):
    d = kd.shape[2]
    scale2 = math.log2(math.e) / math.sqrt(d)
    rows = todo[0][0].shape[0] * LANES
    pairs = (active + 1) // 2

    def attend(width, out, group, read):
        q = read().reshape(rows, d)
        scores = lax.dot_general(
            kd[group, 0:width, :], q, (((1,), (1,)), ((), ())), preferred_element_type=f32
        )
        top = (jnp.max(scores, axis=0, keepdims=True) * scale2).astype(bf16).astype(f32)
        weights = jnp.exp2(scores * scale2 - top).astype(bf16)
        sums = jnp.dot(vt[group, :, 0:width], weights, preferred_element_type=f32)
        total = sums[d:]
        high = total.astype(bf16).astype(f32)
        row = lax.broadcasted_iota(jnp.int32, (STAT, rows), 0)
        stats = jnp.where(row == 0, top, jnp.where(row == 1, high, total - high)).astype(bf16)
        value = sums[:d].astype(bf16)
        for piece in range(rows // LANES):
            at = slice(piece * LANES, (piece + 1) * LANES)
            out[piece, 0:d] = value[:, at]
            out[piece, d:] = stats[:, at]

    for n in range(1, kd.shape[1] // (2 * BLK) + 1):

        @pl.when(pairs == n)
        def _(n=n):
            for out, group, read in todo:
                attend(2 * BLK * n, out, group, read)

    @pl.when(pairs == 0)
    def _():
        row = lax.broadcasted_iota(jnp.int32, (d + STAT, LANES), 0)
        empty = jnp.where(row == d, lowest_top, 0.0).astype(bf16)
        for out, _, _ in todo:
            for piece in range(rows // LANES):
                out[piece] = empty


def merged(parts, d):
    stats = [part[d : d + STAT, :].astype(f32) for part in parts]
    tops = [stat[0:1] for stat in stats]
    top = functools.reduce(jnp.maximum, tops)
    out, total = 0.0, 0.0
    for part, stat, one in zip(parts, stats, tops):
        factor = jnp.exp2(one - top)
        out = out + part[0:d, :].astype(f32) * factor
        total = total + (stat[1:2] + stat[2:3]) * factor
    return out, top, total


def store_merged(ref, z, parts):
    d = ref.shape[1] - STAT
    out, stats = pack_state(*merged(parts, d))
    ref[z, 0:d, :] = out
    ref[z, d : d + STAT, :] = stats


def plane_chips(meta):
    core, my_xy = meta[0], meta[1]
    return [my_xy, my_xy ^ (1 + core), my_xy ^ (2 - core), my_xy ^ 3]


def core_kernel(meta, kept, received, *outs):
    z_size = outs[0].shape[0]
    for chip, out in zip(plane_chips(meta), outs):
        for z in range(z_size):
            piece = chip * z_size + z
            store_merged(out, z, [kept[piece], received[piece]])


def plane_kernel(*refs):
    ins, out = refs[:-1], refs[-1]
    for z in range(out.shape[0]):
        store_merged(out, z, [ref[z] for ref in ins])


def last_kernel(*refs):
    ins, out_ref, turned = refs[:-2], refs[-2], refs[-1]
    d = ins[0].shape[1] - STAT
    tokens = out_ref.shape[1]
    heads = LANES // tokens
    for z in range(out_ref.shape[0]):
        out, _, total = merged([ref[z] for ref in ins], d)
        turned[z] = (out / total).T
        for h in range(heads):
            picked = turned[z, pl.ds(h, tokens, stride=heads), :]
            out_ref[z, :, h * d : (h + 1) * d] = picked.astype(bf16)


def project_kernel(terms, has_earlier, last, meta, weight, *refs):
    z_size, tokens, depth = refs[0].shape
    total = refs[4 * len(terms)][...] if has_earlier else None
    out_ref = refs[-1]
    for i, (chunk, is_other) in enumerate(terms):
        left = jnp.concatenate(
            [part[...].reshape(z_size * tokens, depth) for part in refs[4 * i : 4 * i + 4]], axis=0
        )
        group = 2 * chunk + (1 - meta[0] if is_other else meta[0])
        at = pl.ds(pl.multiple_of(group * depth, depth), depth)
        product = jnp.dot(left, weight[at, :], preferred_element_type=f32)
        total = product if total is None else total + product
    if not last:
        out_ref[...] = total
        return
    size = z_size * tokens
    for j, chip in enumerate(plane_chips(meta)):
        to = pl.ds(pl.multiple_of(chip * size, size), size)
        out_ref[to, :] = total[j * size : (j + 1) * size]


def hop(value, mask):
    pairs = [(source, source ^ mask) for source in range(lax.axis_size("ctx"))]
    return lax.ppermute(value, "ctx", pairs)


def plane_hop(value, number):
    masks = {1: (2, 4), 2: (4, 2), 3: (6, 6)}[number]
    pairs = [(source, source ^ masks[source % 2]) for source in range(lax.axis_size("ctx"))]
    return lax.ppermute(value, "ctx", pairs)


def line_hop(value, reach, z_size):
    masks = (8 * reach, 4 * z_size // reach)
    pairs = [(source, source ^ masks[source % 2]) for source in range(lax.axis_size("ctx"))]
    return lax.ppermute(value, "ctx", pairs)


VMEM = pl.BlockSpec(memory_space=pltpu.VMEM)
SMEM = pl.BlockSpec(memory_space=pltpu.SMEM)
HBM = pl.BlockSpec(memory_space=pltpu.HBM)
SMALL = pltpu.CompilerParams(vmem_limit_bytes=4 << 20)


def fast_body(queries, cache_keys, cache_values, block_mask, key_counts, out_weight):
    index = lax.axis_index("ctx")
    z_size = lax.axis_size("ctx") // 8
    token_count, head_count, d = queries.shape
    kv_count = cache_keys.shape[1]
    group_size = head_count // kv_count
    rows = token_count * group_size
    pieces = rows // LANES
    positions = cache_keys.shape[0]
    features = out_weight.shape[1]
    core = index & 1
    my_xy = (index >> 1) & 3
    tall = d + STAT
    keys = cache_keys.reshape(positions * kv_count, d)
    values = cache_values.reshape(positions * kv_count, d)
    place = jnp.stack([core, my_xy]).astype(jnp.int32)
    kept_in_hbm = functools.partial(pltpu.with_memory_space_constraint, memory_space=pltpu.HBM)
    state = jax.ShapeDtypeStruct((z_size, tall, LANES), bf16)

    partial = jax.ShapeDtypeStruct((pieces, tall, LANES), bf16)
    blocks = positions // BLK

    def split_and_attend():
        return pl.pallas_call(
            split_kernel,
            in_specs=[SMEM] + [HBM] * 5,
            out_specs=[VMEM] * 3 + [SMEM],
            scratch_shapes=[
                pltpu.SMEM((1, blocks), jnp.int32),
                pltpu.SMEM((blocks,), jnp.int32),
                pltpu.SMEM((blocks + 1,), jnp.int32),
                pltpu.SMEM((blocks + 1,), jnp.int32),
                pltpu.VMEM((token_count, group_size, d), bf16),
                pltpu.VMEM((positions * kv_count, d), bf16),
                pltpu.VMEM((positions * kv_count, d), bf16),
                pltpu.VMEM((BLK * kv_count, d), f32),
                pltpu.SemaphoreType.DMA((5,)),
            ],
            out_shape=[
                jax.ShapeDtypeStruct((kv_count, positions, d), bf16),
                jax.ShapeDtypeStruct((kv_count, tall, positions), bf16),
                partial,
                jax.ShapeDtypeStruct((1,), jnp.int32),
            ],
            compiler_params=pltpu.CompilerParams(vmem_limit_bytes=32 << 20),
            cost_estimate=pl.CostEstimate(
                flops=4 * rows * positions * d,
                transcendentals=rows * positions,
                bytes_accessed=4 * positions * d * kv_count,
            ),
            name="split_and_attend",
        )(place, *map(kept_in_hbm, (block_mask, key_counts, keys, values, queries)))

    def attend(chunk_roles, kd, vt, active):
        count = len(chunk_roles)
        return pl.pallas_call(
            functools.partial(attention_kernel, chunk_roles),
            in_specs=[SMEM] * 2 + [VMEM] * 3,
            out_specs=[VMEM] * count,
            out_shape=[partial] * count,
            compiler_params=pltpu.CompilerParams(vmem_limit_bytes=32 << 20),
            cost_estimate=pl.CostEstimate(
                flops=4 * count * rows * positions * d,
                transcendentals=count * rows * positions,
                bytes_accessed=4 * positions * d * count,
            ),
            name="attend",
        )(place, active, kd, vt, queries)

    def merge_cores(kept, received):
        return pl.pallas_call(
            core_kernel,
            in_specs=[SMEM] + [VMEM] * 2,
            out_specs=[VMEM] * 4,
            out_shape=[state] * 4,
            compiler_params=SMALL,
            name="merge_cores",
        )(place, kept, received)

    def merge_chips(parts):
        return pl.pallas_call(
            plane_kernel,
            in_specs=[VMEM] * len(parts),
            out_specs=VMEM,
            out_shape=state,
            compiler_params=SMALL,
            name="merge_chips",
        )(*parts)

    def finish(parts):
        tokens = LANES // group_size
        return pl.pallas_call(
            last_kernel,
            in_specs=[VMEM] * len(parts),
            out_specs=VMEM,
            out_shape=jax.ShapeDtypeStruct((z_size, tokens, group_size * d), bf16),
            scratch_shapes=[pltpu.VMEM((z_size, LANES, d), f32)],
            compiler_params=SMALL,
            name="finish",
        )(*parts)

    def project(terms, parts, earlier, last=False):
        depth = group_size * d
        more = [] if earlier is None else [earlier]
        return pl.pallas_call(
            functools.partial(project_kernel, terms, bool(more), last),
            in_specs=[SMEM] + [VMEM] * (1 + len(parts) + len(more)),
            out_specs=VMEM,
            out_shape=jax.ShapeDtypeStruct((token_count, features), f32),
            compiler_params=pltpu.CompilerParams(vmem_limit_bytes=8 << 20),
            cost_estimate=pl.CostEstimate(
                flops=2 * len(terms) * token_count * depth * features,
                transcendentals=0,
                bytes_accessed=2 * len(terms) * depth * features,
            ),
            name="project",
        )(place, out_weight, *parts, *more)

    def exchange_plane(parts):
        return [parts[0]] + [plane_hop(parts[j], j) for j in (1, 2, 3)]

    def exchange_line(parts):
        part = merge_chips(parts)
        reach = 1
        while 2 * reach < z_size:
            part = merge_chips([part, line_hop(part, reach, z_size)])
            reach *= 2
        return finish([part, line_hop(part, reach, z_size)])

    def gather_plane(attended):
        first, second = plane_hop(attended, 1), plane_hop(attended, 2)
        return [attended, first, second, plane_hop(first, 2)]

    kd, vt, sent, active = split_and_attend()
    received = hop(sent, 1)
    kept, sent = attend([(0, False), (1, True)], kd, vt, active)
    next_received = hop(sent, 1)
    parts = merge_cores(kept, received)
    parts, kd = lax.optimization_barrier((parts, kd))
    first = exchange_plane(parts)
    (kept,) = attend([(1, False)], kd, vt, active)
    parts = merge_cores(kept, next_received)
    parts, first[0] = lax.optimization_barrier((parts, first[0]))
    second = exchange_plane(parts)
    own = gather_plane(exchange_line(first))
    other = [hop(own[j], 1) for j in (0, 2, 1, 3)]
    next_own = gather_plane(exchange_line(second))
    next_other = [hop(next_own[j], 1) for j in (0, 2, 1, 3)]
    total = project([(0, False), (0, True), (1, False)], own + other + next_own, None)
    return project([(1, True)], next_other, total, last=True)


def partner_of(value, axis, distance):
    mask = 2**distance
    pairs = [(source, source ^ mask) for source in range(lax.axis_size(axis))]
    return lax.ppermute(value, axis, pairs)


def combine(earlier, later):
    out_one, top_one, sum_one = earlier
    out_two, top_two, sum_two = later
    new_top = jnp.maximum(top_one, top_two)
    factor_one = jnp.exp(top_one - new_top)
    factor_two = jnp.exp(top_two - new_top)
    new_out = out_one * factor_one[..., None] + out_two * factor_two[..., None]
    return (new_out, new_top, sum_one * factor_one + sum_two * factor_two)


def keep_state(key_block, run_state):
    return run_state


def partial_rows(rows_q, row_mask, cache_keys, cache_values, key_counts):
    row_count, head_count, head_size = rows_q.shape
    kv_count = cache_keys.shape[1]
    group_size = head_count // kv_count
    grouped = rows_q.reshape(row_count, kv_count, group_size, head_size)
    block_count = cache_keys.shape[0] // BLK
    score_scale = 1.0 / math.sqrt(head_size)
    offsets = jnp.arange(BLK, dtype=jnp.int32)

    def update(key_block, run_state):
        out_sum, top_score, weight_sum = run_state
        key_part = lax.dynamic_slice_in_dim(cache_keys, key_block * BLK, BLK, 0)
        value_part = lax.dynamic_slice_in_dim(cache_values, key_block * BLK, BLK, 0)
        scores = (
            jnp.einsum("rgqd,kgd->rgqk", grouped, key_part, preferred_element_type=jnp.float32)
            * score_scale
        )
        active_rows = lax.dynamic_slice_in_dim(row_mask, key_block, 1, 1)[:, 0] > 0
        valid_count = lax.dynamic_slice_in_dim(key_counts, key_block, 1, 0)[0]
        valid = active_rows[:, None, None, None] & (offsets < valid_count)[None, None, None, :]
        scores = jnp.where(valid, scores, very_low)
        new_top = jnp.maximum(top_score, jnp.max(scores, axis=-1))
        weights = jnp.where(valid, jnp.exp(scores - new_top[..., None]), 0.0)
        factor = jnp.exp(top_score - new_top)
        new_sum = weight_sum * factor + jnp.sum(weights, axis=-1)
        new_out = out_sum * factor[..., None] + jnp.einsum(
            "rgqk,kgd->rgqd",
            weights.astype(jnp.bfloat16),
            value_part,
            preferred_element_type=jnp.float32,
        )
        return (new_out, new_top, new_sum)

    def visit_block(key_block, run_state):
        active = jnp.any(lax.dynamic_slice_in_dim(row_mask, key_block, 1, 1) > 0)
        return lax.cond(active, update, keep_state, key_block, run_state)

    initial = (
        jnp.zeros((row_count, kv_count, group_size, head_size), jnp.float32),
        jnp.full((row_count, kv_count, group_size), very_low, jnp.float32),
        jnp.zeros((row_count, kv_count, group_size), jnp.float32),
    )
    return lax.fori_loop(0, block_count, visit_block, initial)


def general_body(queries, cache_keys, cache_values, block_mask, key_counts, out_weight):
    cycle_size = lax.axis_size("ctx")
    cycle_index = lax.axis_index("ctx")
    token_count, head_count, head_size = queries.shape
    segment = token_count // cycle_size
    query_blocks = queries.reshape(block_mask.shape[0], BLK, head_count, head_size)

    def per_block(block_item):
        rows_q, mask_row = block_item
        row_mask = jnp.broadcast_to(mask_row[None, :], (BLK, mask_row.shape[0]))
        return partial_rows(rows_q, row_mask, cache_keys, cache_values, key_counts)

    stacked = lax.map(per_block, (query_blocks, block_mask))
    run_state = tuple((part.reshape((token_count,) + part.shape[2:]) for part in stacked))
    bit_total = cycle_size.bit_length() - 1
    for bit_number in range(bit_total - 1, -1, -1):
        half_rows = run_state[1].shape[0] // 2
        upper_half = jnp.bitwise_and(jnp.right_shift(cycle_index, bit_number), 1)
        kept = tuple(
            (
                lax.dynamic_slice_in_dim(part, upper_half * half_rows, half_rows, 0)
                for part in run_state
            )
        )
        outgoing = tuple(
            (
                lax.dynamic_slice_in_dim(part, (1 - upper_half) * half_rows, half_rows, 0)
                for part in run_state
            )
        )
        received = partner_of((outgoing[0], outgoing[1], outgoing[2]), "ctx", bit_number)
        run_state = combine(kept, received)
    out_sum, top_score, weight_sum = run_state
    attended = (
        (out_sum / weight_sum[..., None])
        .astype(jnp.bfloat16)
        .reshape(segment, head_count * head_size)
    )
    partial_value = jnp.dot(
        lax.all_gather(attended, "ctx", axis=0, tiled=True),
        out_weight,
        preferred_element_type=jnp.float32,
    )
    return lax.psum_scatter(partial_value, "kv", scatter_dimension=0, tiled=True)


def body(queries, cache_keys, cache_values, block_mask, key_counts, out_weight):
    devices = lax.axis_size("ctx")
    token_count, head_count, d = queries.shape
    kv_count = cache_keys.shape[1]
    group_size = head_count // kv_count
    suits = (
        lax.axis_size("kv") == 1
        and devices == 32
        and token_count == BLK
        and block_mask.shape[0] == 1
        and kv_count == 4
        and d == LANES
        and group_size == 16
        and token_count * group_size == LANES * (devices // 2)
    )
    run = fast_body if suits else general_body
    return run(queries, cache_keys, cache_values, block_mask, key_counts, out_weight)


def solution(mesh):
    placed = (
        P("groups", "kv", None),
        P(("groups", "ctx"), "kv", None),
        P(("groups", "ctx"), "kv", None),
        P("groups", "ctx"),
        P(("groups", "ctx")),
        P("kv", "ctx"),
    )
    return jax.shard_map(
        body, mesh=mesh, in_specs=placed, out_specs=P(("groups", "kv"), "ctx"), check_vma=False
    )
```

```python
import functools
import math

import jax
import jax.numpy as jnp
from jax import lax
from jax.experimental import pallas as pl
from jax.experimental.pallas import tpu as pltpu
from jax.sharding import PartitionSpec as P

BLK = 128
LANES = 128
STAT = 8
very_low = -1e30
lowest_top = -(2.0**99)
bf16 = jnp.bfloat16
f32 = jnp.float32


def pack_state(out, top, total):
    high = total.astype(bf16).astype(f32)
    low = total - high
    row = lax.broadcasted_iota(jnp.int32, (STAT, LANES), 0)
    stats = jnp.where(row == 0, top, jnp.where(row == 1, high, jnp.where(row == 2, low, 0.0)))
    return out.astype(bf16), stats.astype(bf16)


def active_count(meta):
    block_count = (meta.shape[0] - 2) // 2
    return sum((meta[2 + block] > 0).astype(jnp.int32) for block in range(block_count))


def split_kernel(meta, k_hbm, v_hbm, q_hbm, kd, vt, sent_ref, *scratch):
    listed, kept_counts, q_ref, k_ref, v_ref, spread, sems = scratch
    d = k_hbm.shape[1]
    kv_count = kd.shape[0]
    group_size = q_ref.shape[1]
    block_count = (meta.shape[0] - 2) // 2
    group = 1 - meta[0]

    heads = pl.ds(pl.multiple_of(group * group_size, group_size), group_size)
    copies = [
        pltpu.make_async_copy(k_hbm, k_ref, sems.at[0]),
        pltpu.make_async_copy(v_hbm, v_ref, sems.at[1]),
        pltpu.make_async_copy(q_hbm.at[:, heads, :], q_ref, sems.at[2]),
    ]
    for copy in copies:
        copy.start()

    def note(block, found):
        listed[found] = block
        kept_counts[found] = meta[2 + block_count + block]
        return found + (meta[2 + block] > 0).astype(jnp.int32)

    active = lax.fori_loop(0, block_count, note, jnp.int32(0))
    place = lax.broadcasted_iota(jnp.int32, (BLK, LANES), 0)
    across = lax.broadcasted_iota(jnp.int32, (STAT, LANES), 1)

    def split(source, position):
        start = pl.multiple_of(listed[position] * (BLK * kv_count), BLK * kv_count)
        spread[...] = source[pl.ds(start, BLK * kv_count), :].astype(f32)
        return [spread[pl.ds(g, BLK, stride=kv_count), :] for g in range(kv_count)]

    def fetch_keys(position, carry):
        at = pl.ds(pl.multiple_of(position * BLK, BLK), BLK)
        valid = place < kept_counts[position]
        for g, key in enumerate(split(k_ref, position)):
            kd[g, at, :] = jnp.where(valid, key, key[0:1]).astype(bf16)
        return carry

    def fetch_values(position, carry):
        at = pl.ds(pl.multiple_of(position * BLK, BLK), BLK)
        count = kept_counts[position]
        for g, value in enumerate(split(v_ref, position)):
            vt[g, 0:d, at] = jnp.where(place < count, value, 0.0).T.astype(bf16)
            vt[g, d:, at] = (across < count).astype(f32).astype(bf16)
        return carry

    copies[0].wait()
    lax.fori_loop(0, active, fetch_keys, 0)
    copies[1].wait()
    lax.fori_loop(0, active, fetch_values, 0)

    @pl.when(active % 2 == 1)
    def _():
        at = pl.ds(pl.multiple_of(active * BLK, BLK), BLK)
        before = pl.ds(pl.multiple_of((active - 1) * BLK, BLK), BLK)
        for g in range(kv_count):
            kd[g, at, :] = kd[g, before, :]
            vt[g, :, at] = jnp.zeros((d + STAT, BLK), bf16)

    copies[2].wait()
    attend_all(active, [(sent_ref, group, lambda: q_ref[...])], kd, vt)


def attention_kernel(chunk_roles, meta, kd, vt, q_ref, *outs):
    group_size = q_ref.shape[1] // kd.shape[0]
    todo = []
    for out, (chunk, is_other) in zip(outs, chunk_roles):
        group = 2 * chunk + (1 - meta[0] if is_other else meta[0])

        def read(group=group):
            heads = pl.ds(pl.multiple_of(group * group_size, group_size), group_size)
            return q_ref[:, heads, :]

        todo.append((out, group, read))
    attend_all(active_count(meta), todo, kd, vt)


def attend_all(active, todo, kd, vt):
    d = kd.shape[2]
    scale2 = math.log2(math.e) / math.sqrt(d)
    rows = todo[0][0].shape[0] * LANES
    pairs = (active + 1) // 2

    def attend(width, out, group, read):
        q = read().reshape(rows, d)
        scores = lax.dot_general(
            kd[group, 0:width, :], q, (((1,), (1,)), ((), ())), preferred_element_type=f32
        )
        top = (jnp.max(scores, axis=0, keepdims=True) * scale2).astype(bf16).astype(f32)
        weights = jnp.exp2(scores * scale2 - top).astype(bf16)
        sums = jnp.dot(vt[group, :, 0:width], weights, preferred_element_type=f32)
        total = sums[d:]
        high = total.astype(bf16).astype(f32)
        row = lax.broadcasted_iota(jnp.int32, (STAT, rows), 0)
        stats = jnp.where(row == 0, top, jnp.where(row == 1, high, total - high)).astype(bf16)
        value = sums[:d].astype(bf16)
        for piece in range(rows // LANES):
            at = slice(piece * LANES, (piece + 1) * LANES)
            out[piece, 0:d] = value[:, at]
            out[piece, d:] = stats[:, at]

    for n in range(1, kd.shape[1] // (2 * BLK) + 1):

        @pl.when(pairs == n)
        def _(n=n):
            for out, group, read in todo:
                attend(2 * BLK * n, out, group, read)

    @pl.when(pairs == 0)
    def _():
        row = lax.broadcasted_iota(jnp.int32, (d + STAT, LANES), 0)
        empty = jnp.where(row == d, lowest_top, 0.0).astype(bf16)
        for out, _, _ in todo:
            for piece in range(rows // LANES):
                out[piece] = empty


def merged(parts, d):
    stats = [part[d : d + STAT, :].astype(f32) for part in parts]
    tops = [stat[0:1] for stat in stats]
    top = functools.reduce(jnp.maximum, tops)
    out, total = 0.0, 0.0
    for part, stat, one in zip(parts, stats, tops):
        factor = jnp.exp2(one - top)
        out = out + part[0:d, :].astype(f32) * factor
        total = total + (stat[1:2] + stat[2:3]) * factor
    return out, top, total


def store_merged(ref, z, parts):
    d = ref.shape[1] - STAT
    out, stats = pack_state(*merged(parts, d))
    ref[z, 0:d, :] = out
    ref[z, d : d + STAT, :] = stats


def plane_chips(meta):
    core, my_xy = meta[0], meta[1]
    return [my_xy, my_xy ^ (1 + core), my_xy ^ (2 - core), my_xy ^ 3]


def core_kernel(meta, kept, received, *outs):
    z_size = outs[0].shape[0]
    for chip, out in zip(plane_chips(meta), outs):
        for z in range(z_size):
            piece = chip * z_size + z
            store_merged(out, z, [kept[piece], received[piece]])


def plane_kernel(*refs):
    ins, out = refs[:-1], refs[-1]
    for z in range(out.shape[0]):
        store_merged(out, z, [ref[z] for ref in ins])


def last_kernel(*refs):
    ins, out_ref, turned = refs[:-2], refs[-2], refs[-1]
    d = ins[0].shape[1] - STAT
    tokens = out_ref.shape[1]
    heads = LANES // tokens
    for z in range(out_ref.shape[0]):
        out, _, total = merged([ref[z] for ref in ins], d)
        turned[z] = (out / total).T
        for h in range(heads):
            picked = turned[z, pl.ds(h, tokens, stride=heads), :]
            out_ref[z, :, h * d : (h + 1) * d] = picked.astype(bf16)


def project_kernel(terms, has_earlier, last, meta, weight, *refs):
    z_size, tokens, depth = refs[0].shape
    total = refs[4 * len(terms)][...] if has_earlier else None
    out_ref = refs[-1]
    for i, (chunk, is_other) in enumerate(terms):
        left = jnp.concatenate(
            [part[...].reshape(z_size * tokens, depth) for part in refs[4 * i : 4 * i + 4]], axis=0
        )
        group = 2 * chunk + (1 - meta[0] if is_other else meta[0])
        at = pl.ds(pl.multiple_of(group * depth, depth), depth)
        product = jnp.dot(left, weight[at, :], preferred_element_type=f32)
        total = product if total is None else total + product
    if not last:
        out_ref[...] = total
        return
    size = z_size * tokens
    for j, chip in enumerate(plane_chips(meta)):
        to = pl.ds(pl.multiple_of(chip * size, size), size)
        out_ref[to, :] = total[j * size : (j + 1) * size]


def hop(value, mask):
    pairs = [(source, source ^ mask) for source in range(lax.axis_size("ctx"))]
    return lax.ppermute(value, "ctx", pairs)


def plane_hop(value, number):
    masks = {1: (2, 4), 2: (4, 2), 3: (6, 6)}[number]
    pairs = [(source, source ^ masks[source % 2]) for source in range(lax.axis_size("ctx"))]
    return lax.ppermute(value, "ctx", pairs)


def line_hop(value, reach, z_size):
    masks = (8 * reach, 4 * z_size // reach)
    pairs = [(source, source ^ masks[source % 2]) for source in range(lax.axis_size("ctx"))]
    return lax.ppermute(value, "ctx", pairs)


VMEM = pl.BlockSpec(memory_space=pltpu.VMEM)
SMEM = pl.BlockSpec(memory_space=pltpu.SMEM)
HBM = pl.BlockSpec(memory_space=pltpu.HBM)
SMALL = pltpu.CompilerParams(vmem_limit_bytes=4 << 20)


def fast_body(queries, cache_keys, cache_values, block_mask, key_counts, out_weight):
    index = lax.axis_index("ctx")
    z_size = lax.axis_size("ctx") // 8
    token_count, head_count, d = queries.shape
    kv_count = cache_keys.shape[1]
    group_size = head_count // kv_count
    rows = token_count * group_size
    pieces = rows // LANES
    positions = cache_keys.shape[0]
    features = out_weight.shape[1]
    core = index & 1
    my_xy = (index >> 1) & 3
    tall = d + STAT
    keys = cache_keys.reshape(positions * kv_count, d)
    values = cache_values.reshape(positions * kv_count, d)
    place = jnp.concatenate(
        [jnp.stack([core, my_xy]).astype(jnp.int32), block_mask[0], key_counts]
    )
    kept_in_hbm = functools.partial(pltpu.with_memory_space_constraint, memory_space=pltpu.HBM)
    state = jax.ShapeDtypeStruct((z_size, tall, LANES), bf16)

    partial = jax.ShapeDtypeStruct((pieces, tall, LANES), bf16)
    blocks = positions // BLK

    def split_and_attend():
        return pl.pallas_call(
            split_kernel,
            in_specs=[SMEM] + [HBM] * 3,
            out_specs=[VMEM] * 3,
            scratch_shapes=[
                pltpu.SMEM((blocks + 1,), jnp.int32),
                pltpu.SMEM((blocks + 1,), jnp.int32),
                pltpu.VMEM((token_count, group_size, d), bf16),
                pltpu.VMEM((positions * kv_count, d), bf16),
                pltpu.VMEM((positions * kv_count, d), bf16),
                pltpu.VMEM((BLK * kv_count, d), f32),
                pltpu.SemaphoreType.DMA((3,)),
            ],
            out_shape=[
                jax.ShapeDtypeStruct((kv_count, positions, d), bf16),
                jax.ShapeDtypeStruct((kv_count, tall, positions), bf16),
                partial,
            ],
            compiler_params=pltpu.CompilerParams(vmem_limit_bytes=32 << 20),
            cost_estimate=pl.CostEstimate(
                flops=4 * rows * positions * d,
                transcendentals=rows * positions,
                bytes_accessed=4 * positions * d * kv_count,
            ),
            name="split_and_attend",
        )(place, kept_in_hbm(keys), kept_in_hbm(values), kept_in_hbm(queries))

    def attend(chunk_roles, kd, vt):
        count = len(chunk_roles)
        return pl.pallas_call(
            functools.partial(attention_kernel, chunk_roles),
            in_specs=[SMEM] + [VMEM] * 3,
            out_specs=[VMEM] * count,
            out_shape=[partial] * count,
            compiler_params=pltpu.CompilerParams(vmem_limit_bytes=32 << 20),
            cost_estimate=pl.CostEstimate(
                flops=4 * count * rows * positions * d,
                transcendentals=count * rows * positions,
                bytes_accessed=4 * positions * d * count,
            ),
            name="attend",
        )(place, kd, vt, queries)

    def merge_cores(kept, received):
        return pl.pallas_call(
            core_kernel,
            in_specs=[SMEM] + [VMEM] * 2,
            out_specs=[VMEM] * 4,
            out_shape=[state] * 4,
            compiler_params=SMALL,
            name="merge_cores",
        )(place, kept, received)

    def merge_chips(parts):
        return pl.pallas_call(
            plane_kernel,
            in_specs=[VMEM] * len(parts),
            out_specs=VMEM,
            out_shape=state,
            compiler_params=SMALL,
            name="merge_chips",
        )(*parts)

    def finish(parts):
        tokens = LANES // group_size
        return pl.pallas_call(
            last_kernel,
            in_specs=[VMEM] * len(parts),
            out_specs=VMEM,
            out_shape=jax.ShapeDtypeStruct((z_size, tokens, group_size * d), bf16),
            scratch_shapes=[pltpu.VMEM((z_size, LANES, d), f32)],
            compiler_params=SMALL,
            name="finish",
        )(*parts)

    def project(terms, parts, earlier, last=False):
        depth = group_size * d
        more = [] if earlier is None else [earlier]
        return pl.pallas_call(
            functools.partial(project_kernel, terms, bool(more), last),
            in_specs=[SMEM] + [VMEM] * (1 + len(parts) + len(more)),
            out_specs=VMEM,
            out_shape=jax.ShapeDtypeStruct((token_count, features), f32),
            compiler_params=pltpu.CompilerParams(vmem_limit_bytes=8 << 20),
            cost_estimate=pl.CostEstimate(
                flops=2 * len(terms) * token_count * depth * features,
                transcendentals=0,
                bytes_accessed=2 * len(terms) * depth * features,
            ),
            name="project",
        )(place, out_weight, *parts, *more)

    def exchange_plane(parts):
        return [parts[0]] + [plane_hop(parts[j], j) for j in (1, 2, 3)]

    def near(part):
        return merge_chips([part, line_hop(part, 1, z_size)])

    def far(part):
        return finish([part, line_hop(part, 2, z_size)])

    def gather_plane(attended, direct):
        first, second = plane_hop(attended, 1), plane_hop(attended, 2)
        third = plane_hop(attended, 3) if direct else plane_hop(first, 2)
        return [attended, first, second, third]

    kd, vt, sent = split_and_attend()
    received = hop(sent, 1)
    kept, sent = attend([(0, False), (1, True)], kd, vt)
    next_received = hop(sent, 1)
    parts = merge_cores(kept, received)
    parts, kd = lax.optimization_barrier((parts, kd))
    first = exchange_plane(parts)
    (kept,) = attend([(1, False)], kd, vt)
    parts = merge_cores(kept, next_received)
    parts, first[0] = lax.optimization_barrier((parts, first[0]))
    second = exchange_plane(parts)
    part = near(merge_chips(first))
    next_part = merge_chips(second)
    part, next_part = lax.optimization_barrier((part, next_part))
    attended = far(part)
    next_part = near(next_part)
    attended, next_part = lax.optimization_barrier((attended, next_part))
    own = gather_plane(attended, True)
    other = [hop(own[j], 1) for j in (0, 2, 1, 3)]
    next_own = gather_plane(far(next_part), False)
    next_other = [hop(next_own[j], 1) for j in (0, 2, 1, 3)]
    total = project([(0, False), (0, True), (1, False)], own + other + next_own, None)
    return project([(1, True)], next_other, total, last=True)


def partner_of(value, axis, distance):
    mask = 2**distance
    pairs = [(source, source ^ mask) for source in range(lax.axis_size(axis))]
    return lax.ppermute(value, axis, pairs)


def combine(earlier, later):
    out_one, top_one, sum_one = earlier
    out_two, top_two, sum_two = later
    new_top = jnp.maximum(top_one, top_two)
    factor_one = jnp.exp(top_one - new_top)
    factor_two = jnp.exp(top_two - new_top)
    new_out = out_one * factor_one[..., None] + out_two * factor_two[..., None]
    return (new_out, new_top, sum_one * factor_one + sum_two * factor_two)


def keep_state(key_block, run_state):
    return run_state


def partial_rows(rows_q, row_mask, cache_keys, cache_values, key_counts):
    row_count, head_count, head_size = rows_q.shape
    kv_count = cache_keys.shape[1]
    group_size = head_count // kv_count
    grouped = rows_q.reshape(row_count, kv_count, group_size, head_size)
    block_count = cache_keys.shape[0] // BLK
    score_scale = 1.0 / math.sqrt(head_size)
    offsets = jnp.arange(BLK, dtype=jnp.int32)

    def update(key_block, run_state):
        out_sum, top_score, weight_sum = run_state
        key_part = lax.dynamic_slice_in_dim(cache_keys, key_block * BLK, BLK, 0)
        value_part = lax.dynamic_slice_in_dim(cache_values, key_block * BLK, BLK, 0)
        scores = (
            jnp.einsum("rgqd,kgd->rgqk", grouped, key_part, preferred_element_type=jnp.float32)
            * score_scale
        )
        active_rows = lax.dynamic_slice_in_dim(row_mask, key_block, 1, 1)[:, 0] > 0
        valid_count = lax.dynamic_slice_in_dim(key_counts, key_block, 1, 0)[0]
        valid = active_rows[:, None, None, None] & (offsets < valid_count)[None, None, None, :]
        scores = jnp.where(valid, scores, very_low)
        new_top = jnp.maximum(top_score, jnp.max(scores, axis=-1))
        weights = jnp.where(valid, jnp.exp(scores - new_top[..., None]), 0.0)
        factor = jnp.exp(top_score - new_top)
        new_sum = weight_sum * factor + jnp.sum(weights, axis=-1)
        new_out = out_sum * factor[..., None] + jnp.einsum(
            "rgqk,kgd->rgqd",
            weights.astype(jnp.bfloat16),
            value_part,
            preferred_element_type=jnp.float32,
        )
        return (new_out, new_top, new_sum)

    def visit_block(key_block, run_state):
        active = jnp.any(lax.dynamic_slice_in_dim(row_mask, key_block, 1, 1) > 0)
        return lax.cond(active, update, keep_state, key_block, run_state)

    initial = (
        jnp.zeros((row_count, kv_count, group_size, head_size), jnp.float32),
        jnp.full((row_count, kv_count, group_size), very_low, jnp.float32),
        jnp.zeros((row_count, kv_count, group_size), jnp.float32),
    )
    return lax.fori_loop(0, block_count, visit_block, initial)


def general_body(queries, cache_keys, cache_values, block_mask, key_counts, out_weight):
    cycle_size = lax.axis_size("ctx")
    cycle_index = lax.axis_index("ctx")
    token_count, head_count, head_size = queries.shape
    segment = token_count // cycle_size
    query_blocks = queries.reshape(block_mask.shape[0], BLK, head_count, head_size)

    def per_block(block_item):
        rows_q, mask_row = block_item
        row_mask = jnp.broadcast_to(mask_row[None, :], (BLK, mask_row.shape[0]))
        return partial_rows(rows_q, row_mask, cache_keys, cache_values, key_counts)

    stacked = lax.map(per_block, (query_blocks, block_mask))
    run_state = tuple((part.reshape((token_count,) + part.shape[2:]) for part in stacked))
    bit_total = cycle_size.bit_length() - 1
    for bit_number in range(bit_total - 1, -1, -1):
        half_rows = run_state[1].shape[0] // 2
        upper_half = jnp.bitwise_and(jnp.right_shift(cycle_index, bit_number), 1)
        kept = tuple(
            (
                lax.dynamic_slice_in_dim(part, upper_half * half_rows, half_rows, 0)
                for part in run_state
            )
        )
        outgoing = tuple(
            (
                lax.dynamic_slice_in_dim(part, (1 - upper_half) * half_rows, half_rows, 0)
                for part in run_state
            )
        )
        received = partner_of((outgoing[0], outgoing[1], outgoing[2]), "ctx", bit_number)
        run_state = combine(kept, received)
    out_sum, top_score, weight_sum = run_state
    attended = (
        (out_sum / weight_sum[..., None])
        .astype(jnp.bfloat16)
        .reshape(segment, head_count * head_size)
    )
    partial_value = jnp.dot(
        lax.all_gather(attended, "ctx", axis=0, tiled=True),
        out_weight,
        preferred_element_type=jnp.float32,
    )
    return lax.psum_scatter(partial_value, "kv", scatter_dimension=0, tiled=True)


def body(queries, cache_keys, cache_values, block_mask, key_counts, out_weight):
    devices = lax.axis_size("ctx")
    token_count, head_count, d = queries.shape
    kv_count = cache_keys.shape[1]
    group_size = head_count // kv_count
    suits = (
        lax.axis_size("kv") == 1
        and devices == 32
        and token_count == BLK
        and block_mask.shape[0] == 1
        and kv_count == 4
        and d == LANES
        and group_size == 16
        and token_count * group_size == LANES * (devices // 2)
    )
    run = fast_body if suits else general_body
    return run(queries, cache_keys, cache_values, block_mask, key_counts, out_weight)


def solution(mesh):
    placed = (
        P("groups", "kv", None),
        P(("groups", "ctx"), "kv", None),
        P(("groups", "ctx"), "kv", None),
        P("groups", "ctx"),
        P(("groups", "ctx")),
        P("kv", "ctx"),
    )
    return jax.shard_map(
        body, mesh=mesh, in_specs=placed, out_specs=P(("groups", "kv"), "ctx"), check_vma=False
    )
```
